32 devices in a mesh: blk: 16 (over z, y, x), tp: 2 (over core).
Axes of the slice: x: 2, y: 2, z: 4, core: 2. Of those that a mesh axis runs over, the one named last changes fastest.
Arguments:
- tokens: bfloat16 [2048, 1024], P('blk'), may hold values from -6 to 6
- first_gain: float32 [1024], replicated, may hold values from 0.5 to 1.5
- first_bias: float32 [1024], replicated, may hold values from -2 to 2
- second_gain: float32 [1024], replicated, may hold values from 0.5 to 1.5
- second_bias: float32 [1024], replicated, may hold values from -2 to 2
- query_weight: bfloat16 [1024, 1024], P(None, 'tp'), may hold values from -0.1875 to 0.1875
- key_weight: bfloat16 [1024, 1024], P(None, 'tp'), may hold values from -0.1875 to 0.1875
- value_weight: bfloat16 [1024, 1024], P(None, 'tp'), may hold values from -0.1875 to 0.1875
- output_weight: bfloat16 [1024, 1024], P(None, 'tp'), may hold values from -1.5 to 1.5
- up_weight: bfloat16 [1024, 4096], P(None, 'tp'), may hold values from -0.1875 to 0.1875
- down_weight: bfloat16 [1024, 4096], P(None, 'tp'), may hold values from -0.09375 to 0.09375
- cotangent: bfloat16 [2048, 1024], P('blk'), may hold values from -6 to 6
- scene_len: int32 [4], replicated, may hold values from 1 to 1024, 2048 in all
Outputs:
- layer_out: bfloat16 [2048, 1024], P('blk')
- input_grad: float32 [2048, 1024], P('blk')
- first_gain_grad: float32 [1024], replicated
- first_bias_grad: float32 [1024], replicated
- second_gain_grad: float32 [1024], replicated
- second_bias_grad: float32 [1024], replicated
- query_grad: float32 [1024, 1024], P(None, 'tp')
- key_grad: float32 [1024, 1024], P(None, 'tp')
- value_grad: float32 [1024, 1024], P(None, 'tp')
- output_grad: float32 [1024, 1024], P(None, 'tp')
- up_grad: float32 [1024, 4096], P(None, 'tp')
- down_grad: float32 [1024, 4096], P(None, 'tp')
The draws below stay inside these ranges and needn't reach their ends.
Inputs may be any that keep to these rules, and one draw needn't show every extreme that they name: `scene_len`: 4 lengths in token order that sum to 2048; the longest is exactly 1024.
All inputs are finite; a program needn't handle non-finite values.
Results may differ from the reference program's by a relative error of at most 0.018.
Values may be sent and summed in bfloat16 or wider, within the bound.
No kernel may reach another device: no remote copies, remote signals or barrier semaphores. Data moves between devices by JAX's collectives and lax.ppermute only.
A program may use at most 128 MiB of HBM per device.

```python
import math
import jax
import jax.numpy as jnp
import numpy as np
from jax import lax

D = 1024
HEADS = 16
HEAD = 64
FF = 4096
SCENES = 4
HD = 1024
TOKENS = 2048
MOST_LEN = 1024


def block_scale(rng, shape, pieces, low, high):
    factor_of, own = 1.0, jax.random.fold_in(rng, 6)
    for position, blocks in pieces:
        heights = jnp.exp(jax.random.uniform(jax.random.fold_in(own, position), (blocks,), jnp.float32, low / len(pieces), high / len(pieces)))
        factor_of = factor_of * jnp.repeat(heights, shape[position] // blocks).reshape([-1 if axis == position else 1 for axis in range(len(shape))])
    return factor_of


def length_profile(number_of, total, limit, slope):
    loads = [(1 << 20) // math.isqrt(standing ** slope) + 1 for standing in range(2, number_of + 1)]
    surplus, holding = total - limit - (number_of - 1), [1] * (number_of - 1)
    while surplus > 0:
        candidates = [i for i in range(number_of - 1) if holding[i] < limit]
        pool, budget = sum([loads[i] for i in candidates]), surplus
        for i in candidates:
            extra = min(limit - holding[i], max(1, budget * loads[i] // pool), surplus)
            holding[i] = holding[i] + extra
            surplus = surplus - extra
    return np.array([limit] + holding)


def ragged(rng, number_of, total, most, slope):
    if number_of == 2:
        one = jax.random.randint(rng, (), max(1, total - most), min(most, total - 1) + 1)
        return jnp.stack([one, total - one])
    tallies = jnp.asarray(length_profile(number_of, total, most, slope), jnp.int32)
    pairs = (number_of - 1) // 2
    giver, receiver = tallies[1:1 + 2 * pairs:2], tallies[2:2 + 2 * pairs:2]
    slack = jnp.minimum(giver - 1, most - receiver)
    passed = jax.random.randint(jax.random.fold_in(rng, 1), (pairs,), 0, 1 << 20) % (slack + 1)
    tallies = tallies.at[1:1 + 2 * pairs:2].set(giver - passed).at[2:2 + 2 * pairs:2].set(receiver + passed)
    return tallies[jax.random.permutation(jax.random.fold_in(rng, 2), number_of)]


def centred(stream_key, shape, scale, most, shards=(), kind=jnp.bfloat16):
    array = scale * jax.random.normal(stream_key, shape, jnp.float32)
    if shards:
        array = array * block_scale(stream_key, shape, shards, -0.22, 0.18)
    return jnp.clip(array, -most, most).astype(kind)


def setup_inputs(seed: int = 0) -> dict:
    key_list = jax.random.split(jax.random.key(seed), 14)
    return {
        "tokens": centred(key_list[0], (TOKENS, D), 1.0, 6.0, ((0, 16),)),
        "first_gain": jnp.clip(1.0 + 0.1 * jax.random.normal(key_list[1], (D,), jnp.float32), 0.5, 1.5),
        "first_bias": centred(key_list[2], (D,), 0.3, 2.0, (), jnp.float32),
        "second_gain": jnp.clip(1.0 + 0.1 * jax.random.normal(key_list[3], (D,), jnp.float32), 0.5, 1.5),
        "second_bias": centred(key_list[4], (D,), 0.3, 2.0, (), jnp.float32),
        "query_weight": centred(key_list[5], (D, HD), D ** -0.5, 0.1875, ((1, 2),)),
        "key_weight": centred(key_list[6], (D, HD), D ** -0.5, 0.1875, ((1, 2),)),
        "value_weight": centred(key_list[7], (D, HD), D ** -0.5, 0.1875, ((1, 2),)),
        "output_weight": centred(key_list[8], (D, HD), (HD // 64) ** -0.5, 1.5, ((1, 2),)),
        "up_weight": centred(key_list[9], (D, FF), D ** -0.5, 0.1875, ((1, 2),)),
        "down_weight": centred(key_list[10], (D, FF), FF ** -0.5, 0.09375, ((1, 2),)),
        "cotangent": centred(key_list[11], (TOKENS, D), 1.0, 6.0, ((0, 16),)),
        "scene_len": ragged(key_list[12], SCENES, TOKENS, MOST_LEN, 0).astype(jnp.int32),
    }


@jax.custom_vjp
def low(v):
    return lax.optimization_barrier(v.astype(jnp.bfloat16)).astype(jnp.float32)

@jax.custom_vjp
def low_back(v):
    return v

def low_keep(v):
    return (low(v), None)

def low_pass(kept, grad):
    return (grad,)

def back_keep(v):
    return (v, None)

def back_low(kept, grad):
    return (low(grad),)
low.defvjp(low_keep, low_pass)
low_back.defvjp(back_keep, back_low)

def layer_norm(values, gain, bias):
    center = values - lax.optimization_barrier(jnp.mean(values, axis=-1, keepdims=True))
    spread = lax.optimization_barrier(jnp.mean(center * center, axis=-1, keepdims=True))
    return center * lax.rsqrt(spread + 1e-05) * gain + bias

def matmul(left, right):
    return jnp.dot(left, right, precision=lax.Precision.HIGHEST)

def attention(query, keys, values, scene):
    width = min(512, TOKENS)
    count = TOKENS // width
    query = query.reshape(count, width, HEADS, HEAD)
    keys = keys.reshape(TOKENS, HEADS, HEAD)
    values = values.reshape(TOKENS, HEADS, HEAD)
    blocks = scene.reshape(count, width)

    def one_block(pair):
        query_block, scene_block = pair
        raw = jnp.einsum('qhd,khd->hqk', query_block, keys, precision=lax.Precision.HIGHEST)
        raw = low_back(raw)
        scores = raw * HEAD ** (-0.5)
        mask = scene_block[:, None] == scene[None, :]
        scores = jnp.where(mask[None], scores, -1e+30)
        probs = low(jax.nn.softmax(scores, axis=-1))
        return jnp.einsum('hqk,khd->qhd', probs, values, precision=lax.Precision.HIGHEST)
    attended = lax.map(jax.checkpoint(one_block), (query, blocks))
    return attended.reshape(TOKENS, HD)

def forward(inputs, first_gain, first_bias, second_gain, second_bias, query_weight, key_weight, value_weight, output_weight, up_weight, down_weight, scene):
    normed_one = low(layer_norm(inputs, first_gain, first_bias))
    query = low(low_back(matmul(normed_one, query_weight)))
    keys = low(low_back(matmul(normed_one, key_weight)))
    values = low(low_back(matmul(normed_one, value_weight)))
    attended = low(low_back(attention(query, keys, values, scene)))
    middle = inputs + low_back(matmul(attended, output_weight.T))
    normed_two = low(layer_norm(middle, second_gain, second_bias))
    before = low_back(matmul(normed_two, up_weight))
    active = low(jax.nn.gelu(before, approximate=False))
    return middle + low_back(matmul(active, down_weight.T))

def reference(tokens, first_gain, first_bias, second_gain, second_bias, query_weight, key_weight, value_weight, output_weight, up_weight, down_weight, cotangent, scene_len):
    ends = jnp.cumsum(scene_len).astype(jnp.int32)
    places = jnp.arange(TOKENS, dtype=jnp.int32)
    scene = lax.optimization_barrier(jnp.sum((places[:, None] >= ends[None, :]).astype(jnp.int32), axis=1)).astype(jnp.int32)
    floats = (tokens.astype(jnp.float32), first_gain.astype(jnp.float32), first_bias.astype(jnp.float32), second_gain.astype(jnp.float32), second_bias.astype(jnp.float32), query_weight.astype(jnp.float32), key_weight.astype(jnp.float32), value_weight.astype(jnp.float32), output_weight.astype(jnp.float32), up_weight.astype(jnp.float32), down_weight.astype(jnp.float32))

    def apply(*params):
        return forward(*params, scene)
    result, pull = jax.vjp(apply, *floats)
    grads = pull(cotangent.astype(jnp.float32))
    return (result.astype(jnp.bfloat16), grads[0], grads[1], grads[2], grads[3], grads[4], grads[5], grads[6], grads[7], grads[8], grads[9], grads[10])
```

```python
import jax
import jax.numpy as jnp
from jax import lax
from jax.experimental import pallas as pl
from jax.experimental.pallas import tpu as pltpu
from jax.sharding import PartitionSpec as P

HEAD = 64
NEG = -1e30
f32 = jnp.float32
bf16 = jnp.bfloat16
LAST = (((1,), (1,)), ((), ()))
FIRST = (((0,), (0,)), ((), ()))


def from_behind(block, axis, distance):
    devices = range(lax.axis_size(axis))
    route = [((i - distance) % len(devices), i) for i in devices]
    return lax.ppermute(block, axis, route)


def layer_norm(values, gain, bias):
    center = values - jnp.mean(values, axis=-1, keepdims=True)
    spread = jnp.mean(center * center, axis=-1, keepdims=True)
    return center * lax.rsqrt(spread + 1e-05) * gain + bias


def move_grads(grad_keys, grad_values, offset):
    return (
        from_behind(grad_keys.astype(jnp.bfloat16), "blk", offset).astype(grad_keys.dtype),
        from_behind(grad_values.astype(jnp.bfloat16), "blk", offset).astype(grad_values.dtype),
    )


def ring_body(
    tokens,
    first_gain,
    first_bias,
    second_gain,
    second_bias,
    query_weight,
    key_weight,
    value_weight,
    output_weight,
    up_weight,
    down_weight,
    cotangent,
    scene_len,
):
    count = lax.axis_size("blk")
    place = lax.axis_index("blk")
    rows = tokens.shape[0]
    heads_here = query_weight.shape[1] // HEAD
    scale = HEAD ** (-0.5)
    ends = jnp.cumsum(scene_len)
    contract_last = (((1,), (1,)), ((), ()))
    contract_first = (((0,), (0,)), ((), ()))

    def scene_of(source):
        places = source * rows + jnp.arange(rows, dtype=jnp.int32)
        return jnp.sum((places[:, None] >= ends[None, :]).astype(jnp.int32), axis=1)

    mine = scene_of(place)

    def shares(source):
        other = scene_of(source)
        return jnp.maximum(mine[0], other[0]) <= jnp.minimum(mine[-1], other[-1])

    directions = (1,)
    steps = count - 1

    def source_of(way, turn):
        raw_source = place - way * turn
        return (raw_source % count, jnp.array(True))

    inputs = tokens.astype(f32)
    normed_one = layer_norm(inputs, first_gain, first_bias).astype(bf16)

    def project(weight):
        return jnp.dot(normed_one, weight, preferred_element_type=f32).astype(bf16)

    query = project(query_weight).reshape(rows, heads_here, HEAD)
    keys = project(key_weight).reshape(rows, heads_here, HEAD)
    values = project(value_weight).reshape(rows, heads_here, HEAD)

    def scores_of(key_block, source):
        mask = mine[:, None] == scene_of(source)[None, :]
        scores = jnp.einsum("qhd,khd->hqk", query, key_block, preferred_element_type=f32) * scale
        return (jnp.where(mask[None], scores, -1e30), mask)

    def absorb(state, key_block, value_block, source):
        top, total, summed = state
        scores, mask = scores_of(key_block, source)
        new_top = jnp.maximum(top, jnp.max(scores, axis=2))
        factor = jnp.exp(top - new_top)
        weights = jnp.where(mask[None], jnp.exp(scores - new_top[:, :, None]), 0.0)
        total = total * factor + jnp.sum(weights, axis=2)
        summed = summed * factor.T[:, :, None] + jnp.einsum(
            "hqk,khd->qhd", weights.astype(bf16), value_block, preferred_element_type=f32
        )
        return (new_top, total, summed)

    start = (
        jnp.full((heads_here, rows), -1e30, f32),
        jnp.zeros((heads_here, rows), f32),
        jnp.zeros((rows, heads_here, HEAD), f32),
    )
    state = absorb(start, keys, values, place)
    way = directions[0]

    def turn_forward(turn, carry):
        current, key_block, value_block = carry
        key_block, value_block = from_behind((key_block, value_block), "blk", way)
        source, inside = source_of(way, turn)
        current = lax.cond(
            inside & shares(source),
            lambda held: absorb(held, key_block, value_block, source),
            lambda held: held,
            current,
        )
        return (current, key_block, value_block)

    state, _, _ = lax.fori_loop(1, steps + 1, turn_forward, (state, keys, values))
    top, total, summed = state
    attended = summed / total.T[:, :, None]
    log_total = top + jnp.log(total)
    attended_low = attended.reshape(rows, -1).astype(bf16)
    branch = lax.dot_general(attended_low, output_weight, contract_last, preferred_element_type=f32)
    branch = lax.psum(branch.astype(jnp.bfloat16), "tp").astype(jnp.float32)
    middle = inputs + branch
    normed_two = layer_norm(middle, second_gain, second_bias).astype(bf16)
    before = jnp.dot(normed_two, up_weight, preferred_element_type=f32)
    active = jax.nn.gelu(before, approximate=False).astype(bf16)
    feed = lax.dot_general(active, down_weight, contract_last, preferred_element_type=f32)
    feed = lax.psum(feed.astype(jnp.bfloat16), "tp").astype(jnp.float32)
    layer_out = (middle + feed).astype(bf16)
    grad_out = cotangent.astype(f32)
    down_grad = lax.dot_general(cotangent, active, contract_first, preferred_element_type=f32)
    grad_active = jnp.dot(cotangent, down_weight, preferred_element_type=f32)
    _, gelu_pull = jax.vjp(lambda arg: jax.nn.gelu(arg, approximate=False), before)
    grad_before = gelu_pull(grad_active)[0].astype(bf16)
    up_grad = lax.dot_general(normed_two, grad_before, contract_first, preferred_element_type=f32)
    grad_two = lax.dot_general(grad_before, up_weight, contract_last, preferred_element_type=f32)
    grad_two = lax.psum(grad_two.astype(jnp.bfloat16), "tp").astype(jnp.float32)
    _, second_pull = jax.vjp(layer_norm, middle, second_gain, second_bias)
    grad_middle_norm, second_gain_grad, second_bias_grad = second_pull(grad_two)
    grad_middle = grad_out + grad_middle_norm
    grad_middle_low = grad_middle.astype(bf16)
    output_grad = lax.dot_general(
        grad_middle_low, attended_low, contract_first, preferred_element_type=f32
    )
    grad_attended = jnp.dot(grad_middle_low, output_weight, preferred_element_type=f32).astype(bf16)
    grad_attended = grad_attended.reshape(rows, heads_here, HEAD)
    delta = jnp.sum(grad_attended * attended, axis=2).T

    def backtrack(grads, key_block, value_block, source):
        grad_query, grad_keys, grad_values = grads
        scores, mask = scores_of(key_block, source)
        probs = jnp.where(mask[None], jnp.exp(scores - log_total[:, :, None]), 0.0)
        grad_values = grad_values + jnp.einsum(
            "hqk,qhd->khd", probs.astype(bf16), grad_attended, preferred_element_type=f32
        )
        grad_probs = jnp.einsum(
            "qhd,khd->hqk", grad_attended, value_block, preferred_element_type=f32
        )
        grad_scores = (probs * (grad_probs - delta[:, :, None]) * scale).astype(bf16)
        grad_query = grad_query + jnp.einsum(
            "hqk,khd->qhd", grad_scores, key_block, preferred_element_type=f32
        )
        grad_keys = grad_keys + jnp.einsum(
            "hqk,qhd->khd", grad_scores, query, preferred_element_type=f32
        )
        return (grad_query, grad_keys, grad_values)

    empty = jnp.zeros((rows, heads_here, HEAD), f32)
    grad_query, home_keys, home_values = backtrack((empty, empty, empty), keys, values, place)
    way = directions[0]

    def turn_backward(turn, carry):
        grad_q, key_block, value_block, grad_k, grad_v = carry
        key_block, value_block = from_behind((key_block, value_block), "blk", way)
        grad_k, grad_v = move_grads(grad_k, grad_v, way)
        source, inside = source_of(way, turn)
        grad_q, grad_k, grad_v = lax.cond(
            inside & shares(source),
            lambda held: backtrack(held, key_block, value_block, source),
            lambda held: held,
            (grad_q, grad_k, grad_v),
        )
        return (grad_q, key_block, value_block, grad_k, grad_v)

    grad_query, _, _, moved_keys, moved_values = lax.fori_loop(
        1, steps + 1, turn_backward, (grad_query, keys, values, empty, empty)
    )
    moved_keys, moved_values = move_grads(moved_keys, moved_values, -way * steps)
    home_keys = home_keys + moved_keys
    home_values = home_values + moved_values
    grad_query = grad_query.reshape(rows, -1).astype(bf16)
    grad_keys = home_keys.reshape(rows, -1).astype(bf16)
    grad_values = home_values.reshape(rows, -1).astype(bf16)
    query_grad = lax.dot_general(normed_one, grad_query, contract_first, preferred_element_type=f32)
    key_grad = lax.dot_general(normed_one, grad_keys, contract_first, preferred_element_type=f32)
    value_grad = lax.dot_general(
        normed_one, grad_values, contract_first, preferred_element_type=f32
    )
    grad_one = lax.dot_general(grad_query, query_weight, contract_last, preferred_element_type=f32)
    grad_one = grad_one + lax.dot_general(
        grad_keys, key_weight, contract_last, preferred_element_type=f32
    )
    grad_one = grad_one + lax.dot_general(
        grad_values, value_weight, contract_last, preferred_element_type=f32
    )
    grad_one = lax.psum(grad_one.astype(jnp.bfloat16), "tp").astype(jnp.float32)
    _, first_pull = jax.vjp(layer_norm, inputs, first_gain, first_bias)
    grad_input_norm, first_gain_grad, first_bias_grad = first_pull(grad_one)
    input_grad = grad_middle + grad_input_norm
    norm_grads = jnp.stack(
        [first_gain_grad, first_bias_grad, second_gain_grad, second_bias_grad], axis=1
    )
    summed_parts = (
        lax.psum_scatter(query_grad, "blk", scatter_dimension=0, tiled=True),
        lax.psum_scatter(key_grad, "blk", scatter_dimension=0, tiled=True),
        lax.psum_scatter(value_grad, "blk", scatter_dimension=0, tiled=True),
        lax.psum_scatter(output_grad, "blk", scatter_dimension=0, tiled=True),
        lax.psum_scatter(up_grad, "blk", scatter_dimension=0, tiled=True),
        lax.psum_scatter(down_grad, "blk", scatter_dimension=0, tiled=True),
        lax.psum_scatter(norm_grads, "blk", scatter_dimension=0, tiled=True),
    )
    totals = (
        lax.all_gather(summed_parts[0].astype(jnp.bfloat16), "blk", axis=0, tiled=True).astype(
            jnp.float32
        ),
        lax.all_gather(summed_parts[1].astype(jnp.bfloat16), "blk", axis=0, tiled=True).astype(
            jnp.float32
        ),
        lax.all_gather(summed_parts[2].astype(jnp.bfloat16), "blk", axis=0, tiled=True).astype(
            jnp.float32
        ),
        lax.all_gather(summed_parts[3].astype(jnp.bfloat16), "blk", axis=0, tiled=True).astype(
            jnp.float32
        ),
        lax.all_gather(summed_parts[4].astype(jnp.bfloat16), "blk", axis=0, tiled=True).astype(
            jnp.float32
        ),
        lax.all_gather(summed_parts[5].astype(jnp.bfloat16), "blk", axis=0, tiled=True).astype(
            jnp.float32
        ),
        lax.all_gather(summed_parts[6].astype(jnp.bfloat16), "blk", axis=0, tiled=True).astype(
            jnp.float32
        ),
    )
    return (
        layer_out,
        input_grad,
        totals[6][:, 0],
        totals[6][:, 1],
        totals[6][:, 2],
        totals[6][:, 3],
        totals[0],
        totals[1],
        totals[2],
        totals[3],
        totals[4],
        totals[5],
    )


def full(shape):
    return pl.BlockSpec(shape, lambda *_: (0,) * len(shape))


def attend_kernel(q_ref, k_ref, v_ref, mine_ref, all_ref, out_ref):
    lane = lax.broadcasted_iota(jnp.int32, q_ref.shape, 1) // HEAD
    mask = mine_ref[...] == all_ref[...]
    parts = []
    for head in range(2):
        q = jnp.where(lane == head, q_ref[...], jnp.zeros_like(q_ref[...]))
        s = lax.dot_general(q, k_ref[...], LAST, preferred_element_type=f32)
        s = jnp.where(mask, s, NEG)
        p = jnp.exp(s - jnp.max(s, axis=1, keepdims=True))
        total = jnp.sum(p, axis=1, keepdims=True)
        part = jnp.dot(p.astype(bf16), v_ref[...], preferred_element_type=f32)
        parts.append(part / total)
    out_ref[...] = jnp.where(lane == 0, parts[0], parts[1]).astype(bf16)


def attend(q, k, v, scene_mine, scene_all):
    rows, width = q.shape
    total = k.shape[0]
    pair = 2 * HEAD
    return pl.pallas_call(
        attend_kernel,
        grid=(width // pair,),
        in_specs=[
            pl.BlockSpec((rows, pair), lambda i: (0, i)),
            pl.BlockSpec((total, pair), lambda i: (0, i)),
            pl.BlockSpec((total, pair), lambda i: (0, i)),
            full((rows, 1)),
            full((1, total)),
        ],
        out_specs=pl.BlockSpec((rows, pair), lambda i: (0, i)),
        out_shape=jax.ShapeDtypeStruct((rows, width), bf16),
        name="attend",
    )(q, k, v, scene_mine.reshape(rows, 1), scene_all.reshape(1, total))


QT = 256
KT = 512


def prepare_kernel(h_ref, row_ref, col_ref, lse_ref, a_ref, k_s):
    @pl.when(pl.program_id(0) == 0)
    def _():
        k_s[...] = h_ref[HEAD : 2 * HEAD, :].T

    at = pl.multiple_of(pl.program_id(0) * QT, QT)
    q = h_ref[0:HEAD, pl.ds(at, QT)]
    s = jnp.dot(k_s[...], q, preferred_element_type=f32)
    s = jnp.where(col_ref[...] == row_ref[...], s, NEG)
    top = jnp.max(s, axis=0, keepdims=True)
    p = jnp.exp(s - top)
    total = jnp.sum(p, axis=0, keepdims=True)
    a = jnp.dot(h_ref[2 * HEAD :, :], p.astype(bf16), preferred_element_type=f32)
    a_ref[...] = a / total
    lse_ref[...] = top + jnp.log(total)


def prepare(head, scene_all):
    total = head.shape[1]
    return pl.pallas_call(
        prepare_kernel,
        grid=(total // QT,),
        in_specs=[
            full(head.shape),
            pl.BlockSpec((1, QT), lambda i: (0, i)),
            full((total, 1)),
        ],
        out_specs=[
            pl.BlockSpec((1, QT), lambda i: (0, i)),
            pl.BlockSpec((HEAD, QT), lambda i: (0, i)),
        ],
        out_shape=[
            jax.ShapeDtypeStruct((1, total), f32),
            jax.ShapeDtypeStruct((HEAD, total), f32),
        ],
        scratch_shapes=[pltpu.VMEM((total, HEAD), bf16)],
        name="prepare",
    )(head, scene_all.reshape(1, total), scene_all.reshape(total, 1))


def back_kernel(h_ref, ga_ref, lse_ref, a_ref, row_ref, col_ref, out_ref, k_s, v_s, gk_s, gv_s):
    step = pl.program_id(0)
    total = h_ref.shape[1]

    @pl.when(step == 0)
    def _():
        k_s[...] = h_ref[HEAD : 2 * HEAD, :].T
        v_s[...] = h_ref[2 * HEAD :, :].T
        gk_s[...] = jnp.zeros_like(gk_s)
        gv_s[...] = jnp.zeros_like(gv_s)

    at = pl.multiple_of(step * QT, QT)
    q_t = h_ref[0:HEAD, pl.ds(at, QT)]
    ga_t = jnp.concatenate([ga_ref[i] for i in range(ga_ref.shape[0])], axis=1)
    q = q_t.T
    ga = ga_t.T
    delta = jnp.sum(ga_t.astype(f32) * a_ref[...], axis=0, keepdims=True)
    gq = jnp.zeros((HEAD, QT), f32)
    for j in range(total // KT):
        keys = slice(j * KT, (j + 1) * KT)
        s = jnp.dot(k_s[keys, :], q_t, preferred_element_type=f32)
        p = jnp.where(col_ref[keys, :] == row_ref[...], jnp.exp(s - lse_ref[...]), 0.0)
        dp = jnp.dot(v_s[keys, :], ga_t, preferred_element_type=f32)
        ds = (p * (dp - delta)).astype(bf16)
        gv_s[keys, :] += jnp.dot(p.astype(bf16), ga, preferred_element_type=f32)
        gk_s[keys, :] += jnp.dot(ds, q, preferred_element_type=f32)
        gq += jnp.dot(h_ref[HEAD : 2 * HEAD, keys], ds, preferred_element_type=f32)
    out_ref[0:HEAD, pl.ds(at, QT)] = (gq * HEAD ** (-0.5)).astype(bf16)

    @pl.when(step == pl.num_programs(0) - 1)
    def _():
        out_ref[HEAD : 2 * HEAD, :] = gk_s[...].T.astype(bf16)
        out_ref[2 * HEAD :, :] = gv_s[...].T.astype(bf16)


def back(head, ga, lse, a, scene_all):
    total = head.shape[1]
    per = QT // ga.shape[2]
    return pl.pallas_call(
        back_kernel,
        grid=(total // QT,),
        in_specs=[
            full(head.shape),
            pl.BlockSpec((per, HEAD, ga.shape[2]), lambda i: (i, 0, 0)),
            pl.BlockSpec((1, QT), lambda i: (0, i)),
            pl.BlockSpec((HEAD, QT), lambda i: (0, i)),
            pl.BlockSpec((1, QT), lambda i: (0, i)),
            full((total, 1)),
        ],
        out_specs=full(head.shape),
        out_shape=jax.ShapeDtypeStruct(head.shape, bf16),
        scratch_shapes=[
            pltpu.VMEM((total, HEAD), bf16),
            pltpu.VMEM((total, HEAD), bf16),
            pltpu.VMEM((total, HEAD), f32),
            pltpu.VMEM((total, HEAD), f32),
        ],
        name="back",
    )(head, ga, lse, a, scene_all.reshape(1, total), scene_all.reshape(total, 1))


FT = 256
TT = 512


def gelu_both(pre, grad):
    half = 0.5 * (1.0 + lax.erf(pre * 0.7071067811865476))
    slope = half + pre * (jnp.exp(-0.5 * pre * pre) * 0.3989422804014327)
    return (pre * half).astype(bf16), (grad * slope).astype(bf16)


def ffn_kernel(h_ref, g_ref, ht_ref, gt_ref, up_ref, down_ref, up_out, down_out):
    total = h_ref.shape[0]
    for j in range(total // TT):
        rows = slice(j * TT, (j + 1) * TT)
        pre = jnp.dot(h_ref[rows, :], up_ref[...], preferred_element_type=f32)
        grad = jnp.dot(g_ref[rows, :], down_ref[...], preferred_element_type=f32)
        act, grad_pre = gelu_both(pre, grad)
        up = jnp.dot(ht_ref[:, rows], grad_pre, preferred_element_type=f32)
        down = jnp.dot(gt_ref[:, rows], act, preferred_element_type=f32)
        if j == 0:
            up_out[...] = up
            down_out[...] = down
        else:
            up_out[...] += up
            down_out[...] += down


def ffn_grads(h, xg, h_t, g_t, up_weight, down_weight):
    total, width = h.shape
    hidden = up_weight.shape[1]
    once = pl.Buffered(1)
    return pl.pallas_call(
        ffn_kernel,
        grid=(hidden // FT,),
        in_specs=[
            pl.BlockSpec((total, width), lambda i: (0, 0), pipeline_mode=once),
            pl.BlockSpec((total, width), lambda i: (0, 1), pipeline_mode=once),
            pl.BlockSpec((width, total), lambda i: (0, 0), pipeline_mode=once),
            pl.BlockSpec((width, total), lambda i: (0, 0), pipeline_mode=once),
            pl.BlockSpec((width, FT), lambda i: (0, i)),
            pl.BlockSpec((width, FT), lambda i: (0, i)),
        ],
        out_specs=[pl.BlockSpec((width, FT), lambda i: (0, i))] * 2,
        out_shape=[jax.ShapeDtypeStruct((width, hidden), f32)] * 2,
        name="ffn_grads",
    )(h, xg, h_t, g_t, up_weight, down_weight)


def both_halves(partial):
    low = lax.optimization_barrier(partial.astype(bf16))
    other = lax.ppermute(low, "tp", [(0, 1), (1, 0)])
    return low.astype(f32) + other.astype(f32)


def fast_body(
    tokens,
    first_gain,
    first_bias,
    second_gain,
    second_bias,
    query_weight,
    key_weight,
    value_weight,
    output_weight,
    up_weight,
    down_weight,
    cotangent,
    scene_len,
):
    count = lax.axis_size("blk")
    place = lax.axis_index("blk")
    side = lax.axis_index("tp")
    rows, width = tokens.shape
    total = rows * count
    heads_here = query_weight.shape[1] // HEAD
    share = count // heads_here
    scale = HEAD ** (-0.5)
    head_at = (place // share) * HEAD
    part = place % share

    def half_of(block):
        return lax.dynamic_slice_in_dim(block, side * (rows // 2), rows // 2, 0)

    both = jnp.concatenate([half_of(tokens), half_of(cotangent)], axis=1)
    xg = lax.all_gather(both, ("blk", "tp"), axis=0, tiled=True)

    ends = jnp.cumsum(scene_len)
    positions = jnp.arange(total, dtype=jnp.int32)
    scene_all = jnp.sum((positions[:, None] >= ends[None, :]).astype(jnp.int32), axis=1)
    scene_mine = lax.dynamic_slice_in_dim(scene_all, place * rows, rows)

    inputs = tokens.astype(f32)
    h1_mine = layer_norm(inputs, first_gain, first_bias).astype(bf16)
    h1_all = layer_norm(xg[:, :width].astype(f32), first_gain, first_bias).astype(bf16)

    def project(rows_in, weight):
        return jnp.dot(rows_in, weight, preferred_element_type=f32)

    query = (project(h1_mine, query_weight).astype(bf16) * scale).astype(bf16)
    keys = project(h1_all, key_weight).astype(bf16)
    values = project(h1_all, value_weight).astype(bf16)
    attended = attend(query, keys, values, scene_mine, scene_all)

    def head_of(weight):
        return lax.dynamic_slice_in_dim(weight, head_at, HEAD, 1)

    head_weight = jnp.concatenate(
        [head_of(query_weight) * jnp.asarray(scale, bf16), head_of(key_weight), head_of(value_weight)], axis=1
    )
    head = lax.dot_general(
        head_weight, h1_all, (((0,), (1,)), ((), ())), preferred_element_type=f32
    ).astype(bf16)
    lse, head_attended = prepare(head, scene_all)

    branch = lax.dot_general(attended, output_weight, LAST, preferred_element_type=f32)
    middle = inputs + both_halves(branch)
    h2 = layer_norm(middle, second_gain, second_bias).astype(bf16)
    h2_all = lax.all_gather(half_of(h2), ("blk", "tp"), axis=0, tiled=True)

    before = jnp.dot(h2, up_weight, preferred_element_type=f32)
    grad_active = jnp.dot(cotangent, down_weight, preferred_element_type=f32)
    active, grad_before = gelu_both(before, grad_active)
    grad_two = lax.dot_general(grad_before, up_weight, LAST, preferred_element_type=f32)
    grad_two = both_halves(grad_two)
    _, second_pull = jax.vjp(layer_norm, middle, second_gain, second_bias)
    grad_middle, second_gain_grad, second_bias_grad = second_pull(grad_two)
    grad_middle = cotangent.astype(f32) + grad_middle
    grad_middle_low = grad_middle.astype(bf16)
    grad_attended = lax.dot_general(
        output_weight, grad_middle_low, (((0,), (1,)), ((), ())), preferred_element_type=f32
    ).astype(bf16)
    to_heads = jnp.repeat(grad_attended.reshape(heads_here, HEAD, rows), share, axis=0)
    ga = lax.all_to_all(to_heads, "blk", 0, 0, tiled=True)

    feed = lax.dot_general(active, down_weight, LAST, preferred_element_type=f32)
    layer_out = (middle + both_halves(feed)).astype(bf16)
    output_part = lax.dot_general(grad_middle_low, attended, FIRST, preferred_element_type=f32)
    output_part = output_part.astype(bf16).reshape(count, width // count, -1)
    output_parts = lax.all_to_all(output_part, "blk", 0, 0, tiled=True)
    output_slice = jnp.sum(output_parts.astype(f32), axis=0).astype(bf16)

    head_grads = back(head, ga, lse, head_attended, scene_all)
    h1_part = lax.dynamic_slice_in_dim(h1_all, part * (width // share), width // share, 1)
    head_slice = jnp.dot(head_grads, h1_part, preferred_element_type=f32).astype(bf16)
    gathered = lax.all_gather(
        jnp.concatenate([head_slice, output_slice.reshape(-1, width // share)], axis=0), "blk", axis=0
    )

    piece = 3 * HEAD // share
    home = lax.dynamic_slice_in_dim(head_grads, part * piece, piece, 0)
    home = home.reshape(piece, count, rows).transpose(1, 0, 2)
    home = lax.all_to_all(home, "blk", 0, 0, tiled=True)
    home = home.reshape(heads_here, 3, HEAD, rows)
    grad_one = 0.0
    for i, weight in enumerate((query_weight, key_weight, value_weight)):
        grad_one = grad_one + lax.dot_general(
            home[:, i].reshape(-1, rows), weight, (((0,), (1,)), ((), ())), preferred_element_type=f32
        )
    grad_one = both_halves(grad_one)
    _, first_pull = jax.vjp(layer_norm, inputs, first_gain, first_bias)
    grad_input, first_gain_grad, first_bias_grad = first_pull(grad_one)
    input_grad = grad_middle + grad_input
    norm_part = jnp.stack([first_gain_grad, first_bias_grad, second_gain_grad, second_bias_grad])
    norm_parts = lax.all_to_all(
        jnp.broadcast_to(norm_part[None], (count,) + norm_part.shape), "blk", 0, 0, tiled=True
    )
    norm_sums = jnp.sum(norm_parts, axis=0)

    up_grad, down_grad = ffn_grads(h2_all, xg, h2_all.T, xg[:, width:].T, up_weight, down_weight)

    def weight_grad(i):
        pieces = gathered[:, i * HEAD : (i + 1) * HEAD].reshape(heads_here, share, HEAD, width // share)
        return pieces.transpose(1, 3, 0, 2).reshape(width, heads_here * HEAD).astype(f32)

    output_grad = gathered[:, 3 * HEAD :].reshape(width, heads_here * HEAD).astype(f32)
    return (
        layer_out,
        input_grad,
        norm_sums[0],
        norm_sums[1],
        norm_sums[2],
        norm_sums[3],
        weight_grad(0),
        weight_grad(1),
        weight_grad(2),
        output_grad,
        up_grad,
        down_grad,
    )


def solution(mesh):
    body = fast_body if mesh.shape["blk"] == 16 else ring_body
    return jax.shard_map(
        body,
        mesh=mesh,
        in_specs=(
            P("blk", None),
            P(),
            P(),
            P(),
            P(),
            P(None, "tp"),
            P(None, "tp"),
            P(None, "tp"),
            P(None, "tp"),
            P(None, "tp"),
            P(None, "tp"),
            P("blk", None),
            P(),
        ),
        out_specs=(
            P("blk", None),
            P("blk", None),
            P(),
            P(),
            P(),
            P(),
            P(None, "tp"),
            P(None, "tp"),
            P(None, "tp"),
            P(None, "tp"),
            P(None, "tp"),
            P(None, "tp"),
        ),
        check_vma=False,
    )
```

```python
import jax
import jax.numpy as jnp
from jax import lax
from jax.experimental import pallas as pl
from jax.experimental.pallas import tpu as pltpu
from jax.sharding import PartitionSpec as P

HEAD = 64
NEG = -1e30
f32 = jnp.float32
bf16 = jnp.bfloat16
LAST = (((1,), (1,)), ((), ()))
FIRST = (((0,), (0,)), ((), ()))


def from_behind(block, axis, distance):
    devices = range(lax.axis_size(axis))
    route = [((i - distance) % len(devices), i) for i in devices]
    return lax.ppermute(block, axis, route)


def layer_norm(values, gain, bias):
    center = values - jnp.mean(values, axis=-1, keepdims=True)
    spread = jnp.mean(center * center, axis=-1, keepdims=True)
    return center * lax.rsqrt(spread + 1e-05) * gain + bias


def move_grads(grad_keys, grad_values, offset):
    return (
        from_behind(grad_keys.astype(jnp.bfloat16), "blk", offset).astype(grad_keys.dtype),
        from_behind(grad_values.astype(jnp.bfloat16), "blk", offset).astype(grad_values.dtype),
    )


def ring_body(
    tokens,
    first_gain,
    first_bias,
    second_gain,
    second_bias,
    query_weight,
    key_weight,
    value_weight,
    output_weight,
    up_weight,
    down_weight,
    cotangent,
    scene_len,
):
    count = lax.axis_size("blk")
    place = lax.axis_index("blk")
    rows = tokens.shape[0]
    heads_here = query_weight.shape[1] // HEAD
    scale = HEAD ** (-0.5)
    ends = jnp.cumsum(scene_len)
    contract_last = (((1,), (1,)), ((), ()))
    contract_first = (((0,), (0,)), ((), ()))

    def scene_of(source):
        places = source * rows + jnp.arange(rows, dtype=jnp.int32)
        return jnp.sum((places[:, None] >= ends[None, :]).astype(jnp.int32), axis=1)

    mine = scene_of(place)

    def shares(source):
        other = scene_of(source)
        return jnp.maximum(mine[0], other[0]) <= jnp.minimum(mine[-1], other[-1])

    directions = (1,)
    steps = count - 1

    def source_of(way, turn):
        raw_source = place - way * turn
        return (raw_source % count, jnp.array(True))

    inputs = tokens.astype(f32)
    normed_one = layer_norm(inputs, first_gain, first_bias).astype(bf16)

    def project(weight):
        return jnp.dot(normed_one, weight, preferred_element_type=f32).astype(bf16)

    query = project(query_weight).reshape(rows, heads_here, HEAD)
    keys = project(key_weight).reshape(rows, heads_here, HEAD)
    values = project(value_weight).reshape(rows, heads_here, HEAD)

    def scores_of(key_block, source):
        mask = mine[:, None] == scene_of(source)[None, :]
        scores = jnp.einsum("qhd,khd->hqk", query, key_block, preferred_element_type=f32) * scale
        return (jnp.where(mask[None], scores, -1e30), mask)

    def absorb(state, key_block, value_block, source):
        top, total, summed = state
        scores, mask = scores_of(key_block, source)
        new_top = jnp.maximum(top, jnp.max(scores, axis=2))
        factor = jnp.exp(top - new_top)
        weights = jnp.where(mask[None], jnp.exp(scores - new_top[:, :, None]), 0.0)
        total = total * factor + jnp.sum(weights, axis=2)
        summed = summed * factor.T[:, :, None] + jnp.einsum(
            "hqk,khd->qhd", weights.astype(bf16), value_block, preferred_element_type=f32
        )
        return (new_top, total, summed)

    start = (
        jnp.full((heads_here, rows), -1e30, f32),
        jnp.zeros((heads_here, rows), f32),
        jnp.zeros((rows, heads_here, HEAD), f32),
    )
    state = absorb(start, keys, values, place)
    way = directions[0]

    def turn_forward(turn, carry):
        current, key_block, value_block = carry
        key_block, value_block = from_behind((key_block, value_block), "blk", way)
        source, inside = source_of(way, turn)
        current = lax.cond(
            inside & shares(source),
            lambda held: absorb(held, key_block, value_block, source),
            lambda held: held,
            current,
        )
        return (current, key_block, value_block)

    state, _, _ = lax.fori_loop(1, steps + 1, turn_forward, (state, keys, values))
    top, total, summed = state
    attended = summed / total.T[:, :, None]
    log_total = top + jnp.log(total)
    attended_low = attended.reshape(rows, -1).astype(bf16)
    branch = lax.dot_general(attended_low, output_weight, contract_last, preferred_element_type=f32)
    branch = lax.psum(branch.astype(jnp.bfloat16), "tp").astype(jnp.float32)
    middle = inputs + branch
    normed_two = layer_norm(middle, second_gain, second_bias).astype(bf16)
    before = jnp.dot(normed_two, up_weight, preferred_element_type=f32)
    active = jax.nn.gelu(before, approximate=False).astype(bf16)
    feed = lax.dot_general(active, down_weight, contract_last, preferred_element_type=f32)
    feed = lax.psum(feed.astype(jnp.bfloat16), "tp").astype(jnp.float32)
    layer_out = (middle + feed).astype(bf16)
    grad_out = cotangent.astype(f32)
    down_grad = lax.dot_general(cotangent, active, contract_first, preferred_element_type=f32)
    grad_active = jnp.dot(cotangent, down_weight, preferred_element_type=f32)
    _, gelu_pull = jax.vjp(lambda arg: jax.nn.gelu(arg, approximate=False), before)
    grad_before = gelu_pull(grad_active)[0].astype(bf16)
    up_grad = lax.dot_general(normed_two, grad_before, contract_first, preferred_element_type=f32)
    grad_two = lax.dot_general(grad_before, up_weight, contract_last, preferred_element_type=f32)
    grad_two = lax.psum(grad_two.astype(jnp.bfloat16), "tp").astype(jnp.float32)
    _, second_pull = jax.vjp(layer_norm, middle, second_gain, second_bias)
    grad_middle_norm, second_gain_grad, second_bias_grad = second_pull(grad_two)
    grad_middle = grad_out + grad_middle_norm
    grad_middle_low = grad_middle.astype(bf16)
    output_grad = lax.dot_general(
        grad_middle_low, attended_low, contract_first, preferred_element_type=f32
    )
    grad_attended = jnp.dot(grad_middle_low, output_weight, preferred_element_type=f32).astype(bf16)
    grad_attended = grad_attended.reshape(rows, heads_here, HEAD)
    delta = jnp.sum(grad_attended * attended, axis=2).T

    def backtrack(grads, key_block, value_block, source):
        grad_query, grad_keys, grad_values = grads
        scores, mask = scores_of(key_block, source)
        probs = jnp.where(mask[None], jnp.exp(scores - log_total[:, :, None]), 0.0)
        grad_values = grad_values + jnp.einsum(
            "hqk,qhd->khd", probs.astype(bf16), grad_attended, preferred_element_type=f32
        )
        grad_probs = jnp.einsum(
            "qhd,khd->hqk", grad_attended, value_block, preferred_element_type=f32
        )
        grad_scores = (probs * (grad_probs - delta[:, :, None]) * scale).astype(bf16)
        grad_query = grad_query + jnp.einsum(
            "hqk,khd->qhd", grad_scores, key_block, preferred_element_type=f32
        )
        grad_keys = grad_keys + jnp.einsum(
            "hqk,qhd->khd", grad_scores, query, preferred_element_type=f32
        )
        return (grad_query, grad_keys, grad_values)

    empty = jnp.zeros((rows, heads_here, HEAD), f32)
    grad_query, home_keys, home_values = backtrack((empty, empty, empty), keys, values, place)
    way = directions[0]

    def turn_backward(turn, carry):
        grad_q, key_block, value_block, grad_k, grad_v = carry
        key_block, value_block = from_behind((key_block, value_block), "blk", way)
        grad_k, grad_v = move_grads(grad_k, grad_v, way)
        source, inside = source_of(way, turn)
        grad_q, grad_k, grad_v = lax.cond(
            inside & shares(source),
            lambda held: backtrack(held, key_block, value_block, source),
            lambda held: held,
            (grad_q, grad_k, grad_v),
        )
        return (grad_q, key_block, value_block, grad_k, grad_v)

    grad_query, _, _, moved_keys, moved_values = lax.fori_loop(
        1, steps + 1, turn_backward, (grad_query, keys, values, empty, empty)
    )
    moved_keys, moved_values = move_grads(moved_keys, moved_values, -way * steps)
    home_keys = home_keys + moved_keys
    home_values = home_values + moved_values
    grad_query = grad_query.reshape(rows, -1).astype(bf16)
    grad_keys = home_keys.reshape(rows, -1).astype(bf16)
    grad_values = home_values.reshape(rows, -1).astype(bf16)
    query_grad = lax.dot_general(normed_one, grad_query, contract_first, preferred_element_type=f32)
    key_grad = lax.dot_general(normed_one, grad_keys, contract_first, preferred_element_type=f32)
    value_grad = lax.dot_general(
        normed_one, grad_values, contract_first, preferred_element_type=f32
    )
    grad_one = lax.dot_general(grad_query, query_weight, contract_last, preferred_element_type=f32)
    grad_one = grad_one + lax.dot_general(
        grad_keys, key_weight, contract_last, preferred_element_type=f32
    )
    grad_one = grad_one + lax.dot_general(
        grad_values, value_weight, contract_last, preferred_element_type=f32
    )
    grad_one = lax.psum(grad_one.astype(jnp.bfloat16), "tp").astype(jnp.float32)
    _, first_pull = jax.vjp(layer_norm, inputs, first_gain, first_bias)
    grad_input_norm, first_gain_grad, first_bias_grad = first_pull(grad_one)
    input_grad = grad_middle + grad_input_norm
    norm_grads = jnp.stack(
        [first_gain_grad, first_bias_grad, second_gain_grad, second_bias_grad], axis=1
    )
    summed_parts = (
        lax.psum_scatter(query_grad, "blk", scatter_dimension=0, tiled=True),
        lax.psum_scatter(key_grad, "blk", scatter_dimension=0, tiled=True),
        lax.psum_scatter(value_grad, "blk", scatter_dimension=0, tiled=True),
        lax.psum_scatter(output_grad, "blk", scatter_dimension=0, tiled=True),
        lax.psum_scatter(up_grad, "blk", scatter_dimension=0, tiled=True),
        lax.psum_scatter(down_grad, "blk", scatter_dimension=0, tiled=True),
        lax.psum_scatter(norm_grads, "blk", scatter_dimension=0, tiled=True),
    )
    totals = (
        lax.all_gather(summed_parts[0].astype(jnp.bfloat16), "blk", axis=0, tiled=True).astype(
            jnp.float32
        ),
        lax.all_gather(summed_parts[1].astype(jnp.bfloat16), "blk", axis=0, tiled=True).astype(
            jnp.float32
        ),
        lax.all_gather(summed_parts[2].astype(jnp.bfloat16), "blk", axis=0, tiled=True).astype(
            jnp.float32
        ),
        lax.all_gather(summed_parts[3].astype(jnp.bfloat16), "blk", axis=0, tiled=True).astype(
            jnp.float32
        ),
        lax.all_gather(summed_parts[4].astype(jnp.bfloat16), "blk", axis=0, tiled=True).astype(
            jnp.float32
        ),
        lax.all_gather(summed_parts[5].astype(jnp.bfloat16), "blk", axis=0, tiled=True).astype(
            jnp.float32
        ),
        lax.all_gather(summed_parts[6].astype(jnp.bfloat16), "blk", axis=0, tiled=True).astype(
            jnp.float32
        ),
    )
    return (
        layer_out,
        input_grad,
        totals[6][:, 0],
        totals[6][:, 1],
        totals[6][:, 2],
        totals[6][:, 3],
        totals[0],
        totals[1],
        totals[2],
        totals[3],
        totals[4],
        totals[5],
    )


HINT = pl.CostEstimate(flops=1, bytes_accessed=1, transcendentals=1)


def full(shape):
    return pl.BlockSpec(shape, lambda *_: (0,) * len(shape))


def attend_kernel(q_ref, k_ref, v_ref, mine_ref, all_ref, out_ref):
    lane = lax.broadcasted_iota(jnp.int32, q_ref.shape, 1) // HEAD
    mask = mine_ref[...] == all_ref[...]
    parts = []
    for head in range(2):
        q = jnp.where(lane == head, q_ref[...], jnp.zeros_like(q_ref[...]))
        s = lax.dot_general(q, k_ref[...], LAST, preferred_element_type=f32)
        s = jnp.where(mask, s, NEG)
        p = jnp.exp(s - jnp.max(s, axis=1, keepdims=True))
        total = jnp.sum(p, axis=1, keepdims=True)
        part = jnp.dot(p.astype(bf16), v_ref[...], preferred_element_type=f32)
        parts.append(part / total)
    out_ref[...] = jnp.where(lane == 0, parts[0], parts[1]).astype(bf16)


def attend(q, k, v, scene_mine, scene_all):
    rows, width = q.shape
    total = k.shape[0]
    pair = 2 * HEAD
    return pl.pallas_call(
        attend_kernel,
        grid=(width // pair,),
        in_specs=[
            pl.BlockSpec((rows, pair), lambda i: (0, i)),
            pl.BlockSpec((total, pair), lambda i: (0, i)),
            pl.BlockSpec((total, pair), lambda i: (0, i)),
            full((rows, 1)),
            full((1, total)),
        ],
        out_specs=pl.BlockSpec((rows, pair), lambda i: (0, i)),
        out_shape=jax.ShapeDtypeStruct((rows, width), bf16),
        cost_estimate=HINT,
        name="attend",
    )(q, k, v, scene_mine.reshape(rows, 1), scene_all.reshape(1, total))


QT = 256
KT = 512


def prepare_kernel(lo_ref, hi_ref, part_ref, t_ref, n_ref, row_ref, col_ref, p_ref, s_s):
    step = pl.program_id(0)
    lo, hi = lo_ref[step], hi_ref[step]
    blocks = [4 * step + 2 * i + part_ref[0] for i in range(2)]
    q = jnp.concatenate([t_ref[b, 0:HEAD, :] for b in blocks], axis=1)
    q = jnp.concatenate([q, jnp.zeros_like(q)], axis=0)
    row = row_ref[...]

    def score(j, top):
        keys = pl.ds(pl.multiple_of(j * KT, KT), KT)
        s = jnp.dot(n_ref[keys, 0 : 2 * HEAD], q, preferred_element_type=f32)
        s = jnp.where(col_ref[keys, :] == row, s, NEG)
        s_s[keys, :] = s
        return jnp.maximum(top, jnp.max(s, axis=0, keepdims=True))

    top = lax.fori_loop(lo, hi, score, jnp.full((1, QT), NEG, f32))

    def weigh(j, total):
        keys = pl.ds(pl.multiple_of(j * KT, KT), KT)
        p = jnp.exp(s_s[keys, :] - top)
        s_s[keys, :] = p
        return total + jnp.sum(p, axis=0, keepdims=True)

    total = lax.fori_loop(lo, hi, weigh, jnp.zeros((1, QT), f32))
    share = 1.0 / total

    def store(j, carry):
        keys = pl.ds(pl.multiple_of(j * KT, KT), KT)
        p_ref[0, keys, :] = (s_s[keys, :] * share).astype(bf16)
        return carry

    lax.fori_loop(lo, hi, store, 0)


def prepare(bounds, head_t, head_n, scene_queries, scene_all):
    total = head_n.shape[0]
    tiles = scene_queries.shape[0] // QT
    return pl.pallas_call(
        prepare_kernel,
        grid_spec=pltpu.PrefetchScalarGridSpec(
            num_scalar_prefetch=3,
            grid=(tiles,),
            in_specs=[
                full(head_t.shape),
                full((total, 4 * HEAD)),
                pl.BlockSpec((1, QT), lambda i, *_: (0, i)),
                full((total, 1)),
            ],
            out_specs=pl.BlockSpec((1, total, QT), lambda i, *_: (i, 0, 0)),
            scratch_shapes=[pltpu.VMEM((total, QT), f32)],
        ),
        out_shape=jax.ShapeDtypeStruct((tiles, total, QT), bf16),
        cost_estimate=HINT,
        name="prepare",
    )(*bounds, head_t, head_n, scene_queries.reshape(1, -1), scene_all.reshape(total, 1))


def back_kernel(
    lo_ref, hi_ref, part_ref, p_ref, ga_ref, t_ref, n_ref, h_ref,
    gq_out, mine_out, other_out, slice_mine, slice_other, dp_s, gkv_s, g_s,
):
    step = pl.program_id(0)
    part = part_ref[0]
    rows = ga_ref.shape[2]
    count = t_ref.shape[0]
    lo, hi = lo_ref[step], hi_ref[step]

    @pl.when(step == 0)
    def _():
        gkv_s[...] = jnp.zeros_like(gkv_s)
        g_s[...] = jnp.zeros_like(g_s)

    blocks = [4 * step + 2 * i + part for i in range(2)]
    spans = [pl.ds(pl.multiple_of(b * rows, rows), rows) for b in blocks]
    ga_t = jnp.concatenate([ga_ref[0], ga_ref[1]], axis=1)
    ga_t = jnp.concatenate([ga_t, jnp.zeros_like(ga_t)], axis=0)
    ga = ga_t.T
    kq = jnp.concatenate([n_ref[span, 0 : 2 * HEAD] for span in spans], axis=0)
    q = jnp.where(lax.broadcasted_iota(jnp.int32, kq.shape, 1) >= HEAD, kq, jnp.zeros_like(kq))

    def first(j, delta):
        keys = pl.ds(pl.multiple_of(j * KT, KT), KT)
        p = p_ref[0, keys, :]
        dp = jnp.dot(n_ref[keys, 2 * HEAD :], ga_t, preferred_element_type=f32)
        dp_s[keys, :] = dp
        gkv_s[keys, :] += jnp.dot(p, ga, preferred_element_type=f32)
        return delta + jnp.sum(p.astype(f32) * dp, axis=0, keepdims=True)

    delta = lax.fori_loop(lo, hi, first, jnp.zeros((1, QT), f32))

    def second(j, gq):
        keys = pl.ds(pl.multiple_of(j * KT, KT), KT)
        ds = (p_ref[0, keys, :].astype(f32) * (dp_s[keys, :] - delta)).astype(bf16)
        gkv_s[keys, :] += jnp.dot(ds, q, preferred_element_type=f32)
        near = KT // rows
        k_t = jnp.concatenate([t_ref[j * near + i, HEAD : 2 * HEAD, :] for i in range(near)], axis=1)
        return gq + jnp.dot(k_t, ds, preferred_element_type=f32)

    gq = lax.fori_loop(lo, hi, second, jnp.zeros((HEAD, QT), f32))
    gq = (gq * HEAD ** (-0.5)).astype(bf16)
    for i in range(2):
        tile = gq[:, i * rows : (i + 1) * rows]
        gq_out[2 * step + i] = tile
        g_s[0:HEAD, spans[i]] = tile

    @pl.when(step == pl.num_programs(0) - 1)
    def _():
        for m in range(count // 2):
            for out, b in ((mine_out, 2 * m + part), (other_out, 2 * m + 1 - part)):
                tokens = pl.ds(pl.multiple_of(b * rows, rows), rows)
                both = gkv_s[tokens, :].T
                out[m] = both.astype(out.dtype)
                g_s[HEAD:, tokens] = both.astype(bf16)
        slices = jnp.dot(g_s[...], h_ref[...], preferred_element_type=f32)
        wide = slice_mine.shape[1]
        left, right = slices[:, :wide], slices[:, wide:]
        slice_mine[...] = jnp.where(part == 0, left, right)
        slice_other[...] = jnp.where(part == 0, right, left).astype(bf16)


def back(bounds, p, ga, head_t, head_n, h1):
    count, three, rows = head_t.shape
    total, width = h1.shape
    half = count // 2
    kept = [
        ((half, HEAD, rows), bf16),
        ((half, 2 * HEAD, rows), f32),
        ((half, 2 * HEAD, rows), bf16),
        ((three, width // 2), f32),
        ((three, width // 2), bf16),
    ]
    return pl.pallas_call(
        back_kernel,
        grid_spec=pltpu.PrefetchScalarGridSpec(
            num_scalar_prefetch=3,
            grid=(p.shape[0],),
            in_specs=[
                pl.BlockSpec((1, total, QT), lambda i, *_: (i, 0, 0)),
                pl.BlockSpec((2, HEAD, rows), lambda i, *_: (i, 0, 0)),
                full(head_t.shape),
                full((total, 4 * HEAD)),
                full(h1.shape),
            ],
            out_specs=[full(shape) for shape, _ in kept],
            scratch_shapes=[
                pltpu.VMEM((total, QT), f32),
                pltpu.VMEM((total, 2 * HEAD), f32),
                pltpu.VMEM((three, total), bf16),
            ],
        ),
        out_shape=[jax.ShapeDtypeStruct(shape, kind) for shape, kind in kept],
        cost_estimate=HINT,
        name="back",
    )(*bounds, p, ga, head_t, head_n, h1)


FT = 256
TT = 1024


def gelu_both(pre, grad):
    half = 0.5 * (1.0 + lax.erf(pre * 0.7071067811865476))
    slope = half + pre * (jnp.exp(-0.5 * pre * pre) * 0.3989422804014327)
    return (pre * half).astype(bf16), (grad * slope).astype(bf16)


def ffn_kernel(h_ref, g_ref, up_ref, down_ref, *outs):
    up_out, down_out = outs[-2:]
    for j in range(h_ref.shape[0] // TT):
        rows = slice(j * TT, (j + 1) * TT)
        pre = jnp.dot(h_ref[rows, :], up_ref[...], preferred_element_type=f32)
        grad = jnp.dot(g_ref[rows, :], down_ref[...], preferred_element_type=f32)
        act, grad_pre = gelu_both(pre, grad)
        up = lax.dot_general(h_ref[rows, :], grad_pre, FIRST, preferred_element_type=f32)
        down = lax.dot_general(g_ref[rows, :], act, FIRST, preferred_element_type=f32)
        if j == 0:
            up_out[...] = up
            down_out[...] = down
        else:
            up_out[...] += up
            down_out[...] += down


def ffn_grads(h, g, up_weight, down_weight, tiles, held):
    total, width = h.shape
    hidden = up_weight.shape[1]
    first, last = tiles
    tokens = pl.BlockSpec((total, width), lambda i: (0, 0), pipeline_mode=pl.Buffered(1))
    units = pl.BlockSpec((width, FT), lambda i: (0, first + i))
    return pl.pallas_call(
        ffn_kernel,
        grid=(last - first,),
        in_specs=[tokens, tokens, units, units] + [pl.BlockSpec(memory_space=pl.ANY)] * len(held),
        out_specs=[units] * 2,
        out_shape=[jax.ShapeDtypeStruct((width, hidden), f32)] * 2,
        input_output_aliases={4: 0, 5: 1} if held else {},
        cost_estimate=pl.CostEstimate(
            flops=8 * total * width * FT * (last - first), bytes_accessed=4 * total * width, transcendentals=0
        ),
        name="ffn_grads",
    )(h, g, up_weight, down_weight, *held)


def project_kernel(where_ref, side_ref, mine_ref, other_ref, gain_ref, bias_ref, k_ref, v_ref, t_ref, n_ref, *rest):
    outs, scratch, sem = rest[-11:-6], rest[-6:-1], rest[-1]
    h_s, k_s, v_s, t_s, n_s = scratch
    n, half, width = mine_ref.shape
    rows = 2 * half
    copies = []

    def send(i):
        for b in range(n):
            copy = pltpu.make_async_copy(scratch[i].at[b], outs[i].at[where_ref[b]], sem.at[i, b])
            copy.start()
            copies.append(copy)

    mine, other = mine_ref[...], other_ref[...]
    first = side_ref[0] == 0
    block = jnp.concatenate([jnp.where(first, mine, other), jnp.where(first, other, mine)], axis=1)
    block = block.reshape(n * rows, width).astype(f32)
    h = layer_norm(block, gain_ref[...], bias_ref[...]).astype(bf16)
    h_s[...] = h.reshape(n, rows, width)
    send(0)
    k_s[...] = jnp.dot(h, k_ref[...], preferred_element_type=f32).astype(bf16).reshape(k_s.shape)
    send(1)
    v_s[...] = jnp.dot(h, v_ref[...], preferred_element_type=f32).astype(bf16).reshape(v_s.shape)
    send(2)
    across = lax.dot_general(t_ref[...], h, LAST, preferred_element_type=f32).astype(bf16)
    for b in range(n):
        t_s[b] = across[:, b * rows : (b + 1) * rows]
    send(3)
    n_s[...] = jnp.dot(h, n_ref[...], preferred_element_type=f32).astype(bf16).reshape(n_s.shape)
    send(4)
    for copy in copies:
        copy.wait()


def project_blocks(where, side, mine, other, params, count, held):
    n, half, width = mine.shape
    _, _, key_weight, value_weight, head_t, head_n = params
    shapes = [
        (2 * half, width),
        (2 * half, key_weight.shape[1]),
        (2 * half, value_weight.shape[1]),
        (head_t.shape[0], 2 * half),
        (2 * half, head_n.shape[1]),
    ]
    return pl.pallas_call(
        project_kernel,
        grid_spec=pltpu.PrefetchScalarGridSpec(
            num_scalar_prefetch=2,
            grid=(1,),
            in_specs=[full(mine.shape)] * 2
            + [full(p.shape) for p in params]
            + [pl.BlockSpec(memory_space=pl.ANY)] * len(held),
            out_specs=[pl.BlockSpec(memory_space=pl.ANY)] * 5,
            scratch_shapes=[pltpu.VMEM((n,) + shape, bf16) for shape in shapes]
            + [pltpu.SemaphoreType.DMA((5, n))],
        ),
        out_shape=[jax.ShapeDtypeStruct((count,) + shape, bf16) for shape in shapes],
        input_output_aliases={10 + i: i for i in range(5)} if held else {},
        cost_estimate=HINT,
        name="project_blocks",
    )(where, side, mine, other, *params, *held)


def own_kernel(h_ref, g_ref, up_ref, down_ref, feed_out, grad_out, feed_s, grad_s):
    step = pl.program_id(0)
    pre = jnp.dot(h_ref[...], up_ref[...], preferred_element_type=f32)
    grad = jnp.dot(g_ref[...], down_ref[...], preferred_element_type=f32)
    act, grad_pre = gelu_both(pre, grad)
    feed = lax.dot_general(act, down_ref[...], LAST, preferred_element_type=f32)
    back_ = lax.dot_general(grad_pre, up_ref[...], LAST, preferred_element_type=f32)

    @pl.when(step == 0)
    def _():
        feed_s[...] = feed
        grad_s[...] = back_

    @pl.when(step > 0)
    def _():
        feed_s[...] += feed
        grad_s[...] += back_

    @pl.when(step == pl.num_programs(0) - 1)
    def _():
        feed_out[...] = feed_s[...].astype(bf16)
        grad_out[...] = grad_s[...].astype(bf16)


def own_ffn(h, g, up_weight, down_weight):
    rows, width = h.shape
    hidden = up_weight.shape[1]
    tile = 512
    return pl.pallas_call(
        own_kernel,
        grid=(hidden // tile,),
        in_specs=[full(h.shape), full(g.shape)] + [pl.BlockSpec((width, tile), lambda i: (0, i))] * 2,
        out_specs=[full(h.shape)] * 2,
        out_shape=[jax.ShapeDtypeStruct(h.shape, bf16)] * 2,
        scratch_shapes=[pltpu.VMEM(h.shape, f32)] * 2,
        cost_estimate=HINT,
        name="own_ffn",
    )(h, g, up_weight, down_weight)


def finish_heads_kernel(at_ref, *refs):
    heads, outs = refs[:4], refs[4:]
    plane, row, part = at_ref[0], at_ref[1], at_ref[2]
    wide = heads[0].shape[2]
    for s in range(4):
        z = lax.rem(plane - s + 4, 4)
        for k, x in ((0, part), (1, 1 - part)):
            rows = pl.ds(pl.multiple_of(x * wide, wide), wide)
            lanes = pl.ds(pl.multiple_of(z * 2 * HEAD, 2 * HEAD), 2 * HEAD)
            for i in range(3):
                near = heads[k][s, i * HEAD : (i + 1) * HEAD, :]
                far = heads[k + 2][s, i * HEAD : (i + 1) * HEAD, :]
                pair = [jnp.where(row == 0, near, far), jnp.where(row == 0, far, near)]
                outs[i][rows, lanes] = jnp.concatenate(pair, axis=0).astype(f32).T


def finish_rows_kernel(at_ref, *refs):
    pieces, out_ref = refs[:4], refs[4]
    slots = pieces[0].shape[1]
    for k in range(4):
        for s in range(4):
            z = lax.rem(at_ref[0] - s + 4, 4)
            y = at_ref[1] if k < 2 else 1 - at_ref[1]
            x = at_ref[2] if k % 2 == 0 else 1 - at_ref[2]
            at = pl.multiple_of((z * 4 + y * 2 + x) * slots, slots)
            out_ref[pl.ds(at, slots), :] = pieces[k][s].astype(f32)


def finish(kernel, at, pieces, outs, width, columns):
    return pl.pallas_call(
        kernel,
        grid_spec=pltpu.PrefetchScalarGridSpec(
            num_scalar_prefetch=1,
            grid=(1,),
            in_specs=[full(p.shape) for p in pieces],
            out_specs=[full((width, columns))] * outs,
        ),
        out_shape=[jax.ShapeDtypeStruct((width, columns), f32)] * outs,
        cost_estimate=HINT,
        name="finish",
    )(at, *pieces)


def shuffle(block, target):
    return lax.ppermute(block, "blk", [(i, target(i)) for i in range(16)])


def over_core(block):
    return lax.ppermute(block, "tp", [(0, 1), (1, 0)])


def gather_column(unit):
    return jnp.stack([unit] + [shuffle(unit, lambda i, s=s: (i + 4 * s) % 16) for s in (1, 2, 3)])


def gather_plane(column):
    return (column,) + tuple(shuffle(column, lambda i, k=k: i ^ k) for k in (1, 2, 3))


def units_at(place):
    z, flat = place // 4, place % 4
    return [jnp.stack([((z - s) % 4) * 4 + (flat ^ k) for s in range(4)]) for k in range(4)]


def after(value, *first):
    return lax.optimization_barrier((value,) + first)[0]


def both_halves(low):
    low = lax.optimization_barrier(low)
    return low.astype(f32) + over_core(low).astype(f32)


def fast_body(
    tokens,
    first_gain,
    first_bias,
    second_gain,
    second_bias,
    query_weight,
    key_weight,
    value_weight,
    output_weight,
    up_weight,
    down_weight,
    cotangent,
    scene_len,
):
    count = lax.axis_size("blk")
    place = lax.axis_index("blk")
    side = lax.axis_index("tp")
    rows, width = tokens.shape
    total = rows * count
    heads_here = query_weight.shape[1] // HEAD
    share = count // heads_here
    scale = HEAD ** (-0.5)
    head_at = (place // share) * HEAD
    part = place % share

    def half_of(block):
        return lax.dynamic_slice_in_dim(block, side * (rows // 2), rows // 2, 0)

    ends = jnp.cumsum(scene_len)
    starts = ends - scene_len
    positions = jnp.arange(total, dtype=jnp.int32)
    scene_all = jnp.sum((positions[:, None] >= ends[None, :]).astype(jnp.int32), axis=1)
    scene_mine = lax.dynamic_slice_in_dim(scene_all, place * rows, rows)
    scene_queries = lax.dynamic_index_in_dim(scene_all.reshape(-1, share, rows), part, 1, False).reshape(-1)
    firsts = jnp.arange(total // QT // share, dtype=jnp.int32) * QT * share + part * rows
    lasts = firsts + QT * share - rows
    lowest = jnp.max(jnp.where(starts[None, :] <= firsts[:, None], starts[None, :], 0), axis=1)
    highest = jnp.min(jnp.where(ends[None, :] >= lasts[:, None], ends[None, :], total), axis=1)
    bounds = (lowest // KT, (highest + KT - 1) // KT, part.reshape(1))

    def head_of(weight):
        return lax.dynamic_slice_in_dim(weight, head_at, HEAD, 1)

    head_query = head_of(query_weight) * jnp.asarray(scale, bf16)
    head_key, head_value = head_of(key_weight), head_of(value_weight)
    head_t = jnp.concatenate([head_query, head_key, head_value], axis=1).T
    head_n = jnp.concatenate([head_key, head_query, head_value, jnp.zeros_like(head_value)], axis=1)
    params = (first_gain.reshape(1, -1), first_bias.reshape(1, -1), key_weight, value_weight, head_t, head_n)

    inputs = tokens.astype(f32)
    h1_mine = layer_norm(inputs, first_gain, first_bias).astype(bf16)
    query = jnp.dot(h1_mine, query_weight, preferred_element_type=f32).astype(bf16) * jnp.asarray(scale, bf16)

    g_all = lax.all_gather(half_of(cotangent), ("blk", "tp"), axis=0, tiled=True)
    where = units_at(place)
    column = gather_column(half_of(tokens))
    across_x = shuffle(column, lambda i: i ^ 1)
    across_y = shuffle(column, lambda i: i ^ 2)
    made = project_blocks(where[0], side.reshape(1), column, over_core(column), params, count, ())
    across_y = after(across_y, made[0])
    diagonal = shuffle(across_y, lambda i: i ^ 1)
    for piece, at in zip((after(across_x, across_y), across_y, diagonal), where[1:], strict=True):
        piece = after(piece, made[0]) if piece is diagonal else piece
        made = project_blocks(at, side.reshape(1), piece, over_core(piece), params, count, made)
    h1_all, keys, values, head_t, head_n = made
    h1_all = h1_all.reshape(total, width)
    head_n = head_n.reshape(total, -1)

    attended = attend(query, keys.reshape(total, -1), values.reshape(total, -1), scene_mine, scene_all)
    branch = lax.dot_general(attended, output_weight, LAST, preferred_element_type=f32)
    middle = inputs + both_halves(branch.astype(bf16))
    h2 = layer_norm(middle, second_gain, second_bias).astype(bf16)
    h2_all = lax.all_gather(after(half_of(h2), g_all), ("blk", "tp"), axis=0, tiled=True)

    feed, grad_two = own_ffn(h2, cotangent, up_weight, down_weight)
    grad_two = both_halves(grad_two)
    _, second_pull = jax.vjp(layer_norm, middle, second_gain, second_bias)
    grad_middle, second_gain_grad, second_bias_grad = second_pull(grad_two)
    grad_middle = cotangent.astype(f32) + grad_middle
    grad_middle_low = grad_middle.astype(bf16)
    grad_attended = lax.dot_general(
        output_weight, grad_middle_low, (((0,), (1,)), ((), ())), preferred_element_type=f32
    ).astype(bf16)
    alike = [list(range(r, count, share)) for r in range(share)]
    to_heads = grad_attended.reshape(heads_here, HEAD, rows)
    ga = lax.all_to_all(to_heads, "blk", 0, 0, tiled=True, axis_index_groups=alike)
    p = prepare(bounds, after(head_t, to_heads), head_n, scene_queries, scene_all)

    grad_q, kept, given, slice_kept, slice_given = back(
        bounds, p, ga, head_t, head_n, h1_all
    )
    output_part = lax.dot_general(after(grad_middle_low, slice_given), attended, FIRST, preferred_element_type=f32)
    output_part = output_part.reshape(count // share, share, width // count, -1)
    output_kept = lax.dynamic_index_in_dim(output_part, part, 1, False)
    output_given = lax.dynamic_index_in_dim(output_part, 1 - part, 1, False).astype(bf16)
    output_half = (output_kept + shuffle(output_given, lambda i: i ^ 1).astype(f32)).astype(bf16)

    head_slice = (slice_kept + shuffle(slice_given, lambda i: i ^ 1).astype(f32)).astype(bf16)
    column = gather_column(head_slice)

    given = after(given, head_slice)
    kept = (kept + shuffle(given, lambda i: i ^ 1).astype(f32)).astype(bf16)
    parcel = jnp.concatenate([grad_q, kept, output_half.reshape(count // share, -1, rows)], axis=1)
    home = lax.all_to_all(after(parcel, column), "blk", 0, 0, tiled=True, axis_index_groups=alike)
    heads = gather_plane(column)

    layer_out = (middle + both_halves(after(feed, parcel))).astype(bf16)
    at = jnp.stack([place // 4, (place // 2) % 2, place % 2])
    held = ffn_grads(after(h2_all, column, parcel), g_all, up_weight, down_weight, (0, 4), ())

    home = after(home, held[0], *heads)
    output_slice = home[:, 3 * HEAD :].reshape(count // share, width // count, -1)
    output_slice = jnp.sum(output_slice.astype(f32), axis=0).astype(bf16)
    home = home[:, : 3 * HEAD].reshape(heads_here, 3, HEAD, rows)
    grad_one = 0.0
    for i, weight in enumerate((query_weight, value_weight, key_weight)):
        grad_one = grad_one + lax.dot_general(
            home[:, i].reshape(-1, rows), weight, (((0,), (1,)), ((), ())), preferred_element_type=f32
        )
    grad_one = both_halves(grad_one.astype(bf16))
    _, first_pull = jax.vjp(layer_norm, inputs, first_gain, first_bias)
    grad_input, first_gain_grad, first_bias_grad = first_pull(grad_one)
    input_grad = grad_middle + grad_input
    norm_part = jnp.stack([first_gain_grad, first_bias_grad, second_gain_grad, second_bias_grad])
    norm_parts = lax.all_to_all(
        jnp.broadcast_to(norm_part[None], (count,) + norm_part.shape), "blk", 0, 0, tiled=True
    )

    column = gather_column(output_slice)
    up_grad, down_grad = ffn_grads(
        after(h2_all, norm_part, *heads), g_all, up_weight, down_weight, (4, 8), held
    )
    rest = gather_plane(after(column, up_grad))
    norm_sums = jnp.sum(after(norm_parts, up_grad), axis=0)
    heads = (after(heads[0], up_grad),) + heads[1:]
    query_grad, value_grad, key_grad = finish(finish_heads_kernel, at, heads, 3, width, heads_here * HEAD)
    (output_grad,) = finish(finish_rows_kernel, at, rest, 1, width, heads_here * HEAD)
    return (
        layer_out,
        input_grad,
        norm_sums[0],
        norm_sums[1],
        norm_sums[2],
        norm_sums[3],
        query_grad,
        key_grad,
        value_grad,
        output_grad,
        up_grad,
        down_grad,
    )


def solution(mesh):
    body = fast_body if mesh.shape["blk"] == 16 else ring_body
    return jax.shard_map(
        body,
        mesh=mesh,
        in_specs=(
            P("blk", None),
            P(),
            P(),
            P(),
            P(),
            P(None, "tp"),
            P(None, "tp"),
            P(None, "tp"),
            P(None, "tp"),
            P(None, "tp"),
            P(None, "tp"),
            P("blk", None),
            P(),
        ),
        out_specs=(
            P("blk", None),
            P("blk", None),
            P(),
            P(),
            P(),
            P(),
            P(None, "tp"),
            P(None, "tp"),
            P(None, "tp"),
            P(None, "tp"),
            P(None, "tp"),
            P(None, "tp"),
        ),
        check_vma=False,
    )
```

```python
import jax
import jax.numpy as jnp
from jax import lax
from jax.experimental import pallas as pl
from jax.experimental.pallas import tpu as pltpu
from jax.sharding import PartitionSpec as P

HEAD = 64
NEG = -1e30
f32 = jnp.float32
bf16 = jnp.bfloat16
LAST = (((1,), (1,)), ((), ()))
FIRST = (((0,), (0,)), ((), ()))


def from_behind(block, axis, distance):
    devices = range(lax.axis_size(axis))
    route = [((i - distance) % len(devices), i) for i in devices]
    return lax.ppermute(block, axis, route)


def layer_norm(values, gain, bias):
    center = values - jnp.mean(values, axis=-1, keepdims=True)
    spread = jnp.mean(center * center, axis=-1, keepdims=True)
    return center * lax.rsqrt(spread + 1e-05) * gain + bias


def move_grads(grad_keys, grad_values, offset):
    return (
        from_behind(grad_keys.astype(jnp.bfloat16), "blk", offset).astype(grad_keys.dtype),
        from_behind(grad_values.astype(jnp.bfloat16), "blk", offset).astype(grad_values.dtype),
    )


def ring_body(
    tokens,
    first_gain,
    first_bias,
    second_gain,
    second_bias,
    query_weight,
    key_weight,
    value_weight,
    output_weight,
    up_weight,
    down_weight,
    cotangent,
    scene_len,
):
    count = lax.axis_size("blk")
    place = lax.axis_index("blk")
    rows = tokens.shape[0]
    heads_here = query_weight.shape[1] // HEAD
    scale = HEAD ** (-0.5)
    ends = jnp.cumsum(scene_len)
    contract_last = (((1,), (1,)), ((), ()))
    contract_first = (((0,), (0,)), ((), ()))

    def scene_of(source):
        places = source * rows + jnp.arange(rows, dtype=jnp.int32)
        return jnp.sum((places[:, None] >= ends[None, :]).astype(jnp.int32), axis=1)

    mine = scene_of(place)

    def shares(source):
        other = scene_of(source)
        return jnp.maximum(mine[0], other[0]) <= jnp.minimum(mine[-1], other[-1])

    directions = (1,)
    steps = count - 1

    def source_of(way, turn):
        raw_source = place - way * turn
        return (raw_source % count, jnp.array(True))

    inputs = tokens.astype(f32)
    normed_one = layer_norm(inputs, first_gain, first_bias).astype(bf16)

    def project(weight):
        return jnp.dot(normed_one, weight, preferred_element_type=f32).astype(bf16)

    query = project(query_weight).reshape(rows, heads_here, HEAD)
    keys = project(key_weight).reshape(rows, heads_here, HEAD)
    values = project(value_weight).reshape(rows, heads_here, HEAD)

    def scores_of(key_block, source):
        mask = mine[:, None] == scene_of(source)[None, :]
        scores = jnp.einsum("qhd,khd->hqk", query, key_block, preferred_element_type=f32) * scale
        return (jnp.where(mask[None], scores, -1e30), mask)

    def absorb(state, key_block, value_block, source):
        top, total, summed = state
        scores, mask = scores_of(key_block, source)
        new_top = jnp.maximum(top, jnp.max(scores, axis=2))
        factor = jnp.exp(top - new_top)
        weights = jnp.where(mask[None], jnp.exp(scores - new_top[:, :, None]), 0.0)
        total = total * factor + jnp.sum(weights, axis=2)
        summed = summed * factor.T[:, :, None] + jnp.einsum(
            "hqk,khd->qhd", weights.astype(bf16), value_block, preferred_element_type=f32
        )
        return (new_top, total, summed)

    start = (
        jnp.full((heads_here, rows), -1e30, f32),
        jnp.zeros((heads_here, rows), f32),
        jnp.zeros((rows, heads_here, HEAD), f32),
    )
    state = absorb(start, keys, values, place)
    way = directions[0]

    def turn_forward(turn, carry):
        current, key_block, value_block = carry
        key_block, value_block = from_behind((key_block, value_block), "blk", way)
        source, inside = source_of(way, turn)
        current = lax.cond(
            inside & shares(source),
            lambda held: absorb(held, key_block, value_block, source),
            lambda held: held,
            current,
        )
        return (current, key_block, value_block)

    state, _, _ = lax.fori_loop(1, steps + 1, turn_forward, (state, keys, values))
    top, total, summed = state
    attended = summed / total.T[:, :, None]
    log_total = top + jnp.log(total)
    attended_low = attended.reshape(rows, -1).astype(bf16)
    branch = lax.dot_general(attended_low, output_weight, contract_last, preferred_element_type=f32)
    branch = lax.psum(branch.astype(jnp.bfloat16), "tp").astype(jnp.float32)
    middle = inputs + branch
    normed_two = layer_norm(middle, second_gain, second_bias).astype(bf16)
    before = jnp.dot(normed_two, up_weight, preferred_element_type=f32)
    active = jax.nn.gelu(before, approximate=False).astype(bf16)
    feed = lax.dot_general(active, down_weight, contract_last, preferred_element_type=f32)
    feed = lax.psum(feed.astype(jnp.bfloat16), "tp").astype(jnp.float32)
    layer_out = (middle + feed).astype(bf16)
    grad_out = cotangent.astype(f32)
    down_grad = lax.dot_general(cotangent, active, contract_first, preferred_element_type=f32)
    grad_active = jnp.dot(cotangent, down_weight, preferred_element_type=f32)
    _, gelu_pull = jax.vjp(lambda arg: jax.nn.gelu(arg, approximate=False), before)
    grad_before = gelu_pull(grad_active)[0].astype(bf16)
    up_grad = lax.dot_general(normed_two, grad_before, contract_first, preferred_element_type=f32)
    grad_two = lax.dot_general(grad_before, up_weight, contract_last, preferred_element_type=f32)
    grad_two = lax.psum(grad_two.astype(jnp.bfloat16), "tp").astype(jnp.float32)
    _, second_pull = jax.vjp(layer_norm, middle, second_gain, second_bias)
    grad_middle_norm, second_gain_grad, second_bias_grad = second_pull(grad_two)
    grad_middle = grad_out + grad_middle_norm
    grad_middle_low = grad_middle.astype(bf16)
    output_grad = lax.dot_general(
        grad_middle_low, attended_low, contract_first, preferred_element_type=f32
    )
    grad_attended = jnp.dot(grad_middle_low, output_weight, preferred_element_type=f32).astype(bf16)
    grad_attended = grad_attended.reshape(rows, heads_here, HEAD)
    delta = jnp.sum(grad_attended * attended, axis=2).T

    def backtrack(grads, key_block, value_block, source):
        grad_query, grad_keys, grad_values = grads
        scores, mask = scores_of(key_block, source)
        probs = jnp.where(mask[None], jnp.exp(scores - log_total[:, :, None]), 0.0)
        grad_values = grad_values + jnp.einsum(
            "hqk,qhd->khd", probs.astype(bf16), grad_attended, preferred_element_type=f32
        )
        grad_probs = jnp.einsum(
            "qhd,khd->hqk", grad_attended, value_block, preferred_element_type=f32
        )
        grad_scores = (probs * (grad_probs - delta[:, :, None]) * scale).astype(bf16)
        grad_query = grad_query + jnp.einsum(
            "hqk,khd->qhd", grad_scores, key_block, preferred_element_type=f32
        )
        grad_keys = grad_keys + jnp.einsum(
            "hqk,qhd->khd", grad_scores, query, preferred_element_type=f32
        )
        return (grad_query, grad_keys, grad_values)

    empty = jnp.zeros((rows, heads_here, HEAD), f32)
    grad_query, home_keys, home_values = backtrack((empty, empty, empty), keys, values, place)
    way = directions[0]

    def turn_backward(turn, carry):
        grad_q, key_block, value_block, grad_k, grad_v = carry
        key_block, value_block = from_behind((key_block, value_block), "blk", way)
        grad_k, grad_v = move_grads(grad_k, grad_v, way)
        source, inside = source_of(way, turn)
        grad_q, grad_k, grad_v = lax.cond(
            inside & shares(source),
            lambda held: backtrack(held, key_block, value_block, source),
            lambda held: held,
            (grad_q, grad_k, grad_v),
        )
        return (grad_q, key_block, value_block, grad_k, grad_v)

    grad_query, _, _, moved_keys, moved_values = lax.fori_loop(
        1, steps + 1, turn_backward, (grad_query, keys, values, empty, empty)
    )
    moved_keys, moved_values = move_grads(moved_keys, moved_values, -way * steps)
    home_keys = home_keys + moved_keys
    home_values = home_values + moved_values
    grad_query = grad_query.reshape(rows, -1).astype(bf16)
    grad_keys = home_keys.reshape(rows, -1).astype(bf16)
    grad_values = home_values.reshape(rows, -1).astype(bf16)
    query_grad = lax.dot_general(normed_one, grad_query, contract_first, preferred_element_type=f32)
    key_grad = lax.dot_general(normed_one, grad_keys, contract_first, preferred_element_type=f32)
    value_grad = lax.dot_general(
        normed_one, grad_values, contract_first, preferred_element_type=f32
    )
    grad_one = lax.dot_general(grad_query, query_weight, contract_last, preferred_element_type=f32)
    grad_one = grad_one + lax.dot_general(
        grad_keys, key_weight, contract_last, preferred_element_type=f32
    )
    grad_one = grad_one + lax.dot_general(
        grad_values, value_weight, contract_last, preferred_element_type=f32
    )
    grad_one = lax.psum(grad_one.astype(jnp.bfloat16), "tp").astype(jnp.float32)
    _, first_pull = jax.vjp(layer_norm, inputs, first_gain, first_bias)
    grad_input_norm, first_gain_grad, first_bias_grad = first_pull(grad_one)
    input_grad = grad_middle + grad_input_norm
    norm_grads = jnp.stack(
        [first_gain_grad, first_bias_grad, second_gain_grad, second_bias_grad], axis=1
    )
    summed_parts = (
        lax.psum_scatter(query_grad, "blk", scatter_dimension=0, tiled=True),
        lax.psum_scatter(key_grad, "blk", scatter_dimension=0, tiled=True),
        lax.psum_scatter(value_grad, "blk", scatter_dimension=0, tiled=True),
        lax.psum_scatter(output_grad, "blk", scatter_dimension=0, tiled=True),
        lax.psum_scatter(up_grad, "blk", scatter_dimension=0, tiled=True),
        lax.psum_scatter(down_grad, "blk", scatter_dimension=0, tiled=True),
        lax.psum_scatter(norm_grads, "blk", scatter_dimension=0, tiled=True),
    )
    totals = (
        lax.all_gather(summed_parts[0].astype(jnp.bfloat16), "blk", axis=0, tiled=True).astype(
            jnp.float32
        ),
        lax.all_gather(summed_parts[1].astype(jnp.bfloat16), "blk", axis=0, tiled=True).astype(
            jnp.float32
        ),
        lax.all_gather(summed_parts[2].astype(jnp.bfloat16), "blk", axis=0, tiled=True).astype(
            jnp.float32
        ),
        lax.all_gather(summed_parts[3].astype(jnp.bfloat16), "blk", axis=0, tiled=True).astype(
            jnp.float32
        ),
        lax.all_gather(summed_parts[4].astype(jnp.bfloat16), "blk", axis=0, tiled=True).astype(
            jnp.float32
        ),
        lax.all_gather(summed_parts[5].astype(jnp.bfloat16), "blk", axis=0, tiled=True).astype(
            jnp.float32
        ),
        lax.all_gather(summed_parts[6].astype(jnp.bfloat16), "blk", axis=0, tiled=True).astype(
            jnp.float32
        ),
    )
    return (
        layer_out,
        input_grad,
        totals[6][:, 0],
        totals[6][:, 1],
        totals[6][:, 2],
        totals[6][:, 3],
        totals[0],
        totals[1],
        totals[2],
        totals[3],
        totals[4],
        totals[5],
    )


HINT = pl.CostEstimate(flops=1, bytes_accessed=1, transcendentals=1)
NEAR = pl.BlockSpec(memory_space=pltpu.VMEM)
FAR = pl.BlockSpec(memory_space=pltpu.HBM)
SCALAR = pl.BlockSpec(memory_space=pltpu.SMEM)
QT = 256
KT = 512
FT = 256
TT = 1024


def near(*arrays):
    return [pltpu.with_memory_space_constraint(array, pltpu.VMEM) for array in arrays]


def room(mib):
    return pltpu.CompilerParams(vmem_limit_bytes=mib << 20)


def full(shape):
    return pl.BlockSpec(shape, lambda *_: (0,) * len(shape))


def borders_of(len_ref):
    borders = [len_ref[0]]
    for s in range(1, len_ref.shape[0] - 1):
        borders.append(borders[-1] + len_ref[s])
    return borders


def scenes(positions, borders):
    scene = jnp.zeros_like(positions)
    for border in borders:
        scene += (positions >= border).astype(jnp.int32)
    return scene


def tiles_of(first, last, borders, total):
    low, high = 0, total
    for border in borders:
        low = jnp.where(border <= first, border, low)
    for border in reversed(borders):
        high = jnp.where(border > last, border, high)
    return lax.div(low, KT), lax.div(high + KT - 1, KT)


def project_kernel(flip, ids_ref, mine_ref, other_ref, gain_ref, bias_ref, k_ref, v_ref, t_ref, n_ref, *rest):
    h_out, k_out, v_out, t_out, n_out, h_s = rest[-6:]
    n, half, width = mine_ref.shape
    rows = 2 * half
    first = ids_ref[1] == 0

    def norm(b, carry):
        mine, other = mine_ref[b], other_ref[b]
        block = jnp.concatenate([jnp.where(first, mine, other), jnp.where(first, other, mine)], axis=0)
        h_s[b] = layer_norm(block.astype(f32), gain_ref[...], bias_ref[...]).astype(bf16)
        return carry

    lax.fori_loop(0, n, norm, 0)
    h = h_s[...].reshape(n * rows, width)
    keys = jnp.dot(h, k_ref[...], preferred_element_type=f32).astype(bf16)
    values = jnp.dot(h, v_ref[...], preferred_element_type=f32).astype(bf16)
    across = lax.dot_general(t_ref[...], h, LAST, preferred_element_type=f32).astype(bf16)
    down = jnp.dot(h, n_ref[...], preferred_element_type=f32).astype(bf16)
    for s in range(n):
        at = ((ids_ref[0] - 4 * s) & 15) ^ flip
        tokens = slice(s * rows, (s + 1) * rows)
        h_out[at] = h[tokens]
        k_out[at] = keys[tokens]
        v_out[at] = values[tokens]
        t_out[at] = across[:, tokens]
        n_out[at] = down[tokens]


def project_blocks(flip, ids, mine, other, params, count, held):
    half, width = mine.shape[1:]
    _, _, key_weight, value_weight, head_t, head_n = params
    shapes = [
        (2 * half, width),
        (2 * half, key_weight.shape[1]),
        (2 * half, value_weight.shape[1]),
        (head_t.shape[0], 2 * half),
        (2 * half, head_n.shape[1]),
    ]
    return pl.pallas_call(
        lambda *refs: project_kernel(flip, *refs),
        in_specs=[SCALAR] + [NEAR] * (8 + len(held)),
        out_specs=[NEAR] * 5,
        out_shape=[pltpu.VMEM((count,) + shape, bf16) for shape in shapes],
        scratch_shapes=[pltpu.VMEM((mine.shape[0], 2 * half, width), bf16)],
        input_output_aliases={9 + i: i for i in range(5)} if held else {},
        compiler_params=room(16),
        cost_estimate=HINT,
        name="project_blocks",
    )(ids, *near(mine, other, *params, *held))


def attend_kernel(ids_ref, len_ref, h_ref, k_ref, v_ref, q_ref, o_ref, out_ref, branch_ref, query_s):
    rows, width = out_ref.shape
    total = k_ref.shape[0]
    pair = 2 * HEAD
    borders = borders_of(len_ref)
    mine = scenes(lax.broadcasted_iota(jnp.int32, (rows, 1), 0) + ids_ref[0] * rows, borders)
    mask = mine == scenes(lax.broadcasted_iota(jnp.int32, (1, total), 1), borders)
    query = jnp.dot(h_ref[ids_ref[0]], q_ref[...], preferred_element_type=f32).astype(bf16)
    query = query * jnp.asarray(HEAD ** (-0.5), bf16)
    lane = lax.broadcasted_iota(jnp.int32, (rows, pair), 1) // HEAD
    query_s[...] = query

    def attend_pair(g, carry):
        lanes = pl.ds(pl.multiple_of(g * pair, pair), pair)
        keys, values, queries = k_ref[:, lanes], v_ref[:, lanes], query_s[:, lanes]
        parts = []
        for head in range(2):
            q = jnp.where(lane == head, queries, jnp.zeros_like(queries))
            s = lax.dot_general(q, keys, LAST, preferred_element_type=f32)
            s = jnp.where(mask, s, NEG)
            p = jnp.exp(s - jnp.max(s, axis=1, keepdims=True))
            weight = jnp.sum(p, axis=1, keepdims=True)
            parts.append(jnp.dot(p.astype(bf16), values, preferred_element_type=f32) / weight)
        out_ref[:, lanes] = jnp.where(lane == 0, parts[0], parts[1]).astype(bf16)
        return carry

    lax.fori_loop(0, width // pair, attend_pair, 0)
    branch = lax.dot_general(out_ref[...], o_ref[...], LAST, preferred_element_type=f32)
    branch_ref[...] = branch.astype(bf16)


def attend(ids, scene_len, h, k, v, query_weight, output_weight):
    rows = h.shape[1]
    return pl.pallas_call(
        attend_kernel,
        in_specs=[SCALAR] * 2 + [NEAR] * 5,
        out_specs=[NEAR] * 2,
        out_shape=[
            jax.ShapeDtypeStruct((rows, query_weight.shape[1]), bf16),
            jax.ShapeDtypeStruct((rows, output_weight.shape[0]), bf16),
        ],
        scratch_shapes=[pltpu.VMEM((rows, query_weight.shape[1]), bf16)],
        compiler_params=room(16),
        cost_estimate=HINT,
        name="attend",
    )(ids, scene_len, *near(h, k, v, query_weight, output_weight))


def gelu_both(pre, grad):
    half = 0.5 * (1.0 + lax.erf(pre * 0.7071067811865476))
    slope = half + pre * (jnp.exp(-0.5 * pre * pre) * 0.3989422804014327)
    return (pre * half).astype(bf16), (grad * slope).astype(bf16)


def own_kernel(h_ref, g_ref, up_ref, down_ref, feed_out, grad_out, feed_s, grad_s):
    step = pl.program_id(0)
    pre = jnp.dot(h_ref[...], up_ref[...], preferred_element_type=f32)
    grad = jnp.dot(g_ref[...], down_ref[...], preferred_element_type=f32)
    act, grad_pre = gelu_both(pre, grad)
    feed = lax.dot_general(act, down_ref[...], LAST, preferred_element_type=f32)
    grad_two = lax.dot_general(grad_pre, up_ref[...], LAST, preferred_element_type=f32)

    @pl.when(step == 0)
    def _():
        feed_s[...] = feed
        grad_s[...] = grad_two

    @pl.when(step > 0)
    def _():
        feed_s[...] += feed
        grad_s[...] += grad_two

    @pl.when(step == pl.num_programs(0) - 1)
    def _():
        feed_out[...] = feed_s[...].astype(bf16)
        grad_out[...] = grad_s[...].astype(bf16)


def own_ffn(h, g, up_weight, down_weight):
    width = h.shape[1]
    hidden = up_weight.shape[1]
    tile = 512
    return pl.pallas_call(
        own_kernel,
        grid=(hidden // tile,),
        in_specs=[NEAR, NEAR] + [pl.BlockSpec((width, tile), lambda i: (0, i))] * 2,
        out_specs=[NEAR] * 2,
        out_shape=[jax.ShapeDtypeStruct(h.shape, bf16)] * 2,
        scratch_shapes=[pltpu.VMEM(h.shape, f32)] * 2,
        cost_estimate=HINT,
        name="own_ffn",
    )(*near(h, g), up_weight, down_weight)


def norm_back_kernel(x_ref, mine_ref, other_ref, gain_ref, g_ref, o_ref, grad_out, low_out, sums_out, heads_out):
    x = x_ref[...]
    center = x - jnp.mean(x, axis=1, keepdims=True)
    scale = lax.rsqrt(jnp.mean(center * center, axis=1, keepdims=True) + 1e-05)
    normed = center * scale
    grad = mine_ref[...].astype(f32) + other_ref[...].astype(f32)
    sums_out[0:1, :] = jnp.sum(grad * normed, axis=0, keepdims=True)
    sums_out[1:2, :] = jnp.sum(grad, axis=0, keepdims=True)
    grad = grad * gain_ref[...]
    inner = jnp.mean(grad * normed, axis=1, keepdims=True)
    grad = scale * (grad - jnp.mean(grad, axis=1, keepdims=True) - normed * inner)
    grad = grad + g_ref[...].astype(f32)
    grad_out[...] = grad
    low = grad.astype(bf16)
    low_out[...] = low
    attended = jnp.dot(low, o_ref[...], preferred_element_type=f32)
    across = attended.T.astype(bf16)
    for head in range(heads_out.shape[0]):
        heads_out[head] = across[head * HEAD : (head + 1) * HEAD, :]


def norm_back(x, mine, other, gain, g, output_weight):
    rows, width = x.shape
    return pl.pallas_call(
        norm_back_kernel,
        in_specs=[NEAR] * 6,
        out_specs=[NEAR] * 4,
        out_shape=[
            jax.ShapeDtypeStruct((rows, width), f32),
            jax.ShapeDtypeStruct((rows, width), bf16),
            jax.ShapeDtypeStruct((2, width), f32),
            jax.ShapeDtypeStruct((output_weight.shape[1] // HEAD, HEAD, rows), bf16),
        ],
        compiler_params=room(16),
        cost_estimate=HINT,
        name="norm_back",
    )(*near(x, mine, other, gain.reshape(1, width), g, output_weight))


def prepare_kernel(ids_ref, len_ref, t_ref, n_ref, p_ref, s_s):
    step = pl.program_id(0)
    count, _, rows = t_ref.shape
    borders = borders_of(len_ref)
    blocks = [4 * step + 2 * i + (ids_ref[0] & 1) for i in range(2)]
    lo, hi = tiles_of(blocks[0] * rows, blocks[1] * rows + rows - 1, borders, count * rows)
    q = jnp.concatenate([t_ref[b, 0:HEAD, :] for b in blocks], axis=1)
    q = jnp.concatenate([q, jnp.zeros_like(q)], axis=0)
    places = lax.broadcasted_iota(jnp.int32, (1, rows), 1)
    row = scenes(jnp.concatenate([places + b * rows for b in blocks], axis=1), borders)

    def score(j, top):
        keys = pl.ds(pl.multiple_of(j * KT, KT), KT)
        s = jnp.dot(n_ref[keys, 0 : 2 * HEAD], q, preferred_element_type=f32)
        col = scenes(lax.broadcasted_iota(jnp.int32, (KT, 1), 0) + j * KT, borders)
        s = jnp.where(col == row, s, NEG)
        s_s[keys, :] = s
        return jnp.maximum(top, jnp.max(s, axis=0, keepdims=True))

    top = lax.fori_loop(lo, hi, score, jnp.full((1, QT), NEG, f32))

    def weigh(j, total):
        keys = pl.ds(pl.multiple_of(j * KT, KT), KT)
        p = jnp.exp(s_s[keys, :] - top)
        s_s[keys, :] = p
        return total + jnp.sum(p, axis=0, keepdims=True)

    total = lax.fori_loop(lo, hi, weigh, jnp.zeros((1, QT), f32))
    share = 1.0 / total

    def store(j, carry):
        keys = pl.ds(pl.multiple_of(j * KT, KT), KT)
        p_ref[0, keys, :] = (s_s[keys, :] * share).astype(bf16)
        return carry

    lax.fori_loop(lo, hi, store, 0)


def prepare(ids, scene_len, head_t, head_n):
    count, _, rows = head_t.shape
    total = count * rows
    tiles = total // 2 // QT
    return pl.pallas_call(
        prepare_kernel,
        grid_spec=pltpu.PrefetchScalarGridSpec(
            num_scalar_prefetch=2,
            grid=(tiles,),
            in_specs=[full(head_t.shape), full((total, 4 * HEAD))],
            out_specs=pl.BlockSpec((1, total, QT), lambda i, *_: (i, 0, 0)),
            scratch_shapes=[pltpu.VMEM((total, QT), f32)],
        ),
        out_shape=jax.ShapeDtypeStruct((tiles, total, QT), bf16),
        cost_estimate=HINT,
        name="prepare",
    )(ids, scene_len, head_t, head_n.reshape(total, 4 * HEAD))


def back_kernel(
    ids_ref, len_ref, p_ref, ga_ref, t_ref, n_ref, h_far,
    gq_out, mine_out, other_out, slice_mine, slice_other, dp_s, gkv_s, g_s, h_ref, sem,
):
    step = pl.program_id(0)
    part = ids_ref[0] & 1
    count, _, rows = t_ref.shape
    blocks = [4 * step + 2 * i + part for i in range(2)]
    lo, hi = tiles_of(blocks[0] * rows, blocks[1] * rows + rows - 1, borders_of(len_ref), count * rows)
    load = pltpu.make_async_copy(h_far, h_ref, sem)

    @pl.when(step == 0)
    def _():
        load.start()
        gkv_s[...] = jnp.zeros_like(gkv_s)
        g_s[...] = jnp.zeros_like(g_s)

    spans = [pl.ds(pl.multiple_of(b * rows, rows), rows) for b in blocks]
    ga_t = jnp.concatenate([ga_ref[0], ga_ref[1]], axis=1)
    ga_t = jnp.concatenate([ga_t, jnp.zeros_like(ga_t)], axis=0)
    ga = ga_t.T
    kq = jnp.concatenate([n_ref[span, 0 : 2 * HEAD] for span in spans], axis=0)
    q = jnp.where(lax.broadcasted_iota(jnp.int32, kq.shape, 1) >= HEAD, kq, jnp.zeros_like(kq))

    def first(j, delta):
        keys = pl.ds(pl.multiple_of(j * KT, KT), KT)
        p = p_ref[0, keys, :]
        dp = jnp.dot(n_ref[keys, 2 * HEAD :], ga_t, preferred_element_type=f32)
        dp_s[keys, :] = dp
        gkv_s[keys, :] += jnp.dot(p, ga, preferred_element_type=f32)
        return delta + jnp.sum(p.astype(f32) * dp, axis=0, keepdims=True)

    delta = lax.fori_loop(lo, hi, first, jnp.zeros((1, QT), f32))

    def second(j, gq):
        keys = pl.ds(pl.multiple_of(j * KT, KT), KT)
        ds = (p_ref[0, keys, :].astype(f32) * (dp_s[keys, :] - delta)).astype(bf16)
        gkv_s[keys, :] += jnp.dot(ds, q, preferred_element_type=f32)
        some = KT // rows
        k_t = jnp.concatenate([t_ref[j * some + i, HEAD : 2 * HEAD, :] for i in range(some)], axis=1)
        return gq + jnp.dot(k_t, ds, preferred_element_type=f32)

    gq = lax.fori_loop(lo, hi, second, jnp.zeros((HEAD, QT), f32))
    gq = (gq * HEAD ** (-0.5)).astype(bf16)
    for i in range(2):
        tile = gq[:, i * rows : (i + 1) * rows]
        gq_out[2 * step + i] = tile
        g_s[0:HEAD, spans[i]] = tile

    @pl.when(step == pl.num_programs(0) - 1)
    def _():
        for m in range(count // 2):
            for out, b in ((mine_out, 2 * m + part), (other_out, 2 * m + 1 - part)):
                tokens = pl.ds(pl.multiple_of(b * rows, rows), rows)
                both = gkv_s[tokens, :].T
                out[m] = both.astype(out.dtype)
                g_s[HEAD:, tokens] = both.astype(bf16)
        load.wait()
        slices = jnp.dot(g_s[...], h_ref[...], preferred_element_type=f32)
        wide = slice_mine.shape[1]
        left, right = slices[:, :wide], slices[:, wide:]
        slice_mine[...] = jnp.where(part == 0, left, right)
        slice_other[...] = jnp.where(part == 0, right, left).astype(bf16)


def back(ids, scene_len, p, ga, head_t, head_n, h1):
    count, three, rows = head_t.shape
    width = h1.shape[-1]
    total = count * rows
    half = count // 2
    kept = [
        ((half, HEAD, rows), bf16),
        ((half, 2 * HEAD, rows), f32),
        ((half, 2 * HEAD, rows), bf16),
        ((three, width // 2), f32),
        ((three, width // 2), bf16),
    ]
    return pl.pallas_call(
        back_kernel,
        grid_spec=pltpu.PrefetchScalarGridSpec(
            num_scalar_prefetch=2,
            grid=(p.shape[0],),
            in_specs=[
                pl.BlockSpec((1, total, QT), lambda i, *_: (i, 0, 0)),
                pl.BlockSpec((2, HEAD, rows), lambda i, *_: (i, 0, 0)),
                full(head_t.shape),
                full((total, 4 * HEAD)),
                FAR,
            ],
            out_specs=[NEAR] * 5,
            scratch_shapes=[
                pltpu.VMEM((total, QT), f32),
                pltpu.VMEM((total, 2 * HEAD), f32),
                pltpu.VMEM((three, total), bf16),
                pltpu.VMEM((total, width), bf16),
                pltpu.SemaphoreType.DMA,
            ],
        ),
        out_shape=[jax.ShapeDtypeStruct(shape, kind) for shape, kind in kept],
        cost_estimate=HINT,
        name="back",
    )(ids, scene_len, p, ga, head_t, head_n.reshape(total, 4 * HEAD), h1.reshape(total, width))


def share_kernel(ids_ref, low_ref, attended_ref, mine_out, other_out):
    part = ids_ref[0] & 1
    whole = lax.dot_general(low_ref[...], attended_ref[...], FIRST, preferred_element_type=f32)
    whole = whole.reshape(mine_out.shape[0], 2, mine_out.shape[1], mine_out.shape[2])
    mine_out[...] = jnp.where(part == 0, whole[:, 0], whole[:, 1])
    other_out[...] = jnp.where(part == 0, whole[:, 1], whole[:, 0]).astype(bf16)


def share_output(ids, low, attended, count):
    shape = (count // 2, low.shape[1] // count, attended.shape[1])
    return pl.pallas_call(
        share_kernel,
        in_specs=[SCALAR, NEAR, NEAR],
        out_specs=[NEAR] * 2,
        out_shape=[jax.ShapeDtypeStruct(shape, f32), jax.ShapeDtypeStruct(shape, bf16)],
        compiler_params=room(16),
        cost_estimate=HINT,
        name="share_output",
    )(ids, *near(low, attended))


def merge_kernel(gq_ref, kept_ref, given_ref, mine_ref, other_ref, out_ref):
    out_ref[:, 0:HEAD, :] = gq_ref[...]
    out_ref[:, HEAD : 3 * HEAD, :] = (kept_ref[...] + given_ref[...].astype(f32)).astype(bf16)
    lanes = out_ref.shape[2]
    slots = mine_ref.shape[1]
    for c in range(mine_ref.shape[2] // lanes):
        span = slice(c * lanes, (c + 1) * lanes)
        both = mine_ref[:, :, span] + other_ref[:, :, span].astype(f32)
        out_ref[:, 3 * HEAD + c * slots : 3 * HEAD + (c + 1) * slots, :] = both.astype(bf16)


def merge(gq, kept, given, mine, other):
    half, _, rows = gq.shape
    extra = mine.shape[1] * mine.shape[2] // rows
    return pl.pallas_call(
        merge_kernel,
        in_specs=[NEAR] * 5,
        out_specs=NEAR,
        out_shape=jax.ShapeDtypeStruct((half, 3 * HEAD + extra, rows), bf16),
        compiler_params=room(8),
        cost_estimate=HINT,
        name="merge",
    )(*near(gq, kept, given, mine, other))


def home_kernel(home_ref, q_ref, v_ref, k_ref, grad_out, slice_out):
    rows = home_ref.shape[2]
    grad = 0.0
    for i, weight in enumerate((q_ref, v_ref, k_ref)):
        across = home_ref[:, i * HEAD : (i + 1) * HEAD, :].reshape(-1, rows)
        grad = grad + lax.dot_general(across.T, weight[...], LAST, preferred_element_type=f32)
    grad_out[...] = grad.astype(bf16)
    slots = slice_out.shape[0]
    for c in range(slice_out.shape[1] // rows):
        at = 3 * HEAD + c * slots
        whole = jnp.sum(home_ref[:, at : at + slots, :].astype(f32), axis=0)
        slice_out[:, c * rows : (c + 1) * rows] = whole.astype(bf16)


def go_home(home, weights, slots):
    rows = home.shape[2]
    width, columns = weights[0].shape
    return pl.pallas_call(
        home_kernel,
        in_specs=[NEAR] * 4,
        out_specs=[NEAR] * 2,
        out_shape=[
            jax.ShapeDtypeStruct((rows, width), bf16),
            jax.ShapeDtypeStruct((slots, columns), bf16),
        ],
        cost_estimate=HINT,
        name="go_home",
    )(home, *weights)


def input_back_kernel(x_ref, mine_ref, other_ref, gain_ref, grad_ref, sums_ref, grad_out, sums_out):
    x = x_ref[...].astype(f32)
    center = x - jnp.mean(x, axis=1, keepdims=True)
    scale = lax.rsqrt(jnp.mean(center * center, axis=1, keepdims=True) + 1e-05)
    normed = center * scale
    grad = mine_ref[...].astype(f32) + other_ref[...].astype(f32)
    sums = [jnp.sum(grad * normed, axis=0, keepdims=True), jnp.sum(grad, axis=0, keepdims=True), sums_ref[...]]
    sums = jnp.concatenate(sums, axis=0)
    for b in range(sums_out.shape[0]):
        sums_out[b] = sums
    grad = grad * gain_ref[...]
    inner = jnp.mean(grad * normed, axis=1, keepdims=True)
    grad_out[...] = grad_ref[...] + scale * (grad - jnp.mean(grad, axis=1, keepdims=True) - normed * inner)


def input_back(x, mine, other, gain, grad_middle, sums, count):
    rows, width = x.shape
    return pl.pallas_call(
        input_back_kernel,
        in_specs=[NEAR] * 6,
        out_specs=[NEAR] * 2,
        out_shape=[
            jax.ShapeDtypeStruct((rows, width), f32),
            jax.ShapeDtypeStruct((count, 4, width), f32),
        ],
        compiler_params=room(16),
        cost_estimate=HINT,
        name="input_back",
    )(x, mine, other, gain.reshape(1, width), grad_middle, sums)


def through_kernel(g_ref, down_ref, out_ref):
    out_ref[...] = jnp.dot(g_ref[...], down_ref[...], preferred_element_type=f32).astype(bf16)


def through(g, weight):
    total, width = g.shape
    hidden = weight.shape[1]
    tile = 2 * FT
    return pl.pallas_call(
        through_kernel,
        grid=(hidden // tile,),
        in_specs=[
            pl.BlockSpec((total, width), lambda i: (0, 0), pipeline_mode=pl.Buffered(1)),
            pl.BlockSpec((width, tile), lambda i: (0, i)),
        ],
        out_specs=pl.BlockSpec((total, tile), lambda i: (0, i)),
        out_shape=jax.ShapeDtypeStruct((total, hidden), bf16),
        cost_estimate=pl.CostEstimate(
            flops=2 * total * width * hidden, bytes_accessed=8 * total * width, transcendentals=0
        ),
        name="through",
    )(g, weight)


def ffn_kernel(h_ref, g_ref, grad_ref, up_ref, *outs):
    up_out, down_out = outs[-2:]
    steps = h_ref.shape[0] // TT

    def product(j):
        return jnp.dot(h_ref[j * TT : (j + 1) * TT, :], up_ref[...], preferred_element_type=f32)

    pre = product(0)
    for j in range(steps):
        later = product(j + 1) if j + 1 < steps else None
        span = slice(j * TT, (j + 1) * TT)
        act, grad_pre = gelu_both(pre, grad_ref[span, :].astype(f32))
        up = lax.dot_general(h_ref[span, :], grad_pre, FIRST, preferred_element_type=f32)
        down = lax.dot_general(g_ref[span, :], act, FIRST, preferred_element_type=f32)
        if j == 0:
            up_out[...] = up
            down_out[...] = down
        else:
            up_out[...] += up
            down_out[...] += down
        pre = later


def ffn_grads(h, g, grad, up_weight, tiles, held):
    total, width = h.shape
    hidden = up_weight.shape[1]
    first, last = tiles
    tokens = pl.BlockSpec((total, width), lambda i: (0, 0), pipeline_mode=pl.Buffered(1))
    units = pl.BlockSpec((width, FT), lambda i: (0, first + i))
    return pl.pallas_call(
        ffn_kernel,
        grid=(last - first,),
        in_specs=[tokens, tokens, pl.BlockSpec((total, FT), lambda i: (0, first + i)), units] + [FAR] * len(held),
        out_specs=[units] * 2,
        out_shape=[jax.ShapeDtypeStruct((width, hidden), f32)] * 2,
        input_output_aliases={4: 0, 5: 1} if held else {},
        cost_estimate=pl.CostEstimate(
            flops=6 * total * width * FT * (last - first), bytes_accessed=4 * total * width, transcendentals=0
        ),
        name="ffn_grads",
    )(h, g, grad, up_weight, *held)


def finish_heads_kernel(ids_ref, *refs):
    heads, outs = refs[:4], refs[4:]
    row, part = (ids_ref[0] >> 1) & 1, ids_ref[0] & 1
    wide = heads[0].shape[2]
    for k, x in ((0, part), (1, 1 - part)):
        rows = pl.ds(pl.multiple_of(x * wide, wide), wide)
        for i in range(3):
            this = heads[k][0, i * HEAD : (i + 1) * HEAD, :]
            that = heads[k + 2][0, i * HEAD : (i + 1) * HEAD, :]
            pair = [jnp.where(row == 0, this, that), jnp.where(row == 0, that, this)]
            outs[i][rows, :] = jnp.concatenate(pair, axis=0).T.astype(f32)


def finish_rows_kernel(ids_ref, *refs):
    pieces, out_ref = refs[:4], refs[4]
    slots = pieces[0].shape[1]
    for k in range(4):
        for s in range(4):
            at = pl.multiple_of((((ids_ref[0] - 4 * s) & 15) ^ k) * slots, slots)
            out_ref[pl.ds(at, slots), :] = pieces[k][s].astype(f32)


def finish_rows(ids, pieces, width, columns):
    return pl.pallas_call(
        finish_rows_kernel,
        in_specs=[SCALAR] + [NEAR] * 4,
        out_specs=NEAR,
        out_shape=jax.ShapeDtypeStruct((width, columns), f32),
        compiler_params=room(16),
        cost_estimate=HINT,
        name="finish_rows",
    )(ids, *near(*pieces))


def finish_heads(ids, pieces, width, columns):
    block = pl.BlockSpec((width, columns // 4), lambda s, ids: (0, ((ids[0] - 4 * s) & 15) >> 2))
    return pl.pallas_call(
        finish_heads_kernel,
        grid_spec=pltpu.PrefetchScalarGridSpec(
            num_scalar_prefetch=1,
            grid=(4,),
            in_specs=[pl.BlockSpec((1,) + p.shape[1:], lambda s, ids: (s, 0, 0)) for p in pieces],
            out_specs=[block] * 3,
        ),
        out_shape=[jax.ShapeDtypeStruct((width, columns), f32)] * 3,
        cost_estimate=HINT,
        name="finish_heads",
    )(ids, *pieces)


def shuffle(block, target):
    return lax.ppermute(block, "blk", [(i, target(i)) for i in range(16)])


def over_core(block):
    return lax.ppermute(block, "tp", [(0, 1), (1, 0)])


def send_column(unit):
    return (unit,) + tuple(shuffle(unit, lambda i, s=s: (i + 4 * s) % 16) for s in (1, 2, 3))


def stack_column(parts, *first):
    return jnp.stack(lax.optimization_barrier(parts + first)[:4])


def gather_plane(column):
    return (column,) + tuple(shuffle(column, lambda i, k=k: i ^ k) for k in (1, 2, 3))


def after(value, *first):
    return lax.optimization_barrier((value,) + first)[0]


def fast_body(
    tokens,
    first_gain,
    first_bias,
    second_gain,
    second_bias,
    query_weight,
    key_weight,
    value_weight,
    output_weight,
    up_weight,
    down_weight,
    cotangent,
    scene_len,
):
    count = lax.axis_size("blk")
    place = lax.axis_index("blk")
    side = lax.axis_index("tp")
    rows, width = tokens.shape
    columns = query_weight.shape[1]
    heads_here = columns // HEAD
    share = count // heads_here
    scale = HEAD ** (-0.5)
    ids = jnp.stack([place, side])
    half_at = side.astype(jnp.uint32) * jnp.uint32(rows // 2)
    head_at = (place.astype(jnp.uint32) >> 1) * jnp.uint32(HEAD)
    alike = [list(range(r, count, share)) for r in range(share)]

    def half_of(block):
        return lax.dynamic_slice(block, (half_at, jnp.uint32(0)), (rows // 2, width))

    def head_of(weight):
        return lax.dynamic_slice(weight, (jnp.uint32(0), head_at), (width, HEAD))

    g_all = lax.all_gather(half_of(cotangent), ("blk", "tp"), axis=0, tiled=True)
    column = jnp.stack(send_column(half_of(tokens)))

    head_query = head_of(query_weight) * jnp.asarray(scale, bf16)
    head_key, head_value = head_of(key_weight), head_of(value_weight)
    head_t = jnp.concatenate([head_query, head_key, head_value], axis=1).T
    head_n = jnp.concatenate([head_key, head_query, head_value, jnp.zeros_like(head_value)], axis=1)
    params = (first_gain.reshape(1, -1), first_bias.reshape(1, -1), key_weight, value_weight, head_t, head_n)

    across_x = shuffle(column, lambda i: i ^ 1)
    across_y = shuffle(column, lambda i: i ^ 2)
    made = project_blocks(0, ids, column, over_core(column), params, count, ())
    across_y = after(across_y, made[0])
    diagonal = shuffle(across_y, lambda i: i ^ 1)
    for flip, piece in ((1, after(across_x, across_y)), (2, across_y), (3, diagonal)):
        piece = after(piece, made[0]) if piece is diagonal else piece
        made = project_blocks(flip, ids, piece, over_core(piece), params, count, made)
    h1_all, keys, values, head_t, head_n = made

    attended, branch = attend(
        ids, scene_len, h1_all, keys.reshape(-1, columns), values.reshape(-1, columns), query_weight, output_weight
    )
    inputs = tokens.astype(f32)
    middle = inputs + (branch.astype(f32) + over_core(branch).astype(f32))
    h2 = layer_norm(middle, second_gain, second_bias).astype(bf16)
    h2_all = lax.all_gather(half_of(h2), ("blk", "tp"), axis=0, tiled=True)

    feed, grad_two = own_ffn(h2, cotangent, up_weight, down_weight)
    grad_middle, grad_middle_low, second_sums, to_heads = norm_back(
        middle, grad_two, over_core(grad_two), second_gain, cotangent, output_weight
    )
    ga = lax.all_to_all(to_heads, "blk", 0, 0, tiled=True, axis_index_groups=alike)
    p = prepare(ids, scene_len, after(head_t, to_heads, g_all), head_n)
    grad_q, kept, given, slice_kept, slice_given = back(ids, scene_len, p, ga, head_t, head_n, h1_all)

    output_kept, output_given = share_output(ids, after(grad_middle_low, slice_given), attended, count)
    output_other = shuffle(output_given, lambda i: i ^ 1)
    head_slice = (slice_kept + shuffle(slice_given, lambda i: i ^ 1).astype(f32)).astype(bf16)
    parts = send_column(head_slice)

    given = after(given, head_slice)
    given = shuffle(given, lambda i: i ^ 1)
    grad_all = through(after(g_all, head_slice), down_weight)
    column = stack_column(parts, grad_all)
    parcel = merge(after(grad_q, column), kept, given, output_kept, output_other)
    home = lax.all_to_all(parcel, "blk", 0, 0, tiled=True, axis_index_groups=alike)
    heads = gather_plane(column)

    feed = after(feed, parcel)
    layer_out = (middle + (feed.astype(f32) + over_core(feed).astype(f32))).astype(bf16)
    held = ffn_grads(after(h2_all, column), g_all, grad_all, up_weight, (0, 4), ())

    home = after(home, held[0])
    grad_one, output_slice = go_home(home, (query_weight, value_weight, key_weight), width // count)
    input_grad, norm_part = input_back(
        tokens, grad_one, over_core(grad_one), first_gain, grad_middle, second_sums, count
    )
    norm_parts = lax.all_to_all(norm_part, "blk", 0, 0, tiled=True)

    parts = send_column(output_slice)
    up_grad, down_grad = ffn_grads(
        after(h2_all, norm_part, *heads), g_all, grad_all, up_weight, (4, 8), held
    )
    rest = gather_plane(stack_column(parts, up_grad, norm_parts))
    norm_sums = jnp.sum(after(norm_parts, up_grad), axis=0)
    heads = (after(heads[0], up_grad),) + heads[1:]
    query_grad, value_grad, key_grad = finish_heads(ids, heads, width, columns)
    output_grad = finish_rows(ids, rest, width, columns)
    return (
        layer_out,
        input_grad,
        norm_sums[0],
        norm_sums[1],
        norm_sums[2],
        norm_sums[3],
        query_grad,
        key_grad,
        value_grad,
        output_grad,
        up_grad,
        down_grad,
    )


def solution(mesh):
    body = fast_body if mesh.shape["blk"] == 16 else ring_body
    return jax.shard_map(
        body,
        mesh=mesh,
        in_specs=(
            P("blk", None),
            P(),
            P(),
            P(),
            P(),
            P(None, "tp"),
            P(None, "tp"),
            P(None, "tp"),
            P(None, "tp"),
            P(None, "tp"),
            P(None, "tp"),
            P("blk", None),
            P(),
        ),
        out_specs=(
            P("blk", None),
            P("blk", None),
            P(),
            P(),
            P(),
            P(),
            P(None, "tp"),
            P(None, "tp"),
            P(None, "tp"),
            P(None, "tp"),
            P(None, "tp"),
            P(None, "tp"),
        ),
        check_vma=False,
    )
```

```python
import jax
import jax.numpy as jnp
from jax import lax
from jax.experimental import pallas as pl
from jax.experimental.pallas import tpu as pltpu
from jax.sharding import PartitionSpec as P

HEAD = 64
NEG = -1e30
f32 = jnp.float32
bf16 = jnp.bfloat16
LAST = (((1,), (1,)), ((), ()))
FIRST = (((0,), (0,)), ((), ()))


def from_behind(block, axis, distance):
    devices = range(lax.axis_size(axis))
    route = [((i - distance) % len(devices), i) for i in devices]
    return lax.ppermute(block, axis, route)


def layer_norm(values, gain, bias):
    center = values - jnp.mean(values, axis=-1, keepdims=True)
    spread = jnp.mean(center * center, axis=-1, keepdims=True)
    return center * lax.rsqrt(spread + 1e-05) * gain + bias


def move_grads(grad_keys, grad_values, offset):
    return (
        from_behind(grad_keys.astype(jnp.bfloat16), "blk", offset).astype(grad_keys.dtype),
        from_behind(grad_values.astype(jnp.bfloat16), "blk", offset).astype(grad_values.dtype),
    )


def ring_body(
    tokens,
    first_gain,
    first_bias,
    second_gain,
    second_bias,
    query_weight,
    key_weight,
    value_weight,
    output_weight,
    up_weight,
    down_weight,
    cotangent,
    scene_len,
):
    count = lax.axis_size("blk")
    place = lax.axis_index("blk")
    rows = tokens.shape[0]
    heads_here = query_weight.shape[1] // HEAD
    scale = HEAD ** (-0.5)
    ends = jnp.cumsum(scene_len)
    contract_last = (((1,), (1,)), ((), ()))
    contract_first = (((0,), (0,)), ((), ()))

    def scene_of(source):
        places = source * rows + jnp.arange(rows, dtype=jnp.int32)
        return jnp.sum((places[:, None] >= ends[None, :]).astype(jnp.int32), axis=1)

    mine = scene_of(place)

    def shares(source):
        other = scene_of(source)
        return jnp.maximum(mine[0], other[0]) <= jnp.minimum(mine[-1], other[-1])

    directions = (1,)
    steps = count - 1

    def source_of(way, turn):
        raw_source = place - way * turn
        return (raw_source % count, jnp.array(True))

    inputs = tokens.astype(f32)
    normed_one = layer_norm(inputs, first_gain, first_bias).astype(bf16)

    def project(weight):
        return jnp.dot(normed_one, weight, preferred_element_type=f32).astype(bf16)

    query = project(query_weight).reshape(rows, heads_here, HEAD)
    keys = project(key_weight).reshape(rows, heads_here, HEAD)
    values = project(value_weight).reshape(rows, heads_here, HEAD)

    def scores_of(key_block, source):
        mask = mine[:, None] == scene_of(source)[None, :]
        scores = jnp.einsum("qhd,khd->hqk", query, key_block, preferred_element_type=f32) * scale
        return (jnp.where(mask[None], scores, -1e30), mask)

    def absorb(state, key_block, value_block, source):
        top, total, summed = state
        scores, mask = scores_of(key_block, source)
        new_top = jnp.maximum(top, jnp.max(scores, axis=2))
        factor = jnp.exp(top - new_top)
        weights = jnp.where(mask[None], jnp.exp(scores - new_top[:, :, None]), 0.0)
        total = total * factor + jnp.sum(weights, axis=2)
        summed = summed * factor.T[:, :, None] + jnp.einsum(
            "hqk,khd->qhd", weights.astype(bf16), value_block, preferred_element_type=f32
        )
        return (new_top, total, summed)

    start = (
        jnp.full((heads_here, rows), -1e30, f32),
        jnp.zeros((heads_here, rows), f32),
        jnp.zeros((rows, heads_here, HEAD), f32),
    )
    state = absorb(start, keys, values, place)
    way = directions[0]

    def turn_forward(turn, carry):
        current, key_block, value_block = carry
        key_block, value_block = from_behind((key_block, value_block), "blk", way)
        source, inside = source_of(way, turn)
        current = lax.cond(
            inside & shares(source),
            lambda held: absorb(held, key_block, value_block, source),
            lambda held: held,
            current,
        )
        return (current, key_block, value_block)

    state, _, _ = lax.fori_loop(1, steps + 1, turn_forward, (state, keys, values))
    top, total, summed = state
    attended = summed / total.T[:, :, None]
    log_total = top + jnp.log(total)
    attended_low = attended.reshape(rows, -1).astype(bf16)
    branch = lax.dot_general(attended_low, output_weight, contract_last, preferred_element_type=f32)
    branch = lax.psum(branch.astype(jnp.bfloat16), "tp").astype(jnp.float32)
    middle = inputs + branch
    normed_two = layer_norm(middle, second_gain, second_bias).astype(bf16)
    before = jnp.dot(normed_two, up_weight, preferred_element_type=f32)
    active = jax.nn.gelu(before, approximate=False).astype(bf16)
    feed = lax.dot_general(active, down_weight, contract_last, preferred_element_type=f32)
    feed = lax.psum(feed.astype(jnp.bfloat16), "tp").astype(jnp.float32)
    layer_out = (middle + feed).astype(bf16)
    grad_out = cotangent.astype(f32)
    down_grad = lax.dot_general(cotangent, active, contract_first, preferred_element_type=f32)
    grad_active = jnp.dot(cotangent, down_weight, preferred_element_type=f32)
    _, gelu_pull = jax.vjp(lambda arg: jax.nn.gelu(arg, approximate=False), before)
    grad_before = gelu_pull(grad_active)[0].astype(bf16)
    up_grad = lax.dot_general(normed_two, grad_before, contract_first, preferred_element_type=f32)
    grad_two = lax.dot_general(grad_before, up_weight, contract_last, preferred_element_type=f32)
    grad_two = lax.psum(grad_two.astype(jnp.bfloat16), "tp").astype(jnp.float32)
    _, second_pull = jax.vjp(layer_norm, middle, second_gain, second_bias)
    grad_middle_norm, second_gain_grad, second_bias_grad = second_pull(grad_two)
    grad_middle = grad_out + grad_middle_norm
    grad_middle_low = grad_middle.astype(bf16)
    output_grad = lax.dot_general(
        grad_middle_low, attended_low, contract_first, preferred_element_type=f32
    )
    grad_attended = jnp.dot(grad_middle_low, output_weight, preferred_element_type=f32).astype(bf16)
    grad_attended = grad_attended.reshape(rows, heads_here, HEAD)
    delta = jnp.sum(grad_attended * attended, axis=2).T

    def backtrack(grads, key_block, value_block, source):
        grad_query, grad_keys, grad_values = grads
        scores, mask = scores_of(key_block, source)
        probs = jnp.where(mask[None], jnp.exp(scores - log_total[:, :, None]), 0.0)
        grad_values = grad_values + jnp.einsum(
            "hqk,qhd->khd", probs.astype(bf16), grad_attended, preferred_element_type=f32
        )
        grad_probs = jnp.einsum(
            "qhd,khd->hqk", grad_attended, value_block, preferred_element_type=f32
        )
        grad_scores = (probs * (grad_probs - delta[:, :, None]) * scale).astype(bf16)
        grad_query = grad_query + jnp.einsum(
            "hqk,khd->qhd", grad_scores, key_block, preferred_element_type=f32
        )
        grad_keys = grad_keys + jnp.einsum(
            "hqk,qhd->khd", grad_scores, query, preferred_element_type=f32
        )
        return (grad_query, grad_keys, grad_values)

    empty = jnp.zeros((rows, heads_here, HEAD), f32)
    grad_query, home_keys, home_values = backtrack((empty, empty, empty), keys, values, place)
    way = directions[0]

    def turn_backward(turn, carry):
        grad_q, key_block, value_block, grad_k, grad_v = carry
        key_block, value_block = from_behind((key_block, value_block), "blk", way)
        grad_k, grad_v = move_grads(grad_k, grad_v, way)
        source, inside = source_of(way, turn)
        grad_q, grad_k, grad_v = lax.cond(
            inside & shares(source),
            lambda held: backtrack(held, key_block, value_block, source),
            lambda held: held,
            (grad_q, grad_k, grad_v),
        )
        return (grad_q, key_block, value_block, grad_k, grad_v)

    grad_query, _, _, moved_keys, moved_values = lax.fori_loop(
        1, steps + 1, turn_backward, (grad_query, keys, values, empty, empty)
    )
    moved_keys, moved_values = move_grads(moved_keys, moved_values, -way * steps)
    home_keys = home_keys + moved_keys
    home_values = home_values + moved_values
    grad_query = grad_query.reshape(rows, -1).astype(bf16)
    grad_keys = home_keys.reshape(rows, -1).astype(bf16)
    grad_values = home_values.reshape(rows, -1).astype(bf16)
    query_grad = lax.dot_general(normed_one, grad_query, contract_first, preferred_element_type=f32)
    key_grad = lax.dot_general(normed_one, grad_keys, contract_first, preferred_element_type=f32)
    value_grad = lax.dot_general(
        normed_one, grad_values, contract_first, preferred_element_type=f32
    )
    grad_one = lax.dot_general(grad_query, query_weight, contract_last, preferred_element_type=f32)
    grad_one = grad_one + lax.dot_general(
        grad_keys, key_weight, contract_last, preferred_element_type=f32
    )
    grad_one = grad_one + lax.dot_general(
        grad_values, value_weight, contract_last, preferred_element_type=f32
    )
    grad_one = lax.psum(grad_one.astype(jnp.bfloat16), "tp").astype(jnp.float32)
    _, first_pull = jax.vjp(layer_norm, inputs, first_gain, first_bias)
    grad_input_norm, first_gain_grad, first_bias_grad = first_pull(grad_one)
    input_grad = grad_middle + grad_input_norm
    norm_grads = jnp.stack(
        [first_gain_grad, first_bias_grad, second_gain_grad, second_bias_grad], axis=1
    )
    summed_parts = (
        lax.psum_scatter(query_grad, "blk", scatter_dimension=0, tiled=True),
        lax.psum_scatter(key_grad, "blk", scatter_dimension=0, tiled=True),
        lax.psum_scatter(value_grad, "blk", scatter_dimension=0, tiled=True),
        lax.psum_scatter(output_grad, "blk", scatter_dimension=0, tiled=True),
        lax.psum_scatter(up_grad, "blk", scatter_dimension=0, tiled=True),
        lax.psum_scatter(down_grad, "blk", scatter_dimension=0, tiled=True),
        lax.psum_scatter(norm_grads, "blk", scatter_dimension=0, tiled=True),
    )
    totals = (
        lax.all_gather(summed_parts[0].astype(jnp.bfloat16), "blk", axis=0, tiled=True).astype(
            jnp.float32
        ),
        lax.all_gather(summed_parts[1].astype(jnp.bfloat16), "blk", axis=0, tiled=True).astype(
            jnp.float32
        ),
        lax.all_gather(summed_parts[2].astype(jnp.bfloat16), "blk", axis=0, tiled=True).astype(
            jnp.float32
        ),
        lax.all_gather(summed_parts[3].astype(jnp.bfloat16), "blk", axis=0, tiled=True).astype(
            jnp.float32
        ),
        lax.all_gather(summed_parts[4].astype(jnp.bfloat16), "blk", axis=0, tiled=True).astype(
            jnp.float32
        ),
        lax.all_gather(summed_parts[5].astype(jnp.bfloat16), "blk", axis=0, tiled=True).astype(
            jnp.float32
        ),
        lax.all_gather(summed_parts[6].astype(jnp.bfloat16), "blk", axis=0, tiled=True).astype(
            jnp.float32
        ),
    )
    return (
        layer_out,
        input_grad,
        totals[6][:, 0],
        totals[6][:, 1],
        totals[6][:, 2],
        totals[6][:, 3],
        totals[0],
        totals[1],
        totals[2],
        totals[3],
        totals[4],
        totals[5],
    )


HINT = pl.CostEstimate(flops=1, bytes_accessed=1, transcendentals=1)
NEAR = pl.BlockSpec(memory_space=pltpu.VMEM)
FAR = pl.BlockSpec(memory_space=pltpu.HBM)
SCALAR = pl.BlockSpec(memory_space=pltpu.SMEM)
QT = 256
KT = 512
FT = 256
TT = 1024


def near(*arrays):
    return [pltpu.with_memory_space_constraint(array, pltpu.VMEM) for array in arrays]


def room(mib):
    return pltpu.CompilerParams(vmem_limit_bytes=mib << 20)


def full(shape):
    return pl.BlockSpec(shape, lambda *_: (0,) * len(shape))


def borders_of(len_ref):
    borders = [len_ref[0]]
    for s in range(1, len_ref.shape[0] - 1):
        borders.append(borders[-1] + len_ref[s])
    return borders


def scenes(positions, borders):
    scene = jnp.zeros_like(positions)
    for border in borders:
        scene += (positions >= border).astype(jnp.int32)
    return scene


def tiles_of(first, last, borders, total):
    low, high = 0, total
    for border in borders:
        low = jnp.where(border <= first, border, low)
    for border in reversed(borders):
        high = jnp.where(border > last, border, high)
    return lax.div(low, KT), lax.div(high + KT - 1, KT)


def project_kernel(flip, ids_ref, mine_ref, other_ref, gain_ref, bias_ref, k_ref, v_ref, t_ref, n_ref, *rest):
    h_out, k_out, v_out, t_out, n_out, h_s = rest[-6:]
    n, half, width = mine_ref.shape
    rows = 2 * half
    first = ids_ref[1] == 0

    def norm(b, carry):
        mine, other = mine_ref[b], other_ref[b]
        block = jnp.concatenate([jnp.where(first, mine, other), jnp.where(first, other, mine)], axis=0)
        h_s[b] = layer_norm(block.astype(f32), gain_ref[...], bias_ref[...]).astype(bf16)
        return carry

    lax.fori_loop(0, n, norm, 0)
    h = h_s[...].reshape(n * rows, width)
    keys = jnp.dot(h, k_ref[...], preferred_element_type=f32).astype(bf16)
    values = jnp.dot(h, v_ref[...], preferred_element_type=f32).astype(bf16)
    across = lax.dot_general(t_ref[...], h, LAST, preferred_element_type=f32).astype(bf16)
    down = jnp.dot(h, n_ref[...], preferred_element_type=f32).astype(bf16)
    for s in range(n):
        at = ((ids_ref[0] - 4 * s) & 15) ^ flip
        tokens = slice(s * rows, (s + 1) * rows)
        h_out[at] = h[tokens]
        k_out[at] = keys[tokens]
        v_out[at] = values[tokens]
        t_out[at] = across[:, tokens]
        n_out[at] = down[tokens]


def project_blocks(flip, ids, mine, other, params, count, held):
    half, width = mine.shape[1:]
    _, _, key_weight, value_weight, head_t, head_n = params
    shapes = [
        (2 * half, width),
        (2 * half, key_weight.shape[1]),
        (2 * half, value_weight.shape[1]),
        (head_t.shape[0], 2 * half),
        (2 * half, head_n.shape[1]),
    ]
    return pl.pallas_call(
        lambda *refs: project_kernel(flip, *refs),
        in_specs=[SCALAR] + [NEAR] * (8 + len(held)),
        out_specs=[NEAR] * 5,
        out_shape=[pltpu.VMEM((count,) + shape, bf16) for shape in shapes],
        scratch_shapes=[pltpu.VMEM((mine.shape[0], 2 * half, width), bf16)],
        input_output_aliases={9 + i: i for i in range(5)} if held else {},
        compiler_params=room(16),
        cost_estimate=HINT,
        name="project_blocks",
    )(ids, *near(mine, other, *params, *held))


def attend_kernel(ids_ref, len_ref, h_ref, k_ref, v_ref, q_ref, o_ref, out_ref, branch_ref, query_s):
    rows, width = out_ref.shape
    total = k_ref.shape[0]
    pair = 2 * HEAD
    borders = borders_of(len_ref)
    mine = scenes(lax.broadcasted_iota(jnp.int32, (rows, 1), 0) + ids_ref[0] * rows, borders)
    mask = mine == scenes(lax.broadcasted_iota(jnp.int32, (1, total), 1), borders)
    query = jnp.dot(h_ref[ids_ref[0]], q_ref[...], preferred_element_type=f32).astype(bf16)
    query = query * jnp.asarray(HEAD ** (-0.5), bf16)
    lane = lax.broadcasted_iota(jnp.int32, (rows, pair), 1) // HEAD
    query_s[...] = query

    def attend_pair(g, carry):
        lanes = pl.ds(pl.multiple_of(g * pair, pair), pair)
        keys, values, queries = k_ref[:, lanes], v_ref[:, lanes], query_s[:, lanes]
        parts = []
        for head in range(2):
            q = jnp.where(lane == head, queries, jnp.zeros_like(queries))
            s = lax.dot_general(q, keys, LAST, preferred_element_type=f32)
            s = jnp.where(mask, s, NEG)
            p = jnp.exp(s - jnp.max(s, axis=1, keepdims=True))
            weight = jnp.sum(p, axis=1, keepdims=True)
            parts.append(jnp.dot(p.astype(bf16), values, preferred_element_type=f32) / weight)
        out_ref[:, lanes] = jnp.where(lane == 0, parts[0], parts[1]).astype(bf16)
        return carry

    lax.fori_loop(0, width // pair, attend_pair, 0)
    branch = lax.dot_general(out_ref[...], o_ref[...], LAST, preferred_element_type=f32)
    branch_ref[...] = branch.astype(bf16)


def attend(ids, scene_len, h, k, v, query_weight, output_weight):
    rows = h.shape[1]
    return pl.pallas_call(
        attend_kernel,
        in_specs=[SCALAR] * 2 + [NEAR] * 5,
        out_specs=[NEAR] * 2,
        out_shape=[
            jax.ShapeDtypeStruct((rows, query_weight.shape[1]), bf16),
            jax.ShapeDtypeStruct((rows, output_weight.shape[0]), bf16),
        ],
        scratch_shapes=[pltpu.VMEM((rows, query_weight.shape[1]), bf16)],
        compiler_params=room(16),
        cost_estimate=HINT,
        name="attend",
    )(ids, scene_len, *near(h, k, v, query_weight, output_weight))


def gelu_both(pre, grad):
    half = 0.5 * (1.0 + lax.erf(pre * 0.7071067811865476))
    slope = half + pre * (jnp.exp(-0.5 * pre * pre) * 0.3989422804014327)
    return (pre * half).astype(bf16), (grad * slope).astype(bf16)


def own_kernel(h_ref, g_ref, up_ref, down_ref, feed_out, grad_out, feed_s, grad_s):
    step = pl.program_id(0)
    pre = jnp.dot(h_ref[...], up_ref[...], preferred_element_type=f32)
    grad = jnp.dot(g_ref[...], down_ref[...], preferred_element_type=f32)
    act, grad_pre = gelu_both(pre, grad)
    feed = lax.dot_general(act, down_ref[...], LAST, preferred_element_type=f32)
    grad_two = lax.dot_general(grad_pre, up_ref[...], LAST, preferred_element_type=f32)

    @pl.when(step == 0)
    def _():
        feed_s[...] = feed
        grad_s[...] = grad_two

    @pl.when(step > 0)
    def _():
        feed_s[...] += feed
        grad_s[...] += grad_two

    @pl.when(step == pl.num_programs(0) - 1)
    def _():
        feed_out[...] = feed_s[...].astype(bf16)
        grad_out[...] = grad_s[...].astype(bf16)


def own_ffn(h, g, up_weight, down_weight):
    width = h.shape[1]
    hidden = up_weight.shape[1]
    tile = 512
    return pl.pallas_call(
        own_kernel,
        grid=(hidden // tile,),
        in_specs=[NEAR, NEAR] + [pl.BlockSpec((width, tile), lambda i: (0, i))] * 2,
        out_specs=[NEAR] * 2,
        out_shape=[jax.ShapeDtypeStruct(h.shape, bf16)] * 2,
        scratch_shapes=[pltpu.VMEM(h.shape, f32)] * 2,
        cost_estimate=HINT,
        name="own_ffn",
    )(*near(h, g), up_weight, down_weight)


def norm_back_kernel(x_ref, mine_ref, other_ref, gain_ref, g_ref, o_ref, grad_out, low_out, sums_out, heads_out):
    x = x_ref[...]
    center = x - jnp.mean(x, axis=1, keepdims=True)
    scale = lax.rsqrt(jnp.mean(center * center, axis=1, keepdims=True) + 1e-05)
    normed = center * scale
    grad = mine_ref[...].astype(f32) + other_ref[...].astype(f32)
    sums_out[0:1, :] = jnp.sum(grad * normed, axis=0, keepdims=True)
    sums_out[1:2, :] = jnp.sum(grad, axis=0, keepdims=True)
    grad = grad * gain_ref[...]
    inner = jnp.mean(grad * normed, axis=1, keepdims=True)
    grad = scale * (grad - jnp.mean(grad, axis=1, keepdims=True) - normed * inner)
    grad = grad + g_ref[...].astype(f32)
    grad_out[...] = grad
    low = grad.astype(bf16)
    low_out[...] = low
    attended = jnp.dot(low, o_ref[...], preferred_element_type=f32)
    across = attended.T.astype(bf16)
    for head in range(heads_out.shape[0]):
        heads_out[head] = across[head * HEAD : (head + 1) * HEAD, :]


def norm_back(x, mine, other, gain, g, output_weight):
    rows, width = x.shape
    return pl.pallas_call(
        norm_back_kernel,
        in_specs=[NEAR] * 6,
        out_specs=[NEAR] * 4,
        out_shape=[
            jax.ShapeDtypeStruct((rows, width), f32),
            jax.ShapeDtypeStruct((rows, width), bf16),
            jax.ShapeDtypeStruct((2, width), f32),
            jax.ShapeDtypeStruct((output_weight.shape[1] // HEAD, HEAD, rows), bf16),
        ],
        compiler_params=room(16),
        cost_estimate=HINT,
        name="norm_back",
    )(*near(x, mine, other, gain.reshape(1, width), g, output_weight))


def prepare_kernel(ids_ref, len_ref, t_ref, n_ref, p_ref, s_s):
    step = pl.program_id(0)
    count, _, rows = t_ref.shape
    borders = borders_of(len_ref)
    blocks = [4 * step + 2 * i + (ids_ref[0] & 1) for i in range(2)]
    lo, hi = tiles_of(blocks[0] * rows, blocks[1] * rows + rows - 1, borders, count * rows)
    q = jnp.concatenate([t_ref[b, 0:HEAD, :] for b in blocks], axis=1)
    q = jnp.concatenate([q, jnp.zeros_like(q)], axis=0)
    places = lax.broadcasted_iota(jnp.int32, (1, rows), 1)
    row = scenes(jnp.concatenate([places + b * rows for b in blocks], axis=1), borders)

    def score(j, top):
        keys = pl.ds(pl.multiple_of(j * KT, KT), KT)
        s = jnp.dot(n_ref[keys, 0 : 2 * HEAD], q, preferred_element_type=f32)
        col = scenes(lax.broadcasted_iota(jnp.int32, (KT, 1), 0) + j * KT, borders)
        s = jnp.where(col == row, s, NEG)
        s_s[keys, :] = s
        return jnp.maximum(top, jnp.max(s, axis=0, keepdims=True))

    top = lax.fori_loop(lo, hi, score, jnp.full((1, QT), NEG, f32))

    def weigh(j, total):
        keys = pl.ds(pl.multiple_of(j * KT, KT), KT)
        p = jnp.exp(s_s[keys, :] - top)
        s_s[keys, :] = p
        return total + jnp.sum(p, axis=0, keepdims=True)

    total = lax.fori_loop(lo, hi, weigh, jnp.zeros((1, QT), f32))
    share = 1.0 / total

    def store(j, carry):
        keys = pl.ds(pl.multiple_of(j * KT, KT), KT)
        p_ref[0, keys, :] = (s_s[keys, :] * share).astype(bf16)
        return carry

    lax.fori_loop(lo, hi, store, 0)


def prepare(ids, scene_len, head_t, head_n):
    count, _, rows = head_t.shape
    total = count * rows
    tiles = total // 2 // QT
    return pl.pallas_call(
        prepare_kernel,
        grid_spec=pltpu.PrefetchScalarGridSpec(
            num_scalar_prefetch=2,
            grid=(tiles,),
            in_specs=[full(head_t.shape), full((total, 4 * HEAD))],
            out_specs=pl.BlockSpec((1, total, QT), lambda i, *_: (i, 0, 0)),
            scratch_shapes=[pltpu.VMEM((total, QT), f32)],
        ),
        out_shape=jax.ShapeDtypeStruct((tiles, total, QT), bf16),
        cost_estimate=HINT,
        name="prepare",
    )(ids, scene_len, head_t, head_n.reshape(total, 4 * HEAD))


def back_kernel(
    ids_ref, len_ref, p_ref, ga_ref, t_ref, n_ref, h_far,
    gq_out, mine_out, other_out, slice_mine, slice_other, dp_s, gkv_s, g_s, h_ref, sem,
):
    step = pl.program_id(0)
    part = ids_ref[0] & 1
    count, _, rows = t_ref.shape
    blocks = [4 * step + 2 * i + part for i in range(2)]
    lo, hi = tiles_of(blocks[0] * rows, blocks[1] * rows + rows - 1, borders_of(len_ref), count * rows)
    load = pltpu.make_async_copy(h_far, h_ref, sem)

    @pl.when(step == 0)
    def _():
        load.start()
        gkv_s[...] = jnp.zeros_like(gkv_s)
        g_s[...] = jnp.zeros_like(g_s)

    spans = [pl.ds(pl.multiple_of(b * rows, rows), rows) for b in blocks]
    ga_t = jnp.concatenate([ga_ref[0], ga_ref[1]], axis=1)
    ga_t = jnp.concatenate([ga_t, jnp.zeros_like(ga_t)], axis=0)
    ga = ga_t.T
    kq = jnp.concatenate([n_ref[span, 0 : 2 * HEAD] for span in spans], axis=0)
    q = jnp.where(lax.broadcasted_iota(jnp.int32, kq.shape, 1) >= HEAD, kq, jnp.zeros_like(kq))

    def first(j, delta):
        keys = pl.ds(pl.multiple_of(j * KT, KT), KT)
        p = p_ref[0, keys, :]
        dp = jnp.dot(n_ref[keys, 2 * HEAD :], ga_t, preferred_element_type=f32)
        dp_s[keys, :] = dp
        gkv_s[keys, :] += jnp.dot(p, ga, preferred_element_type=f32)
        return delta + jnp.sum(p.astype(f32) * dp, axis=0, keepdims=True)

    delta = lax.fori_loop(lo, hi, first, jnp.zeros((1, QT), f32))

    def second(j, gq):
        keys = pl.ds(pl.multiple_of(j * KT, KT), KT)
        ds = (p_ref[0, keys, :].astype(f32) * (dp_s[keys, :] - delta)).astype(bf16)
        gkv_s[keys, :] += jnp.dot(ds, q, preferred_element_type=f32)
        some = KT // rows
        k_t = jnp.concatenate([t_ref[j * some + i, HEAD : 2 * HEAD, :] for i in range(some)], axis=1)
        return gq + jnp.dot(k_t, ds, preferred_element_type=f32)

    gq = lax.fori_loop(lo, hi, second, jnp.zeros((HEAD, QT), f32))
    gq = (gq * HEAD ** (-0.5)).astype(bf16)
    for i in range(2):
        tile = gq[:, i * rows : (i + 1) * rows]
        gq_out[2 * step + i] = tile
        g_s[0:HEAD, spans[i]] = tile

    @pl.when(step == pl.num_programs(0) - 1)
    def _():
        for m in range(count // 2):
            for out, b in ((mine_out, 2 * m + part), (other_out, 2 * m + 1 - part)):
                tokens = pl.ds(pl.multiple_of(b * rows, rows), rows)
                both = gkv_s[tokens, :].T
                out[m] = both.astype(out.dtype)
                g_s[HEAD:, tokens] = both.astype(bf16)
        load.wait()
        slices = jnp.dot(g_s[...], h_ref[...], preferred_element_type=f32)
        wide = slice_mine.shape[1]
        left, right = slices[:, :wide], slices[:, wide:]
        slice_mine[...] = jnp.where(part == 0, left, right)
        slice_other[...] = jnp.where(part == 0, right, left).astype(bf16)


def back(ids, scene_len, p, ga, head_t, head_n, h1):
    count, three, rows = head_t.shape
    width = h1.shape[-1]
    total = count * rows
    half = count // 2
    kept = [
        ((half, HEAD, rows), bf16),
        ((half, 2 * HEAD, rows), f32),
        ((half, 2 * HEAD, rows), bf16),
        ((three, width // 2), f32),
        ((three, width // 2), bf16),
    ]
    return pl.pallas_call(
        back_kernel,
        grid_spec=pltpu.PrefetchScalarGridSpec(
            num_scalar_prefetch=2,
            grid=(p.shape[0],),
            in_specs=[
                pl.BlockSpec((1, total, QT), lambda i, *_: (i, 0, 0)),
                pl.BlockSpec((2, HEAD, rows), lambda i, *_: (i, 0, 0)),
                full(head_t.shape),
                full((total, 4 * HEAD)),
                FAR,
            ],
            out_specs=[NEAR] * 5,
            scratch_shapes=[
                pltpu.VMEM((total, QT), f32),
                pltpu.VMEM((total, 2 * HEAD), f32),
                pltpu.VMEM((three, total), bf16),
                pltpu.VMEM((total, width), bf16),
                pltpu.SemaphoreType.DMA,
            ],
        ),
        out_shape=[jax.ShapeDtypeStruct(shape, kind) for shape, kind in kept],
        cost_estimate=HINT,
        name="back",
    )(ids, scene_len, p, ga, head_t, head_n.reshape(total, 4 * HEAD), h1.reshape(total, width))


def share_kernel(ids_ref, low_ref, attended_ref, mine_out, other_out):
    part = ids_ref[0] & 1
    whole = lax.dot_general(low_ref[...], attended_ref[...], FIRST, preferred_element_type=f32)
    whole = whole.reshape(mine_out.shape[0], 2, mine_out.shape[1], mine_out.shape[2])
    mine_out[...] = jnp.where(part == 0, whole[:, 0], whole[:, 1])
    other_out[...] = jnp.where(part == 0, whole[:, 1], whole[:, 0]).astype(bf16)


def share_output(ids, low, attended, count):
    shape = (count // 2, low.shape[1] // count, attended.shape[1])
    return pl.pallas_call(
        share_kernel,
        in_specs=[SCALAR, NEAR, NEAR],
        out_specs=[NEAR] * 2,
        out_shape=[jax.ShapeDtypeStruct(shape, f32), jax.ShapeDtypeStruct(shape, bf16)],
        compiler_params=room(16),
        cost_estimate=HINT,
        name="share_output",
    )(ids, *near(low, attended))


def merge_kernel(gq_ref, kept_ref, given_ref, mine_ref, other_ref, out_ref):
    out_ref[:, 0:HEAD, :] = gq_ref[...]
    out_ref[:, HEAD : 3 * HEAD, :] = (kept_ref[...] + given_ref[...].astype(f32)).astype(bf16)
    lanes = out_ref.shape[2]
    slots = mine_ref.shape[1]
    for c in range(mine_ref.shape[2] // lanes):
        span = slice(c * lanes, (c + 1) * lanes)
        both = mine_ref[:, :, span] + other_ref[:, :, span].astype(f32)
        out_ref[:, 3 * HEAD + c * slots : 3 * HEAD + (c + 1) * slots, :] = both.astype(bf16)


def merge(gq, kept, given, mine, other):
    half, _, rows = gq.shape
    extra = mine.shape[1] * mine.shape[2] // rows
    return pl.pallas_call(
        merge_kernel,
        in_specs=[NEAR] * 5,
        out_specs=NEAR,
        out_shape=jax.ShapeDtypeStruct((half, 3 * HEAD + extra, rows), bf16),
        compiler_params=room(8),
        cost_estimate=HINT,
        name="merge",
    )(*near(gq, kept, given, mine, other))


def home_kernel(home_ref, q_ref, v_ref, k_ref, grad_out, slice_out):
    rows = home_ref.shape[2]
    grad = 0.0
    for i, weight in enumerate((q_ref, v_ref, k_ref)):
        across = home_ref[:, i * HEAD : (i + 1) * HEAD, :].reshape(-1, rows)
        grad = grad + lax.dot_general(across.T, weight[...], LAST, preferred_element_type=f32)
    grad_out[...] = grad.astype(bf16)
    slots = slice_out.shape[0]
    for c in range(slice_out.shape[1] // rows):
        at = 3 * HEAD + c * slots
        whole = jnp.sum(home_ref[:, at : at + slots, :].astype(f32), axis=0)
        slice_out[:, c * rows : (c + 1) * rows] = whole.astype(bf16)


def go_home(home, weights, slots):
    rows = home.shape[2]
    width, columns = weights[0].shape
    return pl.pallas_call(
        home_kernel,
        in_specs=[NEAR] * 4,
        out_specs=[NEAR] * 2,
        out_shape=[
            jax.ShapeDtypeStruct((rows, width), bf16),
            jax.ShapeDtypeStruct((slots, columns), bf16),
        ],
        cost_estimate=HINT,
        name="go_home",
    )(home, *weights)


def input_back_kernel(x_ref, mine_ref, other_ref, gain_ref, grad_ref, sums_ref, slice_ref, grad_out, unit_out):
    x = x_ref[...].astype(f32)
    center = x - jnp.mean(x, axis=1, keepdims=True)
    scale = lax.rsqrt(jnp.mean(center * center, axis=1, keepdims=True) + 1e-05)
    normed = center * scale
    grad = mine_ref[...].astype(f32) + other_ref[...].astype(f32)
    sums = [jnp.sum(grad * normed, axis=0, keepdims=True), jnp.sum(grad, axis=0, keepdims=True), sums_ref[...]]
    sums = jnp.concatenate(sums, axis=0)
    slots, wide = slice_ref.shape
    left = jnp.concatenate([sums[:, :wide], sums[:, wide:]], axis=0)
    terms = []
    for _ in range(3):
        terms.append(left.astype(bf16))
        left = left - terms[-1].astype(f32)
    unit_out[0:slots, :] = slice_ref[...]
    unit_out[slots:, :] = jnp.concatenate(terms, axis=0)
    grad = grad * gain_ref[...]
    inner = jnp.mean(grad * normed, axis=1, keepdims=True)
    grad_out[...] = grad_ref[...] + scale * (grad - jnp.mean(grad, axis=1, keepdims=True) - normed * inner)


def input_back(x, mine, other, gain, grad_middle, sums, row_slice):
    rows, width = x.shape
    slots, wide = row_slice.shape
    return pl.pallas_call(
        input_back_kernel,
        in_specs=[NEAR] * 7,
        out_specs=[NEAR] * 2,
        out_shape=[
            jax.ShapeDtypeStruct((rows, width), f32),
            jax.ShapeDtypeStruct((slots + 12 * width // wide, wide), bf16),
        ],
        compiler_params=room(16),
        cost_estimate=HINT,
        name="input_back",
    )(x, mine, other, gain.reshape(1, width), grad_middle, sums, row_slice)


def through_kernel(g_ref, down_ref, out_ref):
    out_ref[...] = jnp.dot(g_ref[...], down_ref[...], preferred_element_type=f32).astype(bf16)


def through(g, weight):
    total, width = g.shape
    hidden = weight.shape[1]
    tile = 2 * FT
    return pl.pallas_call(
        through_kernel,
        grid=(hidden // tile,),
        in_specs=[
            pl.BlockSpec((total, width), lambda i: (0, 0), pipeline_mode=pl.Buffered(1)),
            pl.BlockSpec((width, tile), lambda i: (0, i)),
        ],
        out_specs=pl.BlockSpec((total, tile), lambda i: (0, i)),
        out_shape=jax.ShapeDtypeStruct((total, hidden), bf16),
        cost_estimate=pl.CostEstimate(
            flops=2 * total * width * hidden, bytes_accessed=8 * total * width, transcendentals=0
        ),
        name="through",
    )(g, weight)


def ffn_kernel(h_ref, g_ref, grad_ref, up_ref, *outs):
    up_out, down_out = outs[-2:]
    steps = h_ref.shape[0] // TT

    def product(j):
        return jnp.dot(h_ref[j * TT : (j + 1) * TT, :], up_ref[...], preferred_element_type=f32)

    pre = product(0)
    for j in range(steps):
        later = product(j + 1) if j + 1 < steps else None
        span = slice(j * TT, (j + 1) * TT)
        act, grad_pre = gelu_both(pre, grad_ref[span, :].astype(f32))
        up = lax.dot_general(h_ref[span, :], grad_pre, FIRST, preferred_element_type=f32)
        down = lax.dot_general(g_ref[span, :], act, FIRST, preferred_element_type=f32)
        if j == 0:
            up_out[...] = up
            down_out[...] = down
        else:
            up_out[...] += up
            down_out[...] += down
        pre = later


def ffn_grads(h, g, grad, up_weight, tiles, held):
    total, width = h.shape
    hidden = up_weight.shape[1]
    first, last = tiles
    tokens = pl.BlockSpec((total, width), lambda i: (0, 0), pipeline_mode=pl.Buffered(1))
    units = pl.BlockSpec((width, FT), lambda i: (0, first + i))
    return pl.pallas_call(
        ffn_kernel,
        grid=(last - first,),
        in_specs=[tokens, tokens, pl.BlockSpec((total, FT), lambda i: (0, first + i)), units] + [FAR] * len(held),
        out_specs=[units] * 2,
        out_shape=[jax.ShapeDtypeStruct((width, hidden), f32)] * 2,
        input_output_aliases={4: 0, 5: 1} if held else {},
        cost_estimate=pl.CostEstimate(
            flops=6 * total * width * FT * (last - first), bytes_accessed=4 * total * width, transcendentals=0
        ),
        name="ffn_grads",
    )(h, g, grad, up_weight, *held)


def finish_heads_kernel(ids_ref, *refs):
    heads, outs = refs[:4], refs[4:]
    row, part = (ids_ref[0] >> 1) & 1, ids_ref[0] & 1
    wide = heads[0].shape[2]
    for k, x in ((0, part), (1, 1 - part)):
        rows = pl.ds(pl.multiple_of(x * wide, wide), wide)
        for i in range(3):
            this = heads[k][0, i * HEAD : (i + 1) * HEAD, :]
            that = heads[k + 2][0, i * HEAD : (i + 1) * HEAD, :]
            pair = [jnp.where(row == 0, this, that), jnp.where(row == 0, that, this)]
            outs[i][rows, :] = jnp.concatenate(pair, axis=0).T.astype(f32)


def finish_rows_kernel(ids_ref, *refs):
    pieces, out_ref, sums_out, terms_s = refs[:4], refs[4], refs[5], refs[6]
    count = terms_s.shape[0]
    slots = out_ref.shape[0] // count
    wide = out_ref.shape[1]
    for k in range(4):
        for s in range(4):
            block = ((ids_ref[0] - 4 * s) & 15) ^ k
            out_ref[pl.ds(pl.multiple_of(block * slots, slots), slots), :] = pieces[k][s, 0:slots, :].astype(f32)
            terms_s[block] = pieces[k][s, slots:, :].astype(f32)
    n = terms_s.shape[1] // 3
    total = jnp.zeros((n, wide), f32)
    for b in range(count):
        total += terms_s[b, 0:n] + (terms_s[b, n : 2 * n] + terms_s[b, 2 * n :])
    sums_out[:, 0:wide] = total[0 : n // 2]
    sums_out[:, wide:] = total[n // 2 :]


def finish_rows(ids, pieces, width, columns, count):
    extra = pieces[0].shape[1] - width // count
    return pl.pallas_call(
        finish_rows_kernel,
        in_specs=[SCALAR] + [NEAR] * 4,
        out_specs=[NEAR] * 2,
        out_shape=[
            jax.ShapeDtypeStruct((width, columns), f32),
            jax.ShapeDtypeStruct((4, width), f32),
        ],
        scratch_shapes=[pltpu.VMEM((count, extra, columns), f32)],
        compiler_params=room(16),
        cost_estimate=HINT,
        name="finish_rows",
    )(ids, *near(*pieces))


def finish_heads(ids, pieces, width, columns):
    block = pl.BlockSpec((width, columns // 4), lambda s, ids: (0, ((ids[0] - 4 * s) & 15) >> 2))
    return pl.pallas_call(
        finish_heads_kernel,
        grid_spec=pltpu.PrefetchScalarGridSpec(
            num_scalar_prefetch=1,
            grid=(4,),
            in_specs=[pl.BlockSpec((1,) + p.shape[1:], lambda s, ids: (s, 0, 0)) for p in pieces],
            out_specs=[block] * 3,
        ),
        out_shape=[jax.ShapeDtypeStruct((width, columns), f32)] * 3,
        cost_estimate=HINT,
        name="finish_heads",
    )(ids, *pieces)


def shuffle(block, target):
    return lax.ppermute(block, "blk", [(i, target(i)) for i in range(16)])


def over_core(block):
    return lax.ppermute(block, "tp", [(0, 1), (1, 0)])


def send_column(unit):
    return (unit,) + tuple(shuffle(unit, lambda i, s=s: (i + 4 * s) % 16) for s in (1, 2, 3))


def stack_column(parts, *first):
    return jnp.stack(lax.optimization_barrier(parts + first)[:4])


def gather_plane(column):
    return (column,) + tuple(shuffle(column, lambda i, k=k: i ^ k) for k in (1, 2, 3))


def after(value, *first):
    return lax.optimization_barrier((value,) + first)[0]


def fast_body(
    tokens,
    first_gain,
    first_bias,
    second_gain,
    second_bias,
    query_weight,
    key_weight,
    value_weight,
    output_weight,
    up_weight,
    down_weight,
    cotangent,
    scene_len,
):
    count = lax.axis_size("blk")
    place = lax.axis_index("blk")
    side = lax.axis_index("tp")
    rows, width = tokens.shape
    columns = query_weight.shape[1]
    heads_here = columns // HEAD
    share = count // heads_here
    scale = HEAD ** (-0.5)
    ids = jnp.stack([place, side])
    half_at = side.astype(jnp.uint32) * jnp.uint32(rows // 2)
    head_at = (place.astype(jnp.uint32) >> 1) * jnp.uint32(HEAD)
    alike = [list(range(r, count, share)) for r in range(share)]

    def half_of(block):
        return lax.dynamic_slice(block, (half_at, jnp.uint32(0)), (rows // 2, width))

    def head_of(weight):
        return lax.dynamic_slice(weight, (jnp.uint32(0), head_at), (width, HEAD))

    g_all = lax.all_gather(half_of(cotangent), ("blk", "tp"), axis=0, tiled=True)
    column = jnp.stack(send_column(half_of(tokens)))

    head_query = head_of(query_weight) * jnp.asarray(scale, bf16)
    head_key, head_value = head_of(key_weight), head_of(value_weight)
    head_t = jnp.concatenate([head_query, head_key, head_value], axis=1).T
    head_n = jnp.concatenate([head_key, head_query, head_value, jnp.zeros_like(head_value)], axis=1)
    params = (first_gain.reshape(1, -1), first_bias.reshape(1, -1), key_weight, value_weight, head_t, head_n)

    across_x = shuffle(column, lambda i: i ^ 1)
    across_y = shuffle(column, lambda i: i ^ 2)
    made = project_blocks(0, ids, column, over_core(column), params, count, ())
    across_y = after(across_y, made[0])
    diagonal = shuffle(across_y, lambda i: i ^ 1)
    for flip, piece in ((1, after(across_x, across_y)), (2, across_y), (3, diagonal)):
        piece = after(piece, made[0]) if piece is diagonal else piece
        made = project_blocks(flip, ids, piece, over_core(piece), params, count, made)
    h1_all, keys, values, head_t, head_n = made

    attended, branch = attend(
        ids, scene_len, h1_all, keys.reshape(-1, columns), values.reshape(-1, columns), query_weight, output_weight
    )
    inputs = tokens.astype(f32)
    middle = inputs + (branch.astype(f32) + over_core(branch).astype(f32))
    h2 = layer_norm(middle, second_gain, second_bias).astype(bf16)
    h2_all = lax.all_gather(half_of(h2), ("blk", "tp"), axis=0, tiled=True)

    feed, grad_two = own_ffn(h2, cotangent, up_weight, down_weight)
    grad_middle, grad_middle_low, second_sums, to_heads = norm_back(
        middle, grad_two, over_core(grad_two), second_gain, cotangent, output_weight
    )
    ga = lax.all_to_all(to_heads, "blk", 0, 0, tiled=True, axis_index_groups=alike)
    p = prepare(ids, scene_len, after(head_t, to_heads, g_all), head_n)
    grad_q, kept, given, slice_kept, slice_given = back(ids, scene_len, p, ga, head_t, head_n, h1_all)

    output_kept, output_given = share_output(ids, after(grad_middle_low, slice_given), attended, count)
    output_other = shuffle(output_given, lambda i: i ^ 1)
    head_slice = (slice_kept + shuffle(slice_given, lambda i: i ^ 1).astype(f32)).astype(bf16)
    parts = send_column(head_slice)

    given = after(given, head_slice)
    given = shuffle(given, lambda i: i ^ 1)
    grad_all = through(after(g_all, head_slice), down_weight)
    feed = after(feed, head_slice)
    layer_out = (middle + (feed.astype(f32) + over_core(feed).astype(f32))).astype(bf16)
    column = stack_column(parts, grad_all, layer_out)
    parcel = merge(after(grad_q, column), kept, given, output_kept, output_other)
    home = lax.all_to_all(parcel, "blk", 0, 0, tiled=True, axis_index_groups=alike)
    heads = gather_plane(column)

    held = ffn_grads(after(h2_all, column), g_all, grad_all, up_weight, (0, 5), ())

    home = after(home, held[0])
    grad_one, output_slice = go_home(home, (query_weight, value_weight, key_weight), width // count)
    input_grad, unit = input_back(
        tokens, grad_one, over_core(grad_one), first_gain, grad_middle, second_sums, output_slice
    )
    parts = send_column(unit)
    held = ffn_grads(after(h2_all, unit, *heads), g_all, grad_all, up_weight, (5, 7), held)
    column = stack_column(parts, held[0])
    rest = gather_plane(column)
    up_grad, down_grad = ffn_grads(after(h2_all, column), g_all, grad_all, up_weight, (7, 8), held)
    heads = (after(heads[0], up_grad),) + heads[1:]
    query_grad, value_grad, key_grad = finish_heads(ids, heads, width, columns)
    rest = (after(rest[0], query_grad),) + rest[1:]
    output_grad, norm_sums = finish_rows(ids, rest, width, columns, count)
    return (
        layer_out,
        input_grad,
        norm_sums[0],
        norm_sums[1],
        norm_sums[2],
        norm_sums[3],
        query_grad,
        key_grad,
        value_grad,
        output_grad,
        up_grad,
        down_grad,
    )


def solution(mesh):
    body = fast_body if mesh.shape["blk"] == 16 else ring_body
    return jax.shard_map(
        body,
        mesh=mesh,
        in_specs=(
            P("blk", None),
            P(),
            P(),
            P(),
            P(),
            P(None, "tp"),
            P(None, "tp"),
            P(None, "tp"),
            P(None, "tp"),
            P(None, "tp"),
            P(None, "tp"),
            P("blk", None),
            P(),
        ),
        out_specs=(
            P("blk", None),
            P("blk", None),
            P(),
            P(),
            P(),
            P(),
            P(None, "tp"),
            P(None, "tp"),
            P(None, "tp"),
            P(None, "tp"),
            P(None, "tp"),
            P(None, "tp"),
        ),
        check_vma=False,
    )
```

```python
import jax
import jax.numpy as jnp
from jax import lax
from jax.experimental import pallas as pl
from jax.experimental.pallas import tpu as pltpu
from jax.sharding import PartitionSpec as P

HEAD = 64
NEG = -1e30
f32 = jnp.float32
bf16 = jnp.bfloat16
LAST = (((1,), (1,)), ((), ()))
FIRST = (((0,), (0,)), ((), ()))


def from_behind(block, axis, distance):
    devices = range(lax.axis_size(axis))
    route = [((i - distance) % len(devices), i) for i in devices]
    return lax.ppermute(block, axis, route)


def layer_norm(values, gain, bias):
    center = values - jnp.mean(values, axis=-1, keepdims=True)
    spread = jnp.mean(center * center, axis=-1, keepdims=True)
    return center * lax.rsqrt(spread + 1e-05) * gain + bias


def move_grads(grad_keys, grad_values, offset):
    return (
        from_behind(grad_keys.astype(jnp.bfloat16), "blk", offset).astype(grad_keys.dtype),
        from_behind(grad_values.astype(jnp.bfloat16), "blk", offset).astype(grad_values.dtype),
    )


def ring_body(
    tokens,
    first_gain,
    first_bias,
    second_gain,
    second_bias,
    query_weight,
    key_weight,
    value_weight,
    output_weight,
    up_weight,
    down_weight,
    cotangent,
    scene_len,
):
    count = lax.axis_size("blk")
    place = lax.axis_index("blk")
    rows = tokens.shape[0]
    heads_here = query_weight.shape[1] // HEAD
    scale = HEAD ** (-0.5)
    ends = jnp.cumsum(scene_len)
    contract_last = (((1,), (1,)), ((), ()))
    contract_first = (((0,), (0,)), ((), ()))

    def scene_of(source):
        places = source * rows + jnp.arange(rows, dtype=jnp.int32)
        return jnp.sum((places[:, None] >= ends[None, :]).astype(jnp.int32), axis=1)

    mine = scene_of(place)

    def shares(source):
        other = scene_of(source)
        return jnp.maximum(mine[0], other[0]) <= jnp.minimum(mine[-1], other[-1])

    directions = (1,)
    steps = count - 1

    def source_of(way, turn):
        raw_source = place - way * turn
        return (raw_source % count, jnp.array(True))

    inputs = tokens.astype(f32)
    normed_one = layer_norm(inputs, first_gain, first_bias).astype(bf16)

    def project(weight):
        return jnp.dot(normed_one, weight, preferred_element_type=f32).astype(bf16)

    query = project(query_weight).reshape(rows, heads_here, HEAD)
    keys = project(key_weight).reshape(rows, heads_here, HEAD)
    values = project(value_weight).reshape(rows, heads_here, HEAD)

    def scores_of(key_block, source):
        mask = mine[:, None] == scene_of(source)[None, :]
        scores = jnp.einsum("qhd,khd->hqk", query, key_block, preferred_element_type=f32) * scale
        return (jnp.where(mask[None], scores, -1e30), mask)

    def absorb(state, key_block, value_block, source):
        top, total, summed = state
        scores, mask = scores_of(key_block, source)
        new_top = jnp.maximum(top, jnp.max(scores, axis=2))
        factor = jnp.exp(top - new_top)
        weights = jnp.where(mask[None], jnp.exp(scores - new_top[:, :, None]), 0.0)
        total = total * factor + jnp.sum(weights, axis=2)
        summed = summed * factor.T[:, :, None] + jnp.einsum(
            "hqk,khd->qhd", weights.astype(bf16), value_block, preferred_element_type=f32
        )
        return (new_top, total, summed)

    start = (
        jnp.full((heads_here, rows), -1e30, f32),
        jnp.zeros((heads_here, rows), f32),
        jnp.zeros((rows, heads_here, HEAD), f32),
    )
    state = absorb(start, keys, values, place)
    way = directions[0]

    def turn_forward(turn, carry):
        current, key_block, value_block = carry
        key_block, value_block = from_behind((key_block, value_block), "blk", way)
        source, inside = source_of(way, turn)
        current = lax.cond(
            inside & shares(source),
            lambda held: absorb(held, key_block, value_block, source),
            lambda held: held,
            current,
        )
        return (current, key_block, value_block)

    state, _, _ = lax.fori_loop(1, steps + 1, turn_forward, (state, keys, values))
    top, total, summed = state
    attended = summed / total.T[:, :, None]
    log_total = top + jnp.log(total)
    attended_low = attended.reshape(rows, -1).astype(bf16)
    branch = lax.dot_general(attended_low, output_weight, contract_last, preferred_element_type=f32)
    branch = lax.psum(branch.astype(jnp.bfloat16), "tp").astype(jnp.float32)
    middle = inputs + branch
    normed_two = layer_norm(middle, second_gain, second_bias).astype(bf16)
    before = jnp.dot(normed_two, up_weight, preferred_element_type=f32)
    active = jax.nn.gelu(before, approximate=False).astype(bf16)
    feed = lax.dot_general(active, down_weight, contract_last, preferred_element_type=f32)
    feed = lax.psum(feed.astype(jnp.bfloat16), "tp").astype(jnp.float32)
    layer_out = (middle + feed).astype(bf16)
    grad_out = cotangent.astype(f32)
    down_grad = lax.dot_general(cotangent, active, contract_first, preferred_element_type=f32)
    grad_active = jnp.dot(cotangent, down_weight, preferred_element_type=f32)
    _, gelu_pull = jax.vjp(lambda arg: jax.nn.gelu(arg, approximate=False), before)
    grad_before = gelu_pull(grad_active)[0].astype(bf16)
    up_grad = lax.dot_general(normed_two, grad_before, contract_first, preferred_element_type=f32)
    grad_two = lax.dot_general(grad_before, up_weight, contract_last, preferred_element_type=f32)
    grad_two = lax.psum(grad_two.astype(jnp.bfloat16), "tp").astype(jnp.float32)
    _, second_pull = jax.vjp(layer_norm, middle, second_gain, second_bias)
    grad_middle_norm, second_gain_grad, second_bias_grad = second_pull(grad_two)
    grad_middle = grad_out + grad_middle_norm
    grad_middle_low = grad_middle.astype(bf16)
    output_grad = lax.dot_general(
        grad_middle_low, attended_low, contract_first, preferred_element_type=f32
    )
    grad_attended = jnp.dot(grad_middle_low, output_weight, preferred_element_type=f32).astype(bf16)
    grad_attended = grad_attended.reshape(rows, heads_here, HEAD)
    delta = jnp.sum(grad_attended * attended, axis=2).T

    def backtrack(grads, key_block, value_block, source):
        grad_query, grad_keys, grad_values = grads
        scores, mask = scores_of(key_block, source)
        probs = jnp.where(mask[None], jnp.exp(scores - log_total[:, :, None]), 0.0)
        grad_values = grad_values + jnp.einsum(
            "hqk,qhd->khd", probs.astype(bf16), grad_attended, preferred_element_type=f32
        )
        grad_probs = jnp.einsum(
            "qhd,khd->hqk", grad_attended, value_block, preferred_element_type=f32
        )
        grad_scores = (probs * (grad_probs - delta[:, :, None]) * scale).astype(bf16)
        grad_query = grad_query + jnp.einsum(
            "hqk,khd->qhd", grad_scores, key_block, preferred_element_type=f32
        )
        grad_keys = grad_keys + jnp.einsum(
            "hqk,qhd->khd", grad_scores, query, preferred_element_type=f32
        )
        return (grad_query, grad_keys, grad_values)

    empty = jnp.zeros((rows, heads_here, HEAD), f32)
    grad_query, home_keys, home_values = backtrack((empty, empty, empty), keys, values, place)
    way = directions[0]

    def turn_backward(turn, carry):
        grad_q, key_block, value_block, grad_k, grad_v = carry
        key_block, value_block = from_behind((key_block, value_block), "blk", way)
        grad_k, grad_v = move_grads(grad_k, grad_v, way)
        source, inside = source_of(way, turn)
        grad_q, grad_k, grad_v = lax.cond(
            inside & shares(source),
            lambda held: backtrack(held, key_block, value_block, source),
            lambda held: held,
            (grad_q, grad_k, grad_v),
        )
        return (grad_q, key_block, value_block, grad_k, grad_v)

    grad_query, _, _, moved_keys, moved_values = lax.fori_loop(
        1, steps + 1, turn_backward, (grad_query, keys, values, empty, empty)
    )
    moved_keys, moved_values = move_grads(moved_keys, moved_values, -way * steps)
    home_keys = home_keys + moved_keys
    home_values = home_values + moved_values
    grad_query = grad_query.reshape(rows, -1).astype(bf16)
    grad_keys = home_keys.reshape(rows, -1).astype(bf16)
    grad_values = home_values.reshape(rows, -1).astype(bf16)
    query_grad = lax.dot_general(normed_one, grad_query, contract_first, preferred_element_type=f32)
    key_grad = lax.dot_general(normed_one, grad_keys, contract_first, preferred_element_type=f32)
    value_grad = lax.dot_general(
        normed_one, grad_values, contract_first, preferred_element_type=f32
    )
    grad_one = lax.dot_general(grad_query, query_weight, contract_last, preferred_element_type=f32)
    grad_one = grad_one + lax.dot_general(
        grad_keys, key_weight, contract_last, preferred_element_type=f32
    )
    grad_one = grad_one + lax.dot_general(
        grad_values, value_weight, contract_last, preferred_element_type=f32
    )
    grad_one = lax.psum(grad_one.astype(jnp.bfloat16), "tp").astype(jnp.float32)
    _, first_pull = jax.vjp(layer_norm, inputs, first_gain, first_bias)
    grad_input_norm, first_gain_grad, first_bias_grad = first_pull(grad_one)
    input_grad = grad_middle + grad_input_norm
    norm_grads = jnp.stack(
        [first_gain_grad, first_bias_grad, second_gain_grad, second_bias_grad], axis=1
    )
    summed_parts = (
        lax.psum_scatter(query_grad, "blk", scatter_dimension=0, tiled=True),
        lax.psum_scatter(key_grad, "blk", scatter_dimension=0, tiled=True),
        lax.psum_scatter(value_grad, "blk", scatter_dimension=0, tiled=True),
        lax.psum_scatter(output_grad, "blk", scatter_dimension=0, tiled=True),
        lax.psum_scatter(up_grad, "blk", scatter_dimension=0, tiled=True),
        lax.psum_scatter(down_grad, "blk", scatter_dimension=0, tiled=True),
        lax.psum_scatter(norm_grads, "blk", scatter_dimension=0, tiled=True),
    )
    totals = (
        lax.all_gather(summed_parts[0].astype(jnp.bfloat16), "blk", axis=0, tiled=True).astype(
            jnp.float32
        ),
        lax.all_gather(summed_parts[1].astype(jnp.bfloat16), "blk", axis=0, tiled=True).astype(
            jnp.float32
        ),
        lax.all_gather(summed_parts[2].astype(jnp.bfloat16), "blk", axis=0, tiled=True).astype(
            jnp.float32
        ),
        lax.all_gather(summed_parts[3].astype(jnp.bfloat16), "blk", axis=0, tiled=True).astype(
            jnp.float32
        ),
        lax.all_gather(summed_parts[4].astype(jnp.bfloat16), "blk", axis=0, tiled=True).astype(
            jnp.float32
        ),
        lax.all_gather(summed_parts[5].astype(jnp.bfloat16), "blk", axis=0, tiled=True).astype(
            jnp.float32
        ),
        lax.all_gather(summed_parts[6].astype(jnp.bfloat16), "blk", axis=0, tiled=True).astype(
            jnp.float32
        ),
    )
    return (
        layer_out,
        input_grad,
        totals[6][:, 0],
        totals[6][:, 1],
        totals[6][:, 2],
        totals[6][:, 3],
        totals[0],
        totals[1],
        totals[2],
        totals[3],
        totals[4],
        totals[5],
    )


HINT = pl.CostEstimate(flops=1, bytes_accessed=1, transcendentals=1)
NEAR = pl.BlockSpec(memory_space=pltpu.VMEM)
FAR = pl.BlockSpec(memory_space=pltpu.HBM)
SCALAR = pl.BlockSpec(memory_space=pltpu.SMEM)
QT = 256
KT = 512
FT = 256
TT = 1024


def near(*arrays):
    return [pltpu.with_memory_space_constraint(array, pltpu.VMEM) for array in arrays]


def room(mib):
    return pltpu.CompilerParams(vmem_limit_bytes=mib << 20)


def full(shape):
    return pl.BlockSpec(shape, lambda *_: (0,) * len(shape))


def borders_of(len_ref):
    borders = [len_ref[0]]
    for s in range(1, len_ref.shape[0] - 1):
        borders.append(borders[-1] + len_ref[s])
    return borders


def scenes(positions, borders):
    scene = jnp.zeros_like(positions)
    for border in borders:
        scene += (positions >= border).astype(jnp.int32)
    return scene


def tiles_of(first, last, borders, total):
    low, high = 0, total
    for border in borders:
        low = jnp.where(border <= first, border, low)
    for border in reversed(borders):
        high = jnp.where(border > last, border, high)
    return lax.div(low, KT), lax.div(high + KT - 1, KT)


def project_kernel(flip, ids_ref, mine_ref, other_ref, gain_ref, bias_ref, k_ref, v_ref, t_ref, n_ref, *rest):
    h_out, k_out, v_out, t_out, n_out, h_s = rest[-6:]
    n, half, width = mine_ref.shape
    rows = 2 * half
    first = ids_ref[1] == 0

    def norm(b, carry):
        mine, other = mine_ref[b], other_ref[b]
        block = jnp.concatenate([jnp.where(first, mine, other), jnp.where(first, other, mine)], axis=0)
        h_s[b] = layer_norm(block.astype(f32), gain_ref[...], bias_ref[...]).astype(bf16)
        return carry

    lax.fori_loop(0, n, norm, 0)
    h = h_s[...].reshape(n * rows, width)
    keys = jnp.dot(h, k_ref[...], preferred_element_type=f32).astype(bf16)
    values = jnp.dot(h, v_ref[...], preferred_element_type=f32).astype(bf16)
    across = lax.dot_general(t_ref[...], h, LAST, preferred_element_type=f32).astype(bf16)
    down = jnp.dot(h, n_ref[...], preferred_element_type=f32).astype(bf16)
    for s in range(n):
        at = ((ids_ref[0] - 4 * s) & 15) ^ flip
        tokens = slice(s * rows, (s + 1) * rows)
        h_out[at] = h[tokens]
        k_out[at] = keys[tokens]
        v_out[at] = values[tokens]
        t_out[at] = across[:, tokens]
        n_out[at] = down[tokens]


def project_blocks(flip, ids, mine, other, params, count, held):
    half, width = mine.shape[1:]
    _, _, key_weight, value_weight, head_t, head_n = params
    shapes = [
        (2 * half, width),
        (2 * half, key_weight.shape[1]),
        (2 * half, value_weight.shape[1]),
        (head_t.shape[0], 2 * half),
        (2 * half, head_n.shape[1]),
    ]
    return pl.pallas_call(
        lambda *refs: project_kernel(flip, *refs),
        in_specs=[SCALAR] + [NEAR] * (8 + len(held)),
        out_specs=[NEAR] * 5,
        out_shape=[pltpu.VMEM((count,) + shape, bf16) for shape in shapes],
        scratch_shapes=[pltpu.VMEM((mine.shape[0], 2 * half, width), bf16)],
        input_output_aliases={9 + i: i for i in range(5)} if held else {},
        compiler_params=room(16),
        cost_estimate=HINT,
        name="project_blocks",
    )(ids, *near(mine, other, *params, *held))


def attend_kernel(ids_ref, len_ref, h_ref, k_ref, v_ref, q_ref, o_ref, out_ref, branch_ref, query_s):
    rows, width = out_ref.shape
    total = k_ref.shape[0]
    pair = 2 * HEAD
    borders = borders_of(len_ref)
    mine = scenes(lax.broadcasted_iota(jnp.int32, (rows, 1), 0) + ids_ref[0] * rows, borders)
    mask = mine == scenes(lax.broadcasted_iota(jnp.int32, (1, total), 1), borders)
    query = jnp.dot(h_ref[ids_ref[0]], q_ref[...], preferred_element_type=f32).astype(bf16)
    query = query * jnp.asarray(HEAD ** (-0.5), bf16)
    lane = lax.broadcasted_iota(jnp.int32, (rows, pair), 1) // HEAD
    query_s[...] = query

    def attend_pair(g, carry):
        lanes = pl.ds(pl.multiple_of(g * pair, pair), pair)
        keys, values, queries = k_ref[:, lanes], v_ref[:, lanes], query_s[:, lanes]
        parts = []
        for head in range(2):
            q = jnp.where(lane == head, queries, jnp.zeros_like(queries))
            s = lax.dot_general(q, keys, LAST, preferred_element_type=f32)
            s = jnp.where(mask, s, NEG)
            p = jnp.exp(s - jnp.max(s, axis=1, keepdims=True))
            weight = jnp.sum(p, axis=1, keepdims=True)
            parts.append(jnp.dot(p.astype(bf16), values, preferred_element_type=f32) / weight)
        out_ref[:, lanes] = jnp.where(lane == 0, parts[0], parts[1]).astype(bf16)
        return carry

    lax.fori_loop(0, width // pair, attend_pair, 0)
    branch = lax.dot_general(out_ref[...], o_ref[...], LAST, preferred_element_type=f32)
    branch_ref[...] = branch.astype(bf16)


def attend(ids, scene_len, h, k, v, query_weight, output_weight):
    rows = h.shape[1]
    return pl.pallas_call(
        attend_kernel,
        in_specs=[SCALAR] * 2 + [NEAR] * 5,
        out_specs=[NEAR] * 2,
        out_shape=[
            jax.ShapeDtypeStruct((rows, query_weight.shape[1]), bf16),
            jax.ShapeDtypeStruct((rows, output_weight.shape[0]), bf16),
        ],
        scratch_shapes=[pltpu.VMEM((rows, query_weight.shape[1]), bf16)],
        compiler_params=room(16),
        cost_estimate=HINT,
        name="attend",
    )(ids, scene_len, *near(h, k, v, query_weight, output_weight))


def gelu_both(pre, grad):
    half = 0.5 * (1.0 + lax.erf(pre * 0.7071067811865476))
    slope = half + pre * (jnp.exp(-0.5 * pre * pre) * 0.3989422804014327)
    return (pre * half).astype(bf16), (grad * slope).astype(bf16)


def own_kernel(h_ref, g_ref, up_ref, down_ref, feed_out, grad_out, feed_s, grad_s):
    step = pl.program_id(0)
    pre = jnp.dot(h_ref[...], up_ref[...], preferred_element_type=f32)
    grad = jnp.dot(g_ref[...], down_ref[...], preferred_element_type=f32)
    act, grad_pre = gelu_both(pre, grad)
    feed = lax.dot_general(act, down_ref[...], LAST, preferred_element_type=f32)
    grad_two = lax.dot_general(grad_pre, up_ref[...], LAST, preferred_element_type=f32)

    @pl.when(step == 0)
    def _():
        feed_s[...] = feed
        grad_s[...] = grad_two

    @pl.when(step > 0)
    def _():
        feed_s[...] += feed
        grad_s[...] += grad_two

    @pl.when(step == pl.num_programs(0) - 1)
    def _():
        feed_out[...] = feed_s[...].astype(bf16)
        grad_out[...] = grad_s[...].astype(bf16)


def own_ffn(h, g, up_weight, down_weight):
    width = h.shape[1]
    hidden = up_weight.shape[1]
    tile = 512
    return pl.pallas_call(
        own_kernel,
        grid=(hidden // tile,),
        in_specs=[NEAR, NEAR] + [pl.BlockSpec((width, tile), lambda i: (0, i))] * 2,
        out_specs=[NEAR] * 2,
        out_shape=[jax.ShapeDtypeStruct(h.shape, bf16)] * 2,
        scratch_shapes=[pltpu.VMEM(h.shape, f32)] * 2,
        cost_estimate=HINT,
        name="own_ffn",
    )(*near(h, g), up_weight, down_weight)


def norm_back_kernel(x_ref, mine_ref, other_ref, gain_ref, g_ref, o_ref, grad_out, low_out, sums_out, heads_out):
    x = x_ref[...]
    center = x - jnp.mean(x, axis=1, keepdims=True)
    scale = lax.rsqrt(jnp.mean(center * center, axis=1, keepdims=True) + 1e-05)
    normed = center * scale
    grad = mine_ref[...].astype(f32) + other_ref[...].astype(f32)
    sums_out[0:1, :] = jnp.sum(grad * normed, axis=0, keepdims=True)
    sums_out[1:2, :] = jnp.sum(grad, axis=0, keepdims=True)
    grad = grad * gain_ref[...]
    inner = jnp.mean(grad * normed, axis=1, keepdims=True)
    grad = scale * (grad - jnp.mean(grad, axis=1, keepdims=True) - normed * inner)
    grad = grad + g_ref[...].astype(f32)
    grad_out[...] = grad
    low = grad.astype(bf16)
    low_out[...] = low
    attended = jnp.dot(low, o_ref[...], preferred_element_type=f32)
    across = attended.T.astype(bf16)
    for head in range(heads_out.shape[0]):
        heads_out[head] = across[head * HEAD : (head + 1) * HEAD, :]


def norm_back(x, mine, other, gain, g, output_weight):
    rows, width = x.shape
    return pl.pallas_call(
        norm_back_kernel,
        in_specs=[NEAR] * 6,
        out_specs=[NEAR] * 4,
        out_shape=[
            jax.ShapeDtypeStruct((rows, width), f32),
            jax.ShapeDtypeStruct((rows, width), bf16),
            jax.ShapeDtypeStruct((2, width), f32),
            jax.ShapeDtypeStruct((output_weight.shape[1] // HEAD, HEAD, rows), bf16),
        ],
        compiler_params=room(16),
        cost_estimate=HINT,
        name="norm_back",
    )(*near(x, mine, other, gain.reshape(1, width), g, output_weight))


def prepare_kernel(ids_ref, len_ref, t_ref, n_ref, p_ref, s_s):
    step = pl.program_id(0)
    count, _, rows = t_ref.shape
    borders = borders_of(len_ref)
    blocks = [4 * step + 2 * i + (ids_ref[0] & 1) for i in range(2)]
    lo, hi = tiles_of(blocks[0] * rows, blocks[1] * rows + rows - 1, borders, count * rows)
    q = jnp.concatenate([t_ref[b, 0:HEAD, :] for b in blocks], axis=1)
    q = jnp.concatenate([q, jnp.zeros_like(q)], axis=0)
    places = lax.broadcasted_iota(jnp.int32, (1, rows), 1)
    row = scenes(jnp.concatenate([places + b * rows for b in blocks], axis=1), borders)

    def score(j, top):
        keys = pl.ds(pl.multiple_of(j * KT, KT), KT)
        s = jnp.dot(n_ref[keys, 0 : 2 * HEAD], q, preferred_element_type=f32)
        col = scenes(lax.broadcasted_iota(jnp.int32, (KT, 1), 0) + j * KT, borders)
        s = jnp.where(col == row, s, NEG)
        s_s[keys, :] = s
        return jnp.maximum(top, jnp.max(s, axis=0, keepdims=True))

    top = lax.fori_loop(lo, hi, score, jnp.full((1, QT), NEG, f32))

    def weigh(j, total):
        keys = pl.ds(pl.multiple_of(j * KT, KT), KT)
        p = jnp.exp(s_s[keys, :] - top)
        s_s[keys, :] = p
        return total + jnp.sum(p, axis=0, keepdims=True)

    total = lax.fori_loop(lo, hi, weigh, jnp.zeros((1, QT), f32))
    share = 1.0 / total

    def store(j, carry):
        keys = pl.ds(pl.multiple_of(j * KT, KT), KT)
        p_ref[0, keys, :] = (s_s[keys, :] * share).astype(bf16)
        return carry

    lax.fori_loop(lo, hi, store, 0)


def prepare(ids, scene_len, head_t, head_n):
    count, _, rows = head_t.shape
    total = count * rows
    tiles = total // 2 // QT
    return pl.pallas_call(
        prepare_kernel,
        grid_spec=pltpu.PrefetchScalarGridSpec(
            num_scalar_prefetch=2,
            grid=(tiles,),
            in_specs=[full(head_t.shape), full((total, 4 * HEAD))],
            out_specs=pl.BlockSpec((1, total, QT), lambda i, *_: (i, 0, 0)),
            scratch_shapes=[pltpu.VMEM((total, QT), f32)],
        ),
        out_shape=jax.ShapeDtypeStruct((tiles, total, QT), bf16),
        cost_estimate=HINT,
        name="prepare",
    )(ids, scene_len, head_t, head_n.reshape(total, 4 * HEAD))


def back_kernel(
    ids_ref, len_ref, p_ref, ga_ref, t_ref, n_ref, h_far,
    gq_out, mine_out, other_out, slice_mine, slice_other, dp_s, gkv_s, g_s, h_ref, sem,
):
    step = pl.program_id(0)
    part = ids_ref[0] & 1
    count, _, rows = t_ref.shape
    blocks = [4 * step + 2 * i + part for i in range(2)]
    lo, hi = tiles_of(blocks[0] * rows, blocks[1] * rows + rows - 1, borders_of(len_ref), count * rows)
    load = pltpu.make_async_copy(h_far, h_ref, sem)

    @pl.when(step == 0)
    def _():
        load.start()
        gkv_s[...] = jnp.zeros_like(gkv_s)
        g_s[...] = jnp.zeros_like(g_s)

    spans = [pl.ds(pl.multiple_of(b * rows, rows), rows) for b in blocks]
    ga_t = jnp.concatenate([ga_ref[0], ga_ref[1]], axis=1)
    ga_t = jnp.concatenate([ga_t, jnp.zeros_like(ga_t)], axis=0)
    ga = ga_t.T
    kq = jnp.concatenate([n_ref[span, 0 : 2 * HEAD] for span in spans], axis=0)
    q = jnp.where(lax.broadcasted_iota(jnp.int32, kq.shape, 1) >= HEAD, kq, jnp.zeros_like(kq))

    def first(j, delta):
        keys = pl.ds(pl.multiple_of(j * KT, KT), KT)
        p = p_ref[0, keys, :]
        dp = jnp.dot(n_ref[keys, 2 * HEAD :], ga_t, preferred_element_type=f32)
        dp_s[keys, :] = dp
        gkv_s[keys, :] += jnp.dot(p, ga, preferred_element_type=f32)
        return delta + jnp.sum(p.astype(f32) * dp, axis=0, keepdims=True)

    delta = lax.fori_loop(lo, hi, first, jnp.zeros((1, QT), f32))

    def second(j, gq):
        keys = pl.ds(pl.multiple_of(j * KT, KT), KT)
        ds = (p_ref[0, keys, :].astype(f32) * (dp_s[keys, :] - delta)).astype(bf16)
        gkv_s[keys, :] += jnp.dot(ds, q, preferred_element_type=f32)
        some = KT // rows
        k_t = jnp.concatenate([t_ref[j * some + i, HEAD : 2 * HEAD, :] for i in range(some)], axis=1)
        return gq + jnp.dot(k_t, ds, preferred_element_type=f32)

    gq = lax.fori_loop(lo, hi, second, jnp.zeros((HEAD, QT), f32))
    gq = (gq * HEAD ** (-0.5)).astype(bf16)
    for i in range(2):
        tile = gq[:, i * rows : (i + 1) * rows]
        gq_out[2 * step + i] = tile
        g_s[0:HEAD, spans[i]] = tile

    @pl.when(step == pl.num_programs(0) - 1)
    def _():
        for m in range(count // 2):
            for out, b in ((mine_out, 2 * m + part), (other_out, 2 * m + 1 - part)):
                tokens = pl.ds(pl.multiple_of(b * rows, rows), rows)
                both = gkv_s[tokens, :].T
                out[m] = both.astype(out.dtype)
                g_s[HEAD:, tokens] = both.astype(bf16)
        load.wait()
        slices = jnp.dot(g_s[...], h_ref[...], preferred_element_type=f32)
        wide = slice_mine.shape[1]
        left, right = slices[:, :wide], slices[:, wide:]
        slice_mine[...] = jnp.where(part == 0, left, right)
        slice_other[...] = jnp.where(part == 0, right, left).astype(bf16)


def back(ids, scene_len, p, ga, head_t, head_n, h1):
    count, three, rows = head_t.shape
    width = h1.shape[-1]
    total = count * rows
    half = count // 2
    kept = [
        ((half, HEAD, rows), bf16),
        ((half, 2 * HEAD, rows), f32),
        ((half, 2 * HEAD, rows), bf16),
        ((three, width // 2), f32),
        ((three, width // 2), bf16),
    ]
    return pl.pallas_call(
        back_kernel,
        grid_spec=pltpu.PrefetchScalarGridSpec(
            num_scalar_prefetch=2,
            grid=(p.shape[0],),
            in_specs=[
                pl.BlockSpec((1, total, QT), lambda i, *_: (i, 0, 0)),
                pl.BlockSpec((2, HEAD, rows), lambda i, *_: (i, 0, 0)),
                full(head_t.shape),
                full((total, 4 * HEAD)),
                FAR,
            ],
            out_specs=[NEAR] * 5,
            scratch_shapes=[
                pltpu.VMEM((total, QT), f32),
                pltpu.VMEM((total, 2 * HEAD), f32),
                pltpu.VMEM((three, total), bf16),
                pltpu.VMEM((total, width), bf16),
                pltpu.SemaphoreType.DMA,
            ],
        ),
        out_shape=[jax.ShapeDtypeStruct(shape, kind) for shape, kind in kept],
        cost_estimate=HINT,
        name="back",
    )(ids, scene_len, p, ga, head_t, head_n.reshape(total, 4 * HEAD), h1.reshape(total, width))


def share_kernel(ids_ref, low_ref, attended_ref, mine_out, other_out):
    part = ids_ref[0] & 1
    whole = lax.dot_general(low_ref[...], attended_ref[...], FIRST, preferred_element_type=f32)
    whole = whole.reshape(mine_out.shape[0], 2, mine_out.shape[1], mine_out.shape[2])
    mine_out[...] = jnp.where(part == 0, whole[:, 0], whole[:, 1])
    other_out[...] = jnp.where(part == 0, whole[:, 1], whole[:, 0]).astype(bf16)


def share_output(ids, low, attended, count):
    shape = (count // 2, low.shape[1] // count, attended.shape[1])
    return pl.pallas_call(
        share_kernel,
        in_specs=[SCALAR, NEAR, NEAR],
        out_specs=[NEAR] * 2,
        out_shape=[jax.ShapeDtypeStruct(shape, f32), jax.ShapeDtypeStruct(shape, bf16)],
        compiler_params=room(16),
        cost_estimate=HINT,
        name="share_output",
    )(ids, *near(low, attended))


def merge_kernel(gq_ref, kept_ref, given_ref, out_ref):
    out_ref[:, 0:HEAD, :] = gq_ref[...]
    out_ref[:, HEAD:, :] = (kept_ref[...] + given_ref[...].astype(f32)).astype(bf16)


def merge(gq, kept, given):
    half, _, rows = gq.shape
    return pl.pallas_call(
        merge_kernel,
        in_specs=[NEAR] * 3,
        out_specs=NEAR,
        out_shape=jax.ShapeDtypeStruct((half, 3 * HEAD, rows), bf16),
        compiler_params=room(8),
        cost_estimate=HINT,
        name="merge",
    )(*near(gq, kept, given))


def unit_kernel(mine_ref, other_ref, parts_ref, out_ref):
    rows = mine_ref.shape[0]
    out_ref[0:rows, :] = (mine_ref[...] + other_ref[...].astype(f32)).astype(bf16)
    out_ref[rows:, :] = jnp.sum(parts_ref[...].astype(f32), axis=0).astype(bf16)


def make_unit(mine, other, parts):
    rows, wide = mine.shape
    return pl.pallas_call(
        unit_kernel,
        in_specs=[NEAR] * 3,
        out_specs=NEAR,
        out_shape=jax.ShapeDtypeStruct((rows + parts.shape[1], wide), bf16),
        compiler_params=room(8),
        cost_estimate=HINT,
        name="make_unit",
    )(mine, other, parts)


def home_kernel(home_ref, q_ref, v_ref, k_ref, grad_out):
    rows = home_ref.shape[2]
    grad = 0.0
    for i, weight in enumerate((q_ref, v_ref, k_ref)):
        across = home_ref[:, i * HEAD : (i + 1) * HEAD, :].reshape(-1, rows)
        grad = grad + lax.dot_general(across.T, weight[...], LAST, preferred_element_type=f32)
    grad_out[...] = grad.astype(bf16)


def go_home(home, weights):
    return pl.pallas_call(
        home_kernel,
        in_specs=[NEAR] * 4,
        out_specs=NEAR,
        out_shape=jax.ShapeDtypeStruct((home.shape[2], weights[0].shape[0]), bf16),
        cost_estimate=HINT,
        name="go_home",
    )(home, *weights)


def input_back_kernel(x_ref, mine_ref, other_ref, gain_ref, grad_ref, sums_ref, grad_out, sums_out):
    x = x_ref[...].astype(f32)
    center = x - jnp.mean(x, axis=1, keepdims=True)
    scale = lax.rsqrt(jnp.mean(center * center, axis=1, keepdims=True) + 1e-05)
    normed = center * scale
    grad = mine_ref[...].astype(f32) + other_ref[...].astype(f32)
    sums = [jnp.sum(grad * normed, axis=0, keepdims=True), jnp.sum(grad, axis=0, keepdims=True), sums_ref[...]]
    sums = jnp.concatenate(sums, axis=0)
    for b in range(sums_out.shape[0]):
        sums_out[b] = sums
    grad = grad * gain_ref[...]
    inner = jnp.mean(grad * normed, axis=1, keepdims=True)
    grad_out[...] = grad_ref[...] + scale * (grad - jnp.mean(grad, axis=1, keepdims=True) - normed * inner)


def input_back(x, mine, other, gain, grad_middle, sums, count):
    rows, width = x.shape
    return pl.pallas_call(
        input_back_kernel,
        in_specs=[NEAR] * 6,
        out_specs=[NEAR] * 2,
        out_shape=[
            jax.ShapeDtypeStruct((rows, width), f32),
            jax.ShapeDtypeStruct((count, 4, width), f32),
        ],
        compiler_params=room(16),
        cost_estimate=HINT,
        name="input_back",
    )(x, mine, other, gain.reshape(1, width), grad_middle, sums)


def through_kernel(g_ref, down_ref, out_ref):
    out_ref[...] = jnp.dot(g_ref[...], down_ref[...], preferred_element_type=f32).astype(bf16)


def through(g, weight):
    total, width = g.shape
    hidden = weight.shape[1]
    tile = 2 * FT
    return pl.pallas_call(
        through_kernel,
        grid=(hidden // tile,),
        in_specs=[
            pl.BlockSpec((total, width), lambda i: (0, 0), pipeline_mode=pl.Buffered(1)),
            pl.BlockSpec((width, tile), lambda i: (0, i)),
        ],
        out_specs=pl.BlockSpec((total, tile), lambda i: (0, i)),
        out_shape=jax.ShapeDtypeStruct((total, hidden), bf16),
        cost_estimate=pl.CostEstimate(
            flops=2 * total * width * hidden, bytes_accessed=8 * total * width, transcendentals=0
        ),
        name="through",
    )(g, weight)


def ffn_kernel(h_ref, g_ref, grad_ref, up_ref, *outs):
    up_out, down_out = outs[-2:]
    steps = h_ref.shape[0] // TT

    def product(j):
        return jnp.dot(h_ref[j * TT : (j + 1) * TT, :], up_ref[...], preferred_element_type=f32)

    pre = product(0)
    for j in range(steps):
        later = product(j + 1) if j + 1 < steps else None
        span = slice(j * TT, (j + 1) * TT)
        act, grad_pre = gelu_both(pre, grad_ref[span, :].astype(f32))
        up = lax.dot_general(h_ref[span, :], grad_pre, FIRST, preferred_element_type=f32)
        down = lax.dot_general(g_ref[span, :], act, FIRST, preferred_element_type=f32)
        if j == 0:
            up_out[...] = up
            down_out[...] = down
        else:
            up_out[...] += up
            down_out[...] += down
        pre = later


def ffn_grads(h, g, grad, up_weight, tiles, held):
    total, width = h.shape
    hidden = up_weight.shape[1]
    first, last = tiles
    tokens = pl.BlockSpec((total, width), lambda i: (0, 0), pipeline_mode=pl.Buffered(1))
    units = pl.BlockSpec((width, FT), lambda i: (0, first + i))
    return pl.pallas_call(
        ffn_kernel,
        grid=(last - first,),
        in_specs=[tokens, tokens, pl.BlockSpec((total, FT), lambda i: (0, first + i)), units] + [FAR] * len(held),
        out_specs=[units] * 2,
        out_shape=[jax.ShapeDtypeStruct((width, hidden), f32)] * 2,
        input_output_aliases={4: 0, 5: 1} if held else {},
        cost_estimate=pl.CostEstimate(
            flops=6 * total * width * FT * (last - first), bytes_accessed=4 * total * width, transcendentals=0
        ),
        name="ffn_grads",
    )(h, g, grad, up_weight, *held)


def finish_heads_kernel(ids_ref, *refs):
    heads, outs = refs[:5], refs[5:]
    row, part = (ids_ref[0] >> 1) & 1, ids_ref[0] & 1
    wide = heads[0].shape[2]
    early = pl.program_id(0) < 2
    for k, x in ((0, part), (1, 1 - part)):
        rows = pl.ds(pl.multiple_of(x * wide, wide), wide)
        for i in range(3):
            span = slice(i * HEAD, (i + 1) * HEAD)
            this = heads[k][0, span, :]
            that = heads[2][0, span, :] if k == 0 else jnp.where(early, heads[3][0, span, :], heads[4][0, span, :])
            pair = [jnp.where(row == 0, this, that), jnp.where(row == 0, that, this)]
            outs[i][rows, :] = jnp.concatenate(pair, axis=0).T.astype(f32)


def finish_rows_kernel(ids_ref, *refs):
    pieces, out_ref = refs[:5], refs[5]
    slots = pieces[0].shape[1]
    for k in range(4):
        for s in range(4):
            piece = pieces[k][s] if k < 3 else pieces[3 + s // 2][s % 2]
            at = pl.multiple_of((((ids_ref[0] - 4 * s) & 15) ^ k) * slots, slots)
            out_ref[pl.ds(at, slots), :] = piece.astype(f32)


def finish_rows(ids, pieces, width, columns):
    slots = width // 16
    return pl.pallas_call(
        finish_rows_kernel,
        grid_spec=pltpu.PrefetchScalarGridSpec(
            num_scalar_prefetch=1,
            grid=(1,),
            in_specs=[
                pl.BlockSpec((p.shape[0], slots, columns), lambda i, ids: (0, 3 * HEAD // slots, 0)) for p in pieces
            ],
            out_specs=full((width, columns)),
        ),
        out_shape=jax.ShapeDtypeStruct((width, columns), f32),
        cost_estimate=HINT,
        name="finish_rows",
    )(ids, *pieces)


def finish_heads(ids, pieces, width, columns):
    block = pl.BlockSpec((width, columns // 4), lambda s, ids: (0, ((ids[0] - 4 * s) & 15) >> 2))
    shape = (1, 3 * HEAD, pieces[0].shape[2])
    whole = pl.BlockSpec(shape, lambda s, ids: (s, 0, 0))
    early = pl.BlockSpec(shape, lambda s, ids: (jnp.minimum(s, 1), 0, 0))
    late = pl.BlockSpec(shape, lambda s, ids: (jnp.maximum(s - 2, 0), 0, 0))
    return pl.pallas_call(
        finish_heads_kernel,
        grid_spec=pltpu.PrefetchScalarGridSpec(
            num_scalar_prefetch=1,
            grid=(4,),
            in_specs=[whole, whole, whole, early, late],
            out_specs=[block] * 3,
        ),
        out_shape=[jax.ShapeDtypeStruct((width, columns), f32)] * 3,
        cost_estimate=HINT,
        name="finish_heads",
    )(ids, *pieces)


def shuffle(block, target):
    return lax.ppermute(block, "blk", [(i, target(i)) for i in range(16)])


def over_core(block):
    return lax.ppermute(block, "tp", [(0, 1), (1, 0)])


def send_column(unit):
    return (unit,) + tuple(shuffle(unit, lambda i, s=s: (i + 4 * s) % 16) for s in (1, 2, 3))


def stack_column(parts, *first):
    return jnp.stack(lax.optimization_barrier(parts + first)[:4])


def gather_sides(column):
    return shuffle(column, lambda i: i ^ 1), shuffle(column, lambda i: i ^ 2)


def after(value, *first):
    return lax.optimization_barrier((value,) + first)[0]


def fast_body(
    tokens,
    first_gain,
    first_bias,
    second_gain,
    second_bias,
    query_weight,
    key_weight,
    value_weight,
    output_weight,
    up_weight,
    down_weight,
    cotangent,
    scene_len,
):
    count = lax.axis_size("blk")
    place = lax.axis_index("blk")
    side = lax.axis_index("tp")
    rows, width = tokens.shape
    columns = query_weight.shape[1]
    heads_here = columns // HEAD
    share = count // heads_here
    scale = HEAD ** (-0.5)
    ids = jnp.stack([place, side])
    half_at = side.astype(jnp.uint32) * jnp.uint32(rows // 2)
    head_at = (place.astype(jnp.uint32) >> 1) * jnp.uint32(HEAD)
    alike = [list(range(r, count, share)) for r in range(share)]

    def half_of(block):
        return lax.dynamic_slice(block, (half_at, jnp.uint32(0)), (rows // 2, width))

    def head_of(weight):
        return lax.dynamic_slice(weight, (jnp.uint32(0), head_at), (width, HEAD))

    g_all = lax.all_gather(half_of(cotangent), ("blk", "tp"), axis=0, tiled=True)
    column = jnp.stack(send_column(half_of(tokens)))

    head_query = head_of(query_weight) * jnp.asarray(scale, bf16)
    head_key, head_value = head_of(key_weight), head_of(value_weight)
    head_t = jnp.concatenate([head_query, head_key, head_value], axis=1).T
    head_n = jnp.concatenate([head_key, head_query, head_value, jnp.zeros_like(head_value)], axis=1)
    params = (first_gain.reshape(1, -1), first_bias.reshape(1, -1), key_weight, value_weight, head_t, head_n)

    across_x = shuffle(column, lambda i: i ^ 1)
    across_y = shuffle(column, lambda i: i ^ 2)
    made = project_blocks(0, ids, column, over_core(column), params, count, ())
    across_y = after(across_y, made[0])
    diagonal = shuffle(across_y, lambda i: i ^ 1)
    for flip, piece in ((1, after(across_x, across_y)), (2, across_y), (3, diagonal)):
        piece = after(piece, made[0]) if piece is diagonal else piece
        made = project_blocks(flip, ids, piece, over_core(piece), params, count, made)
    h1_all, keys, values, head_t, head_n = made

    attended, branch = attend(
        ids, scene_len, h1_all, keys.reshape(-1, columns), values.reshape(-1, columns), query_weight, output_weight
    )
    inputs = tokens.astype(f32)
    middle = inputs + (branch.astype(f32) + over_core(branch).astype(f32))
    h2 = layer_norm(middle, second_gain, second_bias).astype(bf16)
    h2_all = lax.all_gather(half_of(h2), ("blk", "tp"), axis=0, tiled=True)

    feed, grad_two = own_ffn(h2, cotangent, up_weight, down_weight)
    grad_middle, grad_middle_low, second_sums, to_heads = norm_back(
        middle, grad_two, over_core(grad_two), second_gain, cotangent, output_weight
    )
    ga = lax.all_to_all(to_heads, "blk", 0, 0, tiled=True, axis_index_groups=alike)
    output_kept, output_given = share_output(ids, after(grad_middle_low, to_heads), attended, count)
    output_other = shuffle(output_given, lambda i: i ^ 1)
    p = prepare(ids, scene_len, after(head_t, to_heads, g_all, output_given), head_n)
    output_kept, output_other, _ = lax.optimization_barrier((output_kept, output_other, p))
    output_half = (output_kept + output_other.astype(f32)).astype(bf16)
    output_parts = lax.all_to_all(after(output_half, ga, p), "blk", 0, 0, tiled=True, axis_index_groups=alike)
    grad_q, kept, given, slice_kept, slice_given = back(ids, scene_len, p, ga, head_t, head_n, h1_all)

    grad_all = through(after(g_all, grad_q), down_weight)
    slice_other = shuffle(slice_given, lambda i: i ^ 1)
    unit = make_unit(after(slice_kept, grad_all), slice_other, output_parts)
    parts = send_column(unit)
    given = shuffle(after(given, unit), lambda i: i ^ 1)
    feed = after(feed, unit)
    layer_out = (middle + (feed.astype(f32) + over_core(feed).astype(f32))).astype(bf16)
    parcel = merge(after(grad_q, unit), kept, given)
    home = lax.all_to_all(parcel, "blk", 0, 0, tiled=True, axis_index_groups=alike)
    held = ffn_grads(after(h2_all, unit, parcel), g_all, grad_all, up_weight, (0, 3), ())
    column = stack_column(parts, held[0], layer_out)
    side_x, side_y = gather_sides(column)
    up_grad, down_grad = ffn_grads(after(h2_all, column), g_all, grad_all, up_weight, (3, 8), held)

    half_x, half_y = lax.optimization_barrier((side_x[2:], side_y[:2], up_grad))[:2]
    across = shuffle(half_y, lambda i: i ^ 1), shuffle(half_x, lambda i: i ^ 2)
    home = after(home, up_grad).reshape(heads_here, 3 * HEAD, rows)
    home = after(home, half_x, half_y)
    grad_one = go_home(home, (query_weight, value_weight, key_weight))
    input_grad, norm_part = input_back(
        tokens, grad_one, over_core(grad_one), first_gain, grad_middle, second_sums, count
    )
    norm_parts = lax.all_to_all(after(norm_part, *across), "blk", 0, 0, tiled=True)
    heads = (after(column, norm_part), side_x, side_y) + across
    query_grad, value_grad, key_grad = finish_heads(ids, heads, width, columns)
    output_grad = finish_rows(ids, (after(heads[0], query_grad),) + heads[1:], width, columns)
    norm_sums = jnp.sum(after(norm_parts, output_grad), axis=0)
    return (
        layer_out,
        input_grad,
        norm_sums[0],
        norm_sums[1],
        norm_sums[2],
        norm_sums[3],
        query_grad,
        key_grad,
        value_grad,
        output_grad,
        up_grad,
        down_grad,
    )


def solution(mesh):
    body = fast_body if mesh.shape["blk"] == 16 else ring_body
    return jax.shard_map(
        body,
        mesh=mesh,
        in_specs=(
            P("blk", None),
            P(),
            P(),
            P(),
            P(),
            P(None, "tp"),
            P(None, "tp"),
            P(None, "tp"),
            P(None, "tp"),
            P(None, "tp"),
            P(None, "tp"),
            P("blk", None),
            P(),
        ),
        out_specs=(
            P("blk", None),
            P("blk", None),
            P(),
            P(),
            P(),
            P(),
            P(None, "tp"),
            P(None, "tp"),
            P(None, "tp"),
            P(None, "tp"),
            P(None, "tp"),
            P(None, "tp"),
        ),
        check_vma=False,
    )
```

```python
import jax
import jax.numpy as jnp
from jax import lax
from jax.experimental import pallas as pl
from jax.experimental.pallas import tpu as pltpu
from jax.sharding import PartitionSpec as P

HEAD = 64
NEG = -1e30
f32 = jnp.float32
bf16 = jnp.bfloat16
LAST = (((1,), (1,)), ((), ()))
FIRST = (((0,), (0,)), ((), ()))


def from_behind(block, axis, distance):
    devices = range(lax.axis_size(axis))
    route = [((i - distance) % len(devices), i) for i in devices]
    return lax.ppermute(block, axis, route)


def layer_norm(values, gain, bias):
    center = values - jnp.mean(values, axis=-1, keepdims=True)
    spread = jnp.mean(center * center, axis=-1, keepdims=True)
    return center * lax.rsqrt(spread + 1e-05) * gain + bias


def move_grads(grad_keys, grad_values, offset):
    return (
        from_behind(grad_keys.astype(jnp.bfloat16), "blk", offset).astype(grad_keys.dtype),
        from_behind(grad_values.astype(jnp.bfloat16), "blk", offset).astype(grad_values.dtype),
    )


def ring_body(
    tokens,
    first_gain,
    first_bias,
    second_gain,
    second_bias,
    query_weight,
    key_weight,
    value_weight,
    output_weight,
    up_weight,
    down_weight,
    cotangent,
    scene_len,
):
    count = lax.axis_size("blk")
    place = lax.axis_index("blk")
    rows = tokens.shape[0]
    heads_here = query_weight.shape[1] // HEAD
    scale = HEAD ** (-0.5)
    ends = jnp.cumsum(scene_len)
    contract_last = (((1,), (1,)), ((), ()))
    contract_first = (((0,), (0,)), ((), ()))

    def scene_of(source):
        places = source * rows + jnp.arange(rows, dtype=jnp.int32)
        return jnp.sum((places[:, None] >= ends[None, :]).astype(jnp.int32), axis=1)

    mine = scene_of(place)

    def shares(source):
        other = scene_of(source)
        return jnp.maximum(mine[0], other[0]) <= jnp.minimum(mine[-1], other[-1])

    directions = (1,)
    steps = count - 1

    def source_of(way, turn):
        raw_source = place - way * turn
        return (raw_source % count, jnp.array(True))

    inputs = tokens.astype(f32)
    normed_one = layer_norm(inputs, first_gain, first_bias).astype(bf16)

    def project(weight):
        return jnp.dot(normed_one, weight, preferred_element_type=f32).astype(bf16)

    query = project(query_weight).reshape(rows, heads_here, HEAD)
    keys = project(key_weight).reshape(rows, heads_here, HEAD)
    values = project(value_weight).reshape(rows, heads_here, HEAD)

    def scores_of(key_block, source):
        mask = mine[:, None] == scene_of(source)[None, :]
        scores = jnp.einsum("qhd,khd->hqk", query, key_block, preferred_element_type=f32) * scale
        return (jnp.where(mask[None], scores, -1e30), mask)

    def absorb(state, key_block, value_block, source):
        top, total, summed = state
        scores, mask = scores_of(key_block, source)
        new_top = jnp.maximum(top, jnp.max(scores, axis=2))
        factor = jnp.exp(top - new_top)
        weights = jnp.where(mask[None], jnp.exp(scores - new_top[:, :, None]), 0.0)
        total = total * factor + jnp.sum(weights, axis=2)
        summed = summed * factor.T[:, :, None] + jnp.einsum(
            "hqk,khd->qhd", weights.astype(bf16), value_block, preferred_element_type=f32
        )
        return (new_top, total, summed)

    start = (
        jnp.full((heads_here, rows), -1e30, f32),
        jnp.zeros((heads_here, rows), f32),
        jnp.zeros((rows, heads_here, HEAD), f32),
    )
    state = absorb(start, keys, values, place)
    way = directions[0]

    def turn_forward(turn, carry):
        current, key_block, value_block = carry
        key_block, value_block = from_behind((key_block, value_block), "blk", way)
        source, inside = source_of(way, turn)
        current = lax.cond(
            inside & shares(source),
            lambda held: absorb(held, key_block, value_block, source),
            lambda held: held,
            current,
        )
        return (current, key_block, value_block)

    state, _, _ = lax.fori_loop(1, steps + 1, turn_forward, (state, keys, values))
    top, total, summed = state
    attended = summed / total.T[:, :, None]
    log_total = top + jnp.log(total)
    attended_low = attended.reshape(rows, -1).astype(bf16)
    branch = lax.dot_general(attended_low, output_weight, contract_last, preferred_element_type=f32)
    branch = lax.psum(branch.astype(jnp.bfloat16), "tp").astype(jnp.float32)
    middle = inputs + branch
    normed_two = layer_norm(middle, second_gain, second_bias).astype(bf16)
    before = jnp.dot(normed_two, up_weight, preferred_element_type=f32)
    active = jax.nn.gelu(before, approximate=False).astype(bf16)
    feed = lax.dot_general(active, down_weight, contract_last, preferred_element_type=f32)
    feed = lax.psum(feed.astype(jnp.bfloat16), "tp").astype(jnp.float32)
    layer_out = (middle + feed).astype(bf16)
    grad_out = cotangent.astype(f32)
    down_grad = lax.dot_general(cotangent, active, contract_first, preferred_element_type=f32)
    grad_active = jnp.dot(cotangent, down_weight, preferred_element_type=f32)
    _, gelu_pull = jax.vjp(lambda arg: jax.nn.gelu(arg, approximate=False), before)
    grad_before = gelu_pull(grad_active)[0].astype(bf16)
    up_grad = lax.dot_general(normed_two, grad_before, contract_first, preferred_element_type=f32)
    grad_two = lax.dot_general(grad_before, up_weight, contract_last, preferred_element_type=f32)
    grad_two = lax.psum(grad_two.astype(jnp.bfloat16), "tp").astype(jnp.float32)
    _, second_pull = jax.vjp(layer_norm, middle, second_gain, second_bias)
    grad_middle_norm, second_gain_grad, second_bias_grad = second_pull(grad_two)
    grad_middle = grad_out + grad_middle_norm
    grad_middle_low = grad_middle.astype(bf16)
    output_grad = lax.dot_general(
        grad_middle_low, attended_low, contract_first, preferred_element_type=f32
    )
    grad_attended = jnp.dot(grad_middle_low, output_weight, preferred_element_type=f32).astype(bf16)
    grad_attended = grad_attended.reshape(rows, heads_here, HEAD)
    delta = jnp.sum(grad_attended * attended, axis=2).T

    def backtrack(grads, key_block, value_block, source):
        grad_query, grad_keys, grad_values = grads
        scores, mask = scores_of(key_block, source)
        probs = jnp.where(mask[None], jnp.exp(scores - log_total[:, :, None]), 0.0)
        grad_values = grad_values + jnp.einsum(
            "hqk,qhd->khd", probs.astype(bf16), grad_attended, preferred_element_type=f32
        )
        grad_probs = jnp.einsum(
            "qhd,khd->hqk", grad_attended, value_block, preferred_element_type=f32
        )
        grad_scores = (probs * (grad_probs - delta[:, :, None]) * scale).astype(bf16)
        grad_query = grad_query + jnp.einsum(
            "hqk,khd->qhd", grad_scores, key_block, preferred_element_type=f32
        )
        grad_keys = grad_keys + jnp.einsum(
            "hqk,qhd->khd", grad_scores, query, preferred_element_type=f32
        )
        return (grad_query, grad_keys, grad_values)

    empty = jnp.zeros((rows, heads_here, HEAD), f32)
    grad_query, home_keys, home_values = backtrack((empty, empty, empty), keys, values, place)
    way = directions[0]

    def turn_backward(turn, carry):
        grad_q, key_block, value_block, grad_k, grad_v = carry
        key_block, value_block = from_behind((key_block, value_block), "blk", way)
        grad_k, grad_v = move_grads(grad_k, grad_v, way)
        source, inside = source_of(way, turn)
        grad_q, grad_k, grad_v = lax.cond(
            inside & shares(source),
            lambda held: backtrack(held, key_block, value_block, source),
            lambda held: held,
            (grad_q, grad_k, grad_v),
        )
        return (grad_q, key_block, value_block, grad_k, grad_v)

    grad_query, _, _, moved_keys, moved_values = lax.fori_loop(
        1, steps + 1, turn_backward, (grad_query, keys, values, empty, empty)
    )
    moved_keys, moved_values = move_grads(moved_keys, moved_values, -way * steps)
    home_keys = home_keys + moved_keys
    home_values = home_values + moved_values
    grad_query = grad_query.reshape(rows, -1).astype(bf16)
    grad_keys = home_keys.reshape(rows, -1).astype(bf16)
    grad_values = home_values.reshape(rows, -1).astype(bf16)
    query_grad = lax.dot_general(normed_one, grad_query, contract_first, preferred_element_type=f32)
    key_grad = lax.dot_general(normed_one, grad_keys, contract_first, preferred_element_type=f32)
    value_grad = lax.dot_general(
        normed_one, grad_values, contract_first, preferred_element_type=f32
    )
    grad_one = lax.dot_general(grad_query, query_weight, contract_last, preferred_element_type=f32)
    grad_one = grad_one + lax.dot_general(
        grad_keys, key_weight, contract_last, preferred_element_type=f32
    )
    grad_one = grad_one + lax.dot_general(
        grad_values, value_weight, contract_last, preferred_element_type=f32
    )
    grad_one = lax.psum(grad_one.astype(jnp.bfloat16), "tp").astype(jnp.float32)
    _, first_pull = jax.vjp(layer_norm, inputs, first_gain, first_bias)
    grad_input_norm, first_gain_grad, first_bias_grad = first_pull(grad_one)
    input_grad = grad_middle + grad_input_norm
    norm_grads = jnp.stack(
        [first_gain_grad, first_bias_grad, second_gain_grad, second_bias_grad], axis=1
    )
    summed_parts = (
        lax.psum_scatter(query_grad, "blk", scatter_dimension=0, tiled=True),
        lax.psum_scatter(key_grad, "blk", scatter_dimension=0, tiled=True),
        lax.psum_scatter(value_grad, "blk", scatter_dimension=0, tiled=True),
        lax.psum_scatter(output_grad, "blk", scatter_dimension=0, tiled=True),
        lax.psum_scatter(up_grad, "blk", scatter_dimension=0, tiled=True),
        lax.psum_scatter(down_grad, "blk", scatter_dimension=0, tiled=True),
        lax.psum_scatter(norm_grads, "blk", scatter_dimension=0, tiled=True),
    )
    totals = (
        lax.all_gather(summed_parts[0].astype(jnp.bfloat16), "blk", axis=0, tiled=True).astype(
            jnp.float32
        ),
        lax.all_gather(summed_parts[1].astype(jnp.bfloat16), "blk", axis=0, tiled=True).astype(
            jnp.float32
        ),
        lax.all_gather(summed_parts[2].astype(jnp.bfloat16), "blk", axis=0, tiled=True).astype(
            jnp.float32
        ),
        lax.all_gather(summed_parts[3].astype(jnp.bfloat16), "blk", axis=0, tiled=True).astype(
            jnp.float32
        ),
        lax.all_gather(summed_parts[4].astype(jnp.bfloat16), "blk", axis=0, tiled=True).astype(
            jnp.float32
        ),
        lax.all_gather(summed_parts[5].astype(jnp.bfloat16), "blk", axis=0, tiled=True).astype(
            jnp.float32
        ),
        lax.all_gather(summed_parts[6].astype(jnp.bfloat16), "blk", axis=0, tiled=True).astype(
            jnp.float32
        ),
    )
    return (
        layer_out,
        input_grad,
        totals[6][:, 0],
        totals[6][:, 1],
        totals[6][:, 2],
        totals[6][:, 3],
        totals[0],
        totals[1],
        totals[2],
        totals[3],
        totals[4],
        totals[5],
    )


HINT = pl.CostEstimate(flops=1, bytes_accessed=1, transcendentals=1)
NEAR = pl.BlockSpec(memory_space=pltpu.VMEM)
FAR = pl.BlockSpec(memory_space=pltpu.HBM)
SCALAR = pl.BlockSpec(memory_space=pltpu.SMEM)
QT = 256
KT = 512
FT = 256
TT = 1024


def near(*arrays):
    return [pltpu.with_memory_space_constraint(array, pltpu.VMEM) for array in arrays]


def room(mib):
    return pltpu.CompilerParams(vmem_limit_bytes=mib << 20)


def full(shape):
    return pl.BlockSpec(shape, lambda *_: (0,) * len(shape))


def borders_of(len_ref):
    borders = [len_ref[0]]
    for s in range(1, len_ref.shape[0] - 1):
        borders.append(borders[-1] + len_ref[s])
    return borders


def scenes(positions, borders):
    scene = jnp.zeros_like(positions)
    for border in borders:
        scene += (positions >= border).astype(jnp.int32)
    return scene


def tiles_of(first, last, borders, total):
    low, high = 0, total
    for border in borders:
        low = jnp.where(border <= first, border, low)
    for border in reversed(borders):
        high = jnp.where(border > last, border, high)
    return lax.div(low, KT), lax.div(high + KT - 1, KT)


def project_kernel(flip, ids_ref, mine_ref, other_ref, gain_ref, bias_ref, k_ref, v_ref, t_ref, n_ref, *rest):
    h_out, k_out, v_out, t_out, n_out, h_s = rest[-6:]
    n, half, width = mine_ref.shape
    rows = 2 * half
    first = ids_ref[1] == 0

    def norm(b, carry):
        mine, other = mine_ref[b], other_ref[b]
        block = jnp.concatenate([jnp.where(first, mine, other), jnp.where(first, other, mine)], axis=0)
        h_s[b] = layer_norm(block.astype(f32), gain_ref[...], bias_ref[...]).astype(bf16)
        return carry

    lax.fori_loop(0, n, norm, 0)
    h = h_s[...].reshape(n * rows, width)
    keys = jnp.dot(h, k_ref[...], preferred_element_type=f32).astype(bf16)
    values = jnp.dot(h, v_ref[...], preferred_element_type=f32).astype(bf16)
    across = lax.dot_general(t_ref[...], h, LAST, preferred_element_type=f32).astype(bf16)
    down = jnp.dot(h, n_ref[...], preferred_element_type=f32).astype(bf16)
    for s in range(n):
        at = ((ids_ref[0] - 4 * s) & 15) ^ flip
        tokens = slice(s * rows, (s + 1) * rows)
        h_out[at] = h[tokens]
        k_out[at] = keys[tokens]
        v_out[at] = values[tokens]
        t_out[at] = across[:, tokens]
        n_out[at] = down[tokens]


def project_blocks(flip, ids, mine, other, params, count, held):
    half, width = mine.shape[1:]
    _, _, key_weight, value_weight, head_t, head_n = params
    shapes = [
        (2 * half, width),
        (2 * half, key_weight.shape[1]),
        (2 * half, value_weight.shape[1]),
        (head_t.shape[0], 2 * half),
        (2 * half, head_n.shape[1]),
    ]
    return pl.pallas_call(
        lambda *refs: project_kernel(flip, *refs),
        in_specs=[SCALAR] + [NEAR] * (8 + len(held)),
        out_specs=[NEAR] * 5,
        out_shape=[pltpu.VMEM((count,) + shape, bf16) for shape in shapes],
        scratch_shapes=[pltpu.VMEM((mine.shape[0], 2 * half, width), bf16)],
        input_output_aliases={9 + i: i for i in range(5)} if held else {},
        compiler_params=room(16),
        cost_estimate=HINT,
        name="project_blocks",
    )(ids, *near(mine, other, *params, *held))


def attend_kernel(ids_ref, len_ref, h_ref, k_ref, v_ref, q_ref, o_ref, out_ref, branch_ref, query_s):
    rows, width = out_ref.shape
    total = k_ref.shape[0]
    pair = 2 * HEAD
    borders = borders_of(len_ref)
    mine = scenes(lax.broadcasted_iota(jnp.int32, (rows, 1), 0) + ids_ref[0] * rows, borders)
    mask = mine == scenes(lax.broadcasted_iota(jnp.int32, (1, total), 1), borders)
    query = jnp.dot(h_ref[ids_ref[0]], q_ref[...], preferred_element_type=f32).astype(bf16)
    query = query * jnp.asarray(HEAD ** (-0.5), bf16)
    lane = lax.broadcasted_iota(jnp.int32, (rows, pair), 1) // HEAD
    query_s[...] = query

    def attend_pair(g, carry):
        lanes = pl.ds(pl.multiple_of(g * pair, pair), pair)
        keys, values, queries = k_ref[:, lanes], v_ref[:, lanes], query_s[:, lanes]
        parts = []
        for head in range(2):
            q = jnp.where(lane == head, queries, jnp.zeros_like(queries))
            s = lax.dot_general(q, keys, LAST, preferred_element_type=f32)
            s = jnp.where(mask, s, NEG)
            p = jnp.exp(s - jnp.max(s, axis=1, keepdims=True))
            weight = jnp.sum(p, axis=1, keepdims=True)
            parts.append(jnp.dot(p.astype(bf16), values, preferred_element_type=f32) / weight)
        out_ref[:, lanes] = jnp.where(lane == 0, parts[0], parts[1]).astype(bf16)
        return carry

    lax.fori_loop(0, width // pair, attend_pair, 0)
    branch = lax.dot_general(out_ref[...], o_ref[...], LAST, preferred_element_type=f32)
    branch_ref[...] = branch.astype(bf16)


def attend(ids, scene_len, h, k, v, query_weight, output_weight):
    rows = h.shape[1]
    return pl.pallas_call(
        attend_kernel,
        in_specs=[SCALAR] * 2 + [NEAR] * 5,
        out_specs=[NEAR] * 2,
        out_shape=[
            jax.ShapeDtypeStruct((rows, query_weight.shape[1]), bf16),
            jax.ShapeDtypeStruct((rows, output_weight.shape[0]), bf16),
        ],
        scratch_shapes=[pltpu.VMEM((rows, query_weight.shape[1]), bf16)],
        compiler_params=room(16),
        cost_estimate=HINT,
        name="attend",
    )(ids, scene_len, *near(h, k, v, query_weight, output_weight))


def gelu_both(pre, grad):
    half = 0.5 * (1.0 + lax.erf(pre * 0.7071067811865476))
    slope = half + pre * (jnp.exp(-0.5 * pre * pre) * 0.3989422804014327)
    return (pre * half).astype(bf16), (grad * slope).astype(bf16)


def own_kernel(h_ref, g_ref, up_ref, down_ref, feed_out, grad_out, feed_s, grad_s):
    step = pl.program_id(0)
    pre = jnp.dot(h_ref[...], up_ref[...], preferred_element_type=f32)
    grad = jnp.dot(g_ref[...], down_ref[...], preferred_element_type=f32)
    act, grad_pre = gelu_both(pre, grad)
    feed = lax.dot_general(act, down_ref[...], LAST, preferred_element_type=f32)
    grad_two = lax.dot_general(grad_pre, up_ref[...], LAST, preferred_element_type=f32)

    @pl.when(step == 0)
    def _():
        feed_s[...] = feed
        grad_s[...] = grad_two

    @pl.when(step > 0)
    def _():
        feed_s[...] += feed
        grad_s[...] += grad_two

    @pl.when(step == pl.num_programs(0) - 1)
    def _():
        feed_out[...] = feed_s[...].astype(bf16)
        grad_out[...] = grad_s[...].astype(bf16)


def own_ffn(h, g, up_weight, down_weight):
    width = h.shape[1]
    hidden = up_weight.shape[1]
    tile = 512
    return pl.pallas_call(
        own_kernel,
        grid=(hidden // tile,),
        in_specs=[NEAR, NEAR] + [pl.BlockSpec((width, tile), lambda i: (0, i))] * 2,
        out_specs=[NEAR] * 2,
        out_shape=[jax.ShapeDtypeStruct(h.shape, bf16)] * 2,
        scratch_shapes=[pltpu.VMEM(h.shape, f32)] * 2,
        cost_estimate=HINT,
        name="own_ffn",
    )(*near(h, g), up_weight, down_weight)


def norm_back_kernel(x_ref, mine_ref, other_ref, gain_ref, g_ref, o_ref, grad_out, low_out, sums_out, heads_out):
    x = x_ref[...]
    center = x - jnp.mean(x, axis=1, keepdims=True)
    scale = lax.rsqrt(jnp.mean(center * center, axis=1, keepdims=True) + 1e-05)
    normed = center * scale
    grad = mine_ref[...].astype(f32) + other_ref[...].astype(f32)
    sums_out[0:1, :] = jnp.sum(grad * normed, axis=0, keepdims=True)
    sums_out[1:2, :] = jnp.sum(grad, axis=0, keepdims=True)
    grad = grad * gain_ref[...]
    inner = jnp.mean(grad * normed, axis=1, keepdims=True)
    grad = scale * (grad - jnp.mean(grad, axis=1, keepdims=True) - normed * inner)
    grad = grad + g_ref[...].astype(f32)
    grad_out[...] = grad
    low = grad.astype(bf16)
    low_out[...] = low
    attended = jnp.dot(low, o_ref[...], preferred_element_type=f32)
    across = attended.T.astype(bf16)
    for head in range(heads_out.shape[0]):
        heads_out[head] = across[head * HEAD : (head + 1) * HEAD, :]


def norm_back(x, mine, other, gain, g, output_weight):
    rows, width = x.shape
    return pl.pallas_call(
        norm_back_kernel,
        in_specs=[NEAR] * 6,
        out_specs=[NEAR] * 4,
        out_shape=[
            jax.ShapeDtypeStruct((rows, width), f32),
            jax.ShapeDtypeStruct((rows, width), bf16),
            jax.ShapeDtypeStruct((2, width), f32),
            jax.ShapeDtypeStruct((output_weight.shape[1] // HEAD, HEAD, rows), bf16),
        ],
        compiler_params=room(16),
        cost_estimate=HINT,
        name="norm_back",
    )(*near(x, mine, other, gain.reshape(1, width), g, output_weight))


def prepare_kernel(ids_ref, len_ref, t_ref, n_ref, p_ref, s_s):
    step = pl.program_id(0)
    count, _, rows = t_ref.shape
    borders = borders_of(len_ref)
    blocks = [4 * step + 2 * i + (ids_ref[0] & 1) for i in range(2)]
    lo, hi = tiles_of(blocks[0] * rows, blocks[1] * rows + rows - 1, borders, count * rows)
    q = jnp.concatenate([t_ref[b, 0:HEAD, :] for b in blocks], axis=1)
    q = jnp.concatenate([q, jnp.zeros_like(q)], axis=0)
    places = lax.broadcasted_iota(jnp.int32, (1, rows), 1)
    row = scenes(jnp.concatenate([places + b * rows for b in blocks], axis=1), borders)

    def score(j, top):
        keys = pl.ds(pl.multiple_of(j * KT, KT), KT)
        s = jnp.dot(n_ref[keys, 0 : 2 * HEAD], q, preferred_element_type=f32)
        col = scenes(lax.broadcasted_iota(jnp.int32, (KT, 1), 0) + j * KT, borders)
        s = jnp.where(col == row, s, NEG)
        s_s[keys, :] = s
        return jnp.maximum(top, jnp.max(s, axis=0, keepdims=True))

    top = lax.fori_loop(lo, hi, score, jnp.full((1, QT), NEG, f32))

    def weigh(j, total):
        keys = pl.ds(pl.multiple_of(j * KT, KT), KT)
        p = jnp.exp(s_s[keys, :] - top)
        s_s[keys, :] = p
        return total + jnp.sum(p, axis=0, keepdims=True)

    total = lax.fori_loop(lo, hi, weigh, jnp.zeros((1, QT), f32))
    share = 1.0 / total

    def store(j, carry):
        keys = pl.ds(pl.multiple_of(j * KT, KT), KT)
        p_ref[0, keys, :] = (s_s[keys, :] * share).astype(bf16)
        return carry

    lax.fori_loop(lo, hi, store, 0)


def prepare(ids, scene_len, head_t, head_n):
    count, _, rows = head_t.shape
    total = count * rows
    tiles = total // 2 // QT
    return pl.pallas_call(
        prepare_kernel,
        grid_spec=pltpu.PrefetchScalarGridSpec(
            num_scalar_prefetch=2,
            grid=(tiles,),
            in_specs=[full(head_t.shape), full((total, 4 * HEAD))],
            out_specs=pl.BlockSpec((1, total, QT), lambda i, *_: (i, 0, 0)),
            scratch_shapes=[pltpu.VMEM((total, QT), f32)],
        ),
        out_shape=jax.ShapeDtypeStruct((tiles, total, QT), bf16),
        cost_estimate=HINT,
        name="prepare",
    )(ids, scene_len, head_t, head_n.reshape(total, 4 * HEAD))


def back_kernel(
    ids_ref, len_ref, p_ref, ga_ref, t_ref, n_ref, h_far,
    gq_out, mine_out, other_out, slice_mine, slice_other, dp_s, gkv_s, g_s, h_ref, sem,
):
    step = pl.program_id(0)
    part = ids_ref[0] & 1
    count, _, rows = t_ref.shape
    blocks = [4 * step + 2 * i + part for i in range(2)]
    lo, hi = tiles_of(blocks[0] * rows, blocks[1] * rows + rows - 1, borders_of(len_ref), count * rows)
    load = pltpu.make_async_copy(h_far, h_ref, sem)

    @pl.when(step == 0)
    def _():
        load.start()
        gkv_s[...] = jnp.zeros_like(gkv_s)
        g_s[...] = jnp.zeros_like(g_s)

    spans = [pl.ds(pl.multiple_of(b * rows, rows), rows) for b in blocks]
    ga_t = jnp.concatenate([ga_ref[0], ga_ref[1]], axis=1)
    ga_t = jnp.concatenate([ga_t, jnp.zeros_like(ga_t)], axis=0)
    ga = ga_t.T
    kq = jnp.concatenate([n_ref[span, 0 : 2 * HEAD] for span in spans], axis=0)
    q = jnp.where(lax.broadcasted_iota(jnp.int32, kq.shape, 1) >= HEAD, kq, jnp.zeros_like(kq))

    def first(j, delta):
        keys = pl.ds(pl.multiple_of(j * KT, KT), KT)
        p = p_ref[0, keys, :]
        dp = jnp.dot(n_ref[keys, 2 * HEAD :], ga_t, preferred_element_type=f32)
        dp_s[keys, :] = dp
        gkv_s[keys, :] += jnp.dot(p, ga, preferred_element_type=f32)
        return delta + jnp.sum(p.astype(f32) * dp, axis=0, keepdims=True)

    delta = lax.fori_loop(lo, hi, first, jnp.zeros((1, QT), f32))

    def second(j, gq):
        keys = pl.ds(pl.multiple_of(j * KT, KT), KT)
        ds = (p_ref[0, keys, :].astype(f32) * (dp_s[keys, :] - delta)).astype(bf16)
        gkv_s[keys, :] += jnp.dot(ds, q, preferred_element_type=f32)
        some = KT // rows
        k_t = jnp.concatenate([t_ref[j * some + i, HEAD : 2 * HEAD, :] for i in range(some)], axis=1)
        return gq + jnp.dot(k_t, ds, preferred_element_type=f32)

    gq = lax.fori_loop(lo, hi, second, jnp.zeros((HEAD, QT), f32))
    gq = (gq * HEAD ** (-0.5)).astype(bf16)
    for i in range(2):
        tile = gq[:, i * rows : (i + 1) * rows]
        gq_out[2 * step + i] = tile
        g_s[0:HEAD, spans[i]] = tile

    @pl.when(step == pl.num_programs(0) - 1)
    def _():
        for m in range(count // 2):
            for out, b in ((mine_out, 2 * m + part), (other_out, 2 * m + 1 - part)):
                tokens = pl.ds(pl.multiple_of(b * rows, rows), rows)
                both = gkv_s[tokens, :].T
                out[m] = both.astype(out.dtype)
                g_s[HEAD:, tokens] = both.astype(bf16)
        load.wait()
        slices = jnp.dot(g_s[...], h_ref[...], preferred_element_type=f32)
        wide = slice_mine.shape[1]
        left, right = slices[:, :wide], slices[:, wide:]
        slice_mine[...] = jnp.where(part == 0, left, right)
        slice_other[...] = jnp.where(part == 0, right, left).astype(bf16)


def back(ids, scene_len, p, ga, head_t, head_n, h1):
    count, three, rows = head_t.shape
    width = h1.shape[-1]
    total = count * rows
    half = count // 2
    kept = [
        ((half, HEAD, rows), bf16),
        ((half, 2 * HEAD, rows), f32),
        ((half, 2 * HEAD, rows), bf16),
        ((three, width // 2), f32),
        ((three, width // 2), bf16),
    ]
    return pl.pallas_call(
        back_kernel,
        grid_spec=pltpu.PrefetchScalarGridSpec(
            num_scalar_prefetch=2,
            grid=(p.shape[0],),
            in_specs=[
                pl.BlockSpec((1, total, QT), lambda i, *_: (i, 0, 0)),
                pl.BlockSpec((2, HEAD, rows), lambda i, *_: (i, 0, 0)),
                full(head_t.shape),
                full((total, 4 * HEAD)),
                FAR,
            ],
            out_specs=[NEAR] * 5,
            scratch_shapes=[
                pltpu.VMEM((total, QT), f32),
                pltpu.VMEM((total, 2 * HEAD), f32),
                pltpu.VMEM((three, total), bf16),
                pltpu.VMEM((total, width), bf16),
                pltpu.SemaphoreType.DMA,
            ],
        ),
        out_shape=[jax.ShapeDtypeStruct(shape, kind) for shape, kind in kept],
        cost_estimate=HINT,
        name="back",
    )(ids, scene_len, p, ga, head_t, head_n.reshape(total, 4 * HEAD), h1.reshape(total, width))


def share_kernel(ids_ref, low_ref, attended_ref, mine_out, other_out):
    part = ids_ref[0] & 1
    whole = lax.dot_general(low_ref[...], attended_ref[...], FIRST, preferred_element_type=f32)
    whole = whole.reshape(mine_out.shape[0], 2, mine_out.shape[1], mine_out.shape[2])
    mine_out[...] = jnp.where(part == 0, whole[:, 0], whole[:, 1])
    other_out[...] = jnp.where(part == 0, whole[:, 1], whole[:, 0]).astype(bf16)


def share_output(ids, low, attended, count):
    shape = (count // 2, low.shape[1] // count, attended.shape[1])
    return pl.pallas_call(
        share_kernel,
        in_specs=[SCALAR, NEAR, NEAR],
        out_specs=[NEAR] * 2,
        out_shape=[jax.ShapeDtypeStruct(shape, f32), jax.ShapeDtypeStruct(shape, bf16)],
        compiler_params=room(16),
        cost_estimate=HINT,
        name="share_output",
    )(ids, *near(low, attended))


def merge_kernel(gq_ref, kept_ref, given_ref, out_ref):
    out_ref[:, 0:HEAD, :] = gq_ref[...]
    out_ref[:, HEAD:, :] = (kept_ref[...] + given_ref[...].astype(f32)).astype(bf16)


def merge(gq, kept, given):
    half, _, rows = gq.shape
    return pl.pallas_call(
        merge_kernel,
        in_specs=[NEAR] * 3,
        out_specs=NEAR,
        out_shape=jax.ShapeDtypeStruct((half, 3 * HEAD, rows), bf16),
        compiler_params=room(8),
        cost_estimate=HINT,
        name="merge",
    )(*near(gq, kept, given))


def unit_kernel(mine_ref, other_ref, parts_ref, out_ref):
    rows = mine_ref.shape[0]
    out_ref[0:rows, :] = (mine_ref[...] + other_ref[...].astype(f32)).astype(bf16)
    out_ref[rows:, :] = jnp.sum(parts_ref[...].astype(f32), axis=0).astype(bf16)


def make_unit(mine, other, parts):
    rows, wide = mine.shape
    return pl.pallas_call(
        unit_kernel,
        in_specs=[NEAR] * 3,
        out_specs=NEAR,
        out_shape=jax.ShapeDtypeStruct((rows + parts.shape[1], wide), bf16),
        compiler_params=room(8),
        cost_estimate=HINT,
        name="make_unit",
    )(mine, other, parts)


def home_kernel(home_ref, q_ref, v_ref, k_ref, grad_out):
    rows = home_ref.shape[2]
    grad = 0.0
    for i, weight in enumerate((q_ref, v_ref, k_ref)):
        across = home_ref[:, i * HEAD : (i + 1) * HEAD, :].reshape(-1, rows)
        grad = grad + lax.dot_general(across.T, weight[...], LAST, preferred_element_type=f32)
    grad_out[...] = grad.astype(bf16)


def go_home(home, weights):
    return pl.pallas_call(
        home_kernel,
        in_specs=[NEAR] * 4,
        out_specs=NEAR,
        out_shape=jax.ShapeDtypeStruct((home.shape[2], weights[0].shape[0]), bf16),
        cost_estimate=HINT,
        name="go_home",
    )(home, *weights)


def input_back_kernel(x_ref, mine_ref, other_ref, gain_ref, grad_ref, sums_ref, grad_out, sums_out):
    x = x_ref[...].astype(f32)
    center = x - jnp.mean(x, axis=1, keepdims=True)
    scale = lax.rsqrt(jnp.mean(center * center, axis=1, keepdims=True) + 1e-05)
    normed = center * scale
    grad = mine_ref[...].astype(f32) + other_ref[...].astype(f32)
    sums = [jnp.sum(grad * normed, axis=0, keepdims=True), jnp.sum(grad, axis=0, keepdims=True), sums_ref[...]]
    sums = jnp.concatenate(sums, axis=0)
    for b in range(sums_out.shape[0]):
        sums_out[b] = sums
    grad = grad * gain_ref[...]
    inner = jnp.mean(grad * normed, axis=1, keepdims=True)
    grad_out[...] = grad_ref[...] + scale * (grad - jnp.mean(grad, axis=1, keepdims=True) - normed * inner)


def input_back(x, mine, other, gain, grad_middle, sums, count):
    rows, width = x.shape
    return pl.pallas_call(
        input_back_kernel,
        in_specs=[NEAR] * 6,
        out_specs=[NEAR] * 2,
        out_shape=[
            jax.ShapeDtypeStruct((rows, width), f32),
            jax.ShapeDtypeStruct((count, 4, width), f32),
        ],
        compiler_params=room(16),
        cost_estimate=HINT,
        name="input_back",
    )(x, mine, other, gain.reshape(1, width), grad_middle, sums)


def through_kernel(g_ref, down_ref, out_ref):
    out_ref[...] = jnp.dot(g_ref[...], down_ref[...], preferred_element_type=f32).astype(bf16)


def through(g, weight):
    total, width = g.shape
    hidden = weight.shape[1]
    tile = 2 * FT
    return pl.pallas_call(
        through_kernel,
        grid=(hidden // tile,),
        in_specs=[
            pl.BlockSpec((total, width), lambda i: (0, 0), pipeline_mode=pl.Buffered(1)),
            pl.BlockSpec((width, tile), lambda i: (0, i)),
        ],
        out_specs=pl.BlockSpec((total, tile), lambda i: (0, i)),
        out_shape=jax.ShapeDtypeStruct((total, hidden), bf16),
        cost_estimate=pl.CostEstimate(
            flops=2 * total * width * hidden, bytes_accessed=8 * total * width, transcendentals=0
        ),
        name="through",
    )(g, weight)


def ffn_kernel(h_ref, g_ref, grad_ref, up_ref, *outs):
    up_out, down_out = outs[-2:]
    steps = h_ref.shape[0] // TT

    def product(j):
        return jnp.dot(h_ref[j * TT : (j + 1) * TT, :], up_ref[...], preferred_element_type=f32)

    pre = product(0)
    for j in range(steps):
        later = product(j + 1) if j + 1 < steps else None
        span = slice(j * TT, (j + 1) * TT)
        act, grad_pre = gelu_both(pre, grad_ref[span, :].astype(f32))
        up = lax.dot_general(h_ref[span, :], grad_pre, FIRST, preferred_element_type=f32)
        down = lax.dot_general(g_ref[span, :], act, FIRST, preferred_element_type=f32)
        if j == 0:
            up_out[...] = up
            down_out[...] = down
        else:
            up_out[...] += up
            down_out[...] += down
        pre = later


def ffn_grads(h, g, grad, up_weight, tiles, held):
    total, width = h.shape
    hidden = up_weight.shape[1]
    first, last = tiles
    tokens = pl.BlockSpec((total, width), lambda i: (0, 0), pipeline_mode=pl.Buffered(1))
    units = pl.BlockSpec((width, FT), lambda i: (0, first + i))
    return pl.pallas_call(
        ffn_kernel,
        grid=(last - first,),
        in_specs=[tokens, tokens, pl.BlockSpec((total, FT), lambda i: (0, first + i)), units] + [FAR] * len(held),
        out_specs=[units] * 2,
        out_shape=[jax.ShapeDtypeStruct((width, hidden), f32)] * 2,
        input_output_aliases={4: 0, 5: 1} if held else {},
        cost_estimate=pl.CostEstimate(
            flops=6 * total * width * FT * (last - first), bytes_accessed=4 * total * width, transcendentals=0
        ),
        name="ffn_grads",
    )(h, g, grad, up_weight, *held)


def finish_kernel(ids_ref, *refs):
    pieces, outs = refs[:5], refs[5:]
    row, part = (ids_ref[0] >> 1) & 1, ids_ref[0] & 1
    wide = pieces[0].shape[2]
    early = pl.program_id(0) < 2

    def rows_of(k, span):
        if k < 3:
            return pieces[k][0, span, :]
        return jnp.where(early, pieces[3][0, span, :], pieces[4][0, span, :])

    for k, x in ((0, part), (1, 1 - part)):
        rows = pl.ds(pl.multiple_of(x * wide, wide), wide)
        for i in range(3):
            span = slice(i * HEAD, (i + 1) * HEAD)
            this, that = rows_of(k, span), rows_of(k + 2, span)
            pair = [jnp.where(row == 0, this, that), jnp.where(row == 0, that, this)]
            outs[i][rows, :] = jnp.concatenate(pair, axis=0).T.astype(f32)
    slots = pieces[0].shape[1] - 3 * HEAD
    for k in range(4):
        at = pl.multiple_of(((ids_ref[0] & 3) ^ k) * slots, slots)
        outs[3][pl.ds(at, slots), :] = rows_of(k, slice(3 * HEAD, None)).astype(f32)


def finish(ids, pieces, width, columns):
    def plane(s, ids):
        return ((ids[0] - 4 * s) & 15) >> 2

    shape = (1,) + pieces[0].shape[1:]
    whole = pl.BlockSpec(shape, lambda s, ids: (s, 0, 0))
    early = pl.BlockSpec(shape, lambda s, ids: (jnp.minimum(s, 1), 0, 0))
    late = pl.BlockSpec(shape, lambda s, ids: (jnp.maximum(s - 2, 0), 0, 0))
    across = pl.BlockSpec((width, columns // 4), lambda s, ids: (0, plane(s, ids)))
    down = pl.BlockSpec((width // 4, columns), lambda s, ids: (plane(s, ids), 0))
    return pl.pallas_call(
        finish_kernel,
        grid_spec=pltpu.PrefetchScalarGridSpec(
            num_scalar_prefetch=1,
            grid=(4,),
            in_specs=[whole, whole, whole, early, late],
            out_specs=[across] * 3 + [down],
        ),
        out_shape=[jax.ShapeDtypeStruct((width, columns), f32)] * 4,
        cost_estimate=HINT,
        name="finish",
    )(ids, *pieces)


def shuffle(block, target):
    return lax.ppermute(block, "blk", [(i, target(i)) for i in range(16)])


def over_core(block):
    return lax.ppermute(block, "tp", [(0, 1), (1, 0)])


def send_column(unit):
    return (unit,) + tuple(shuffle(unit, lambda i, s=s: (i + 4 * s) % 16) for s in (1, 2, 3))


def stack_column(parts, *first):
    return jnp.stack(lax.optimization_barrier(parts + first)[:4])


def gather_sides(column):
    return shuffle(column, lambda i: i ^ 1), shuffle(column, lambda i: i ^ 2)


def after(value, *first):
    return lax.optimization_barrier((value,) + first)[0]


def fast_body(
    tokens,
    first_gain,
    first_bias,
    second_gain,
    second_bias,
    query_weight,
    key_weight,
    value_weight,
    output_weight,
    up_weight,
    down_weight,
    cotangent,
    scene_len,
):
    count = lax.axis_size("blk")
    place = lax.axis_index("blk")
    side = lax.axis_index("tp")
    rows, width = tokens.shape
    columns = query_weight.shape[1]
    heads_here = columns // HEAD
    share = count // heads_here
    scale = HEAD ** (-0.5)
    ids = jnp.stack([place, side])
    half_at = side.astype(jnp.uint32) * jnp.uint32(rows // 2)
    head_at = (place.astype(jnp.uint32) >> 1) * jnp.uint32(HEAD)
    alike = [list(range(r, count, share)) for r in range(share)]

    def half_of(block):
        return lax.dynamic_slice(block, (half_at, jnp.uint32(0)), (rows // 2, width))

    def head_of(weight):
        return lax.dynamic_slice(weight, (jnp.uint32(0), head_at), (width, HEAD))

    g_all = lax.all_gather(half_of(cotangent), ("blk", "tp"), axis=0, tiled=True)
    column = jnp.stack(send_column(half_of(tokens)))

    head_query = head_of(query_weight) * jnp.asarray(scale, bf16)
    head_key, head_value = head_of(key_weight), head_of(value_weight)
    head_t = jnp.concatenate([head_query, head_key, head_value], axis=1).T
    head_n = jnp.concatenate([head_key, head_query, head_value, jnp.zeros_like(head_value)], axis=1)
    params = (first_gain.reshape(1, -1), first_bias.reshape(1, -1), key_weight, value_weight, head_t, head_n)

    across_x = shuffle(column, lambda i: i ^ 1)
    across_y = shuffle(column, lambda i: i ^ 2)
    made = project_blocks(0, ids, column, over_core(column), params, count, ())
    across_y = after(across_y, made[0])
    diagonal = shuffle(across_y, lambda i: i ^ 1)
    for flip, piece in ((1, after(across_x, across_y)), (2, across_y), (3, diagonal)):
        piece = after(piece, made[0]) if piece is diagonal else piece
        made = project_blocks(flip, ids, piece, over_core(piece), params, count, made)
    h1_all, keys, values, head_t, head_n = made

    attended, branch = attend(
        ids, scene_len, h1_all, keys.reshape(-1, columns), values.reshape(-1, columns), query_weight, output_weight
    )
    inputs = tokens.astype(f32)
    middle = inputs + (branch.astype(f32) + over_core(branch).astype(f32))
    h2 = layer_norm(middle, second_gain, second_bias).astype(bf16)
    h2_all = lax.all_gather(half_of(h2), ("blk", "tp"), axis=0, tiled=True)

    feed, grad_two = own_ffn(h2, cotangent, up_weight, down_weight)
    grad_middle, grad_middle_low, second_sums, to_heads = norm_back(
        middle, grad_two, over_core(grad_two), second_gain, cotangent, output_weight
    )
    ga = lax.all_to_all(to_heads, "blk", 0, 0, tiled=True, axis_index_groups=alike)
    output_kept, output_given = share_output(ids, after(grad_middle_low, to_heads), attended, count)
    output_other = shuffle(output_given, lambda i: i ^ 1)
    p = prepare(ids, scene_len, after(head_t, to_heads, g_all, output_given), head_n)
    output_kept, output_other, _ = lax.optimization_barrier((output_kept, output_other, p))
    output_half = (output_kept + output_other.astype(f32)).astype(bf16)
    output_parts = lax.all_to_all(after(output_half, ga, p), "blk", 0, 0, tiled=True, axis_index_groups=alike)
    grad_q, kept, given, slice_kept, slice_given = back(ids, scene_len, p, ga, head_t, head_n, h1_all)

    grad_all = through(after(g_all, grad_q), down_weight)
    slice_other = shuffle(slice_given, lambda i: i ^ 1)
    unit = make_unit(after(slice_kept, grad_all), slice_other, output_parts)
    parts = send_column(unit)
    given = shuffle(after(given, unit), lambda i: i ^ 1)
    feed = after(feed, unit)
    layer_out = (middle + (feed.astype(f32) + over_core(feed).astype(f32))).astype(bf16)
    parcel = merge(after(grad_q, unit), kept, given)
    home = lax.all_to_all(parcel, "blk", 0, 0, tiled=True, axis_index_groups=alike)
    held = ffn_grads(after(h2_all, unit, parcel), g_all, grad_all, up_weight, (0, 3), ())
    column = stack_column(parts, held[0], layer_out)
    side_x, side_y = gather_sides(column)
    up_grad, down_grad = ffn_grads(after(h2_all, column), g_all, grad_all, up_weight, (3, 8), held)

    half_x, half_y = lax.optimization_barrier((side_x[2:], side_y[:2], up_grad))[:2]
    across = shuffle(half_y, lambda i: i ^ 1), shuffle(half_x, lambda i: i ^ 2)
    home = after(home, up_grad).reshape(heads_here, 3 * HEAD, rows)
    home = after(home, half_x, half_y)
    grad_one = go_home(home, (query_weight, value_weight, key_weight))
    input_grad, norm_part = input_back(
        tokens, grad_one, over_core(grad_one), first_gain, grad_middle, second_sums, count
    )
    norm_parts = lax.all_to_all(norm_part, "blk", 0, 0, tiled=True)
    heads = (after(column, norm_part), side_x, side_y) + across
    query_grad, value_grad, key_grad, output_grad = finish(ids, heads, width, columns)
    norm_sums = jnp.sum(after(norm_parts, output_grad), axis=0)
    return (
        layer_out,
        input_grad,
        norm_sums[0],
        norm_sums[1],
        norm_sums[2],
        norm_sums[3],
        query_grad,
        key_grad,
        value_grad,
        output_grad,
        up_grad,
        down_grad,
    )


def solution(mesh):
    body = fast_body if mesh.shape["blk"] == 16 else ring_body
    return jax.shard_map(
        body,
        mesh=mesh,
        in_specs=(
            P("blk", None),
            P(),
            P(),
            P(),
            P(),
            P(None, "tp"),
            P(None, "tp"),
            P(None, "tp"),
            P(None, "tp"),
            P(None, "tp"),
            P(None, "tp"),
            P("blk", None),
            P(),
        ),
        out_specs=(
            P("blk", None),
            P("blk", None),
            P(),
            P(),
            P(),
            P(),
            P(None, "tp"),
            P(None, "tp"),
            P(None, "tp"),
            P(None, "tp"),
            P(None, "tp"),
            P(None, "tp"),
        ),
        check_vma=False,
    )
```

```python
import jax
import jax.numpy as jnp
from jax import lax
from jax.experimental import pallas as pl
from jax.experimental.pallas import tpu as pltpu
from jax.sharding import PartitionSpec as P

HEAD = 64
NEG = -1e30
f32 = jnp.float32
bf16 = jnp.bfloat16
LAST = (((1,), (1,)), ((), ()))
FIRST = (((0,), (0,)), ((), ()))


def from_behind(block, axis, distance):
    devices = range(lax.axis_size(axis))
    route = [((i - distance) % len(devices), i) for i in devices]
    return lax.ppermute(block, axis, route)


def layer_norm(values, gain, bias):
    center = values - jnp.mean(values, axis=-1, keepdims=True)
    spread = jnp.mean(center * center, axis=-1, keepdims=True)
    return center * lax.rsqrt(spread + 1e-05) * gain + bias


def move_grads(grad_keys, grad_values, offset):
    return (
        from_behind(grad_keys.astype(jnp.bfloat16), "blk", offset).astype(grad_keys.dtype),
        from_behind(grad_values.astype(jnp.bfloat16), "blk", offset).astype(grad_values.dtype),
    )


def ring_body(
    tokens,
    first_gain,
    first_bias,
    second_gain,
    second_bias,
    query_weight,
    key_weight,
    value_weight,
    output_weight,
    up_weight,
    down_weight,
    cotangent,
    scene_len,
):
    count = lax.axis_size("blk")
    place = lax.axis_index("blk")
    rows = tokens.shape[0]
    heads_here = query_weight.shape[1] // HEAD
    scale = HEAD ** (-0.5)
    ends = jnp.cumsum(scene_len)
    contract_last = (((1,), (1,)), ((), ()))
    contract_first = (((0,), (0,)), ((), ()))

    def scene_of(source):
        places = source * rows + jnp.arange(rows, dtype=jnp.int32)
        return jnp.sum((places[:, None] >= ends[None, :]).astype(jnp.int32), axis=1)

    mine = scene_of(place)

    def shares(source):
        other = scene_of(source)
        return jnp.maximum(mine[0], other[0]) <= jnp.minimum(mine[-1], other[-1])

    directions = (1,)
    steps = count - 1

    def source_of(way, turn):
        raw_source = place - way * turn
        return (raw_source % count, jnp.array(True))

    inputs = tokens.astype(f32)
    normed_one = layer_norm(inputs, first_gain, first_bias).astype(bf16)

    def project(weight):
        return jnp.dot(normed_one, weight, preferred_element_type=f32).astype(bf16)

    query = project(query_weight).reshape(rows, heads_here, HEAD)
    keys = project(key_weight).reshape(rows, heads_here, HEAD)
    values = project(value_weight).reshape(rows, heads_here, HEAD)

    def scores_of(key_block, source):
        mask = mine[:, None] == scene_of(source)[None, :]
        scores = jnp.einsum("qhd,khd->hqk", query, key_block, preferred_element_type=f32) * scale
        return (jnp.where(mask[None], scores, -1e30), mask)

    def absorb(state, key_block, value_block, source):
        top, total, summed = state
        scores, mask = scores_of(key_block, source)
        new_top = jnp.maximum(top, jnp.max(scores, axis=2))
        factor = jnp.exp(top - new_top)
        weights = jnp.where(mask[None], jnp.exp(scores - new_top[:, :, None]), 0.0)
        total = total * factor + jnp.sum(weights, axis=2)
        summed = summed * factor.T[:, :, None] + jnp.einsum(
            "hqk,khd->qhd", weights.astype(bf16), value_block, preferred_element_type=f32
        )
        return (new_top, total, summed)

    start = (
        jnp.full((heads_here, rows), -1e30, f32),
        jnp.zeros((heads_here, rows), f32),
        jnp.zeros((rows, heads_here, HEAD), f32),
    )
    state = absorb(start, keys, values, place)
    way = directions[0]

    def turn_forward(turn, carry):
        current, key_block, value_block = carry
        key_block, value_block = from_behind((key_block, value_block), "blk", way)
        source, inside = source_of(way, turn)
        current = lax.cond(
            inside & shares(source),
            lambda held: absorb(held, key_block, value_block, source),
            lambda held: held,
            current,
        )
        return (current, key_block, value_block)

    state, _, _ = lax.fori_loop(1, steps + 1, turn_forward, (state, keys, values))
    top, total, summed = state
    attended = summed / total.T[:, :, None]
    log_total = top + jnp.log(total)
    attended_low = attended.reshape(rows, -1).astype(bf16)
    branch = lax.dot_general(attended_low, output_weight, contract_last, preferred_element_type=f32)
    branch = lax.psum(branch.astype(jnp.bfloat16), "tp").astype(jnp.float32)
    middle = inputs + branch
    normed_two = layer_norm(middle, second_gain, second_bias).astype(bf16)
    before = jnp.dot(normed_two, up_weight, preferred_element_type=f32)
    active = jax.nn.gelu(before, approximate=False).astype(bf16)
    feed = lax.dot_general(active, down_weight, contract_last, preferred_element_type=f32)
    feed = lax.psum(feed.astype(jnp.bfloat16), "tp").astype(jnp.float32)
    layer_out = (middle + feed).astype(bf16)
    grad_out = cotangent.astype(f32)
    down_grad = lax.dot_general(cotangent, active, contract_first, preferred_element_type=f32)
    grad_active = jnp.dot(cotangent, down_weight, preferred_element_type=f32)
    _, gelu_pull = jax.vjp(lambda arg: jax.nn.gelu(arg, approximate=False), before)
    grad_before = gelu_pull(grad_active)[0].astype(bf16)
    up_grad = lax.dot_general(normed_two, grad_before, contract_first, preferred_element_type=f32)
    grad_two = lax.dot_general(grad_before, up_weight, contract_last, preferred_element_type=f32)
    grad_two = lax.psum(grad_two.astype(jnp.bfloat16), "tp").astype(jnp.float32)
    _, second_pull = jax.vjp(layer_norm, middle, second_gain, second_bias)
    grad_middle_norm, second_gain_grad, second_bias_grad = second_pull(grad_two)
    grad_middle = grad_out + grad_middle_norm
    grad_middle_low = grad_middle.astype(bf16)
    output_grad = lax.dot_general(
        grad_middle_low, attended_low, contract_first, preferred_element_type=f32
    )
    grad_attended = jnp.dot(grad_middle_low, output_weight, preferred_element_type=f32).astype(bf16)
    grad_attended = grad_attended.reshape(rows, heads_here, HEAD)
    delta = jnp.sum(grad_attended * attended, axis=2).T

    def backtrack(grads, key_block, value_block, source):
        grad_query, grad_keys, grad_values = grads
        scores, mask = scores_of(key_block, source)
        probs = jnp.where(mask[None], jnp.exp(scores - log_total[:, :, None]), 0.0)
        grad_values = grad_values + jnp.einsum(
            "hqk,qhd->khd", probs.astype(bf16), grad_attended, preferred_element_type=f32
        )
        grad_probs = jnp.einsum(
            "qhd,khd->hqk", grad_attended, value_block, preferred_element_type=f32
        )
        grad_scores = (probs * (grad_probs - delta[:, :, None]) * scale).astype(bf16)
        grad_query = grad_query + jnp.einsum(
            "hqk,khd->qhd", grad_scores, key_block, preferred_element_type=f32
        )
        grad_keys = grad_keys + jnp.einsum(
            "hqk,qhd->khd", grad_scores, query, preferred_element_type=f32
        )
        return (grad_query, grad_keys, grad_values)

    empty = jnp.zeros((rows, heads_here, HEAD), f32)
    grad_query, home_keys, home_values = backtrack((empty, empty, empty), keys, values, place)
    way = directions[0]

    def turn_backward(turn, carry):
        grad_q, key_block, value_block, grad_k, grad_v = carry
        key_block, value_block = from_behind((key_block, value_block), "blk", way)
        grad_k, grad_v = move_grads(grad_k, grad_v, way)
        source, inside = source_of(way, turn)
        grad_q, grad_k, grad_v = lax.cond(
            inside & shares(source),
            lambda held: backtrack(held, key_block, value_block, source),
            lambda held: held,
            (grad_q, grad_k, grad_v),
        )
        return (grad_q, key_block, value_block, grad_k, grad_v)

    grad_query, _, _, moved_keys, moved_values = lax.fori_loop(
        1, steps + 1, turn_backward, (grad_query, keys, values, empty, empty)
    )
    moved_keys, moved_values = move_grads(moved_keys, moved_values, -way * steps)
    home_keys = home_keys + moved_keys
    home_values = home_values + moved_values
    grad_query = grad_query.reshape(rows, -1).astype(bf16)
    grad_keys = home_keys.reshape(rows, -1).astype(bf16)
    grad_values = home_values.reshape(rows, -1).astype(bf16)
    query_grad = lax.dot_general(normed_one, grad_query, contract_first, preferred_element_type=f32)
    key_grad = lax.dot_general(normed_one, grad_keys, contract_first, preferred_element_type=f32)
    value_grad = lax.dot_general(
        normed_one, grad_values, contract_first, preferred_element_type=f32
    )
    grad_one = lax.dot_general(grad_query, query_weight, contract_last, preferred_element_type=f32)
    grad_one = grad_one + lax.dot_general(
        grad_keys, key_weight, contract_last, preferred_element_type=f32
    )
    grad_one = grad_one + lax.dot_general(
        grad_values, value_weight, contract_last, preferred_element_type=f32
    )
    grad_one = lax.psum(grad_one.astype(jnp.bfloat16), "tp").astype(jnp.float32)
    _, first_pull = jax.vjp(layer_norm, inputs, first_gain, first_bias)
    grad_input_norm, first_gain_grad, first_bias_grad = first_pull(grad_one)
    input_grad = grad_middle + grad_input_norm
    norm_grads = jnp.stack(
        [first_gain_grad, first_bias_grad, second_gain_grad, second_bias_grad], axis=1
    )
    summed_parts = (
        lax.psum_scatter(query_grad, "blk", scatter_dimension=0, tiled=True),
        lax.psum_scatter(key_grad, "blk", scatter_dimension=0, tiled=True),
        lax.psum_scatter(value_grad, "blk", scatter_dimension=0, tiled=True),
        lax.psum_scatter(output_grad, "blk", scatter_dimension=0, tiled=True),
        lax.psum_scatter(up_grad, "blk", scatter_dimension=0, tiled=True),
        lax.psum_scatter(down_grad, "blk", scatter_dimension=0, tiled=True),
        lax.psum_scatter(norm_grads, "blk", scatter_dimension=0, tiled=True),
    )
    totals = (
        lax.all_gather(summed_parts[0].astype(jnp.bfloat16), "blk", axis=0, tiled=True).astype(
            jnp.float32
        ),
        lax.all_gather(summed_parts[1].astype(jnp.bfloat16), "blk", axis=0, tiled=True).astype(
            jnp.float32
        ),
        lax.all_gather(summed_parts[2].astype(jnp.bfloat16), "blk", axis=0, tiled=True).astype(
            jnp.float32
        ),
        lax.all_gather(summed_parts[3].astype(jnp.bfloat16), "blk", axis=0, tiled=True).astype(
            jnp.float32
        ),
        lax.all_gather(summed_parts[4].astype(jnp.bfloat16), "blk", axis=0, tiled=True).astype(
            jnp.float32
        ),
        lax.all_gather(summed_parts[5].astype(jnp.bfloat16), "blk", axis=0, tiled=True).astype(
            jnp.float32
        ),
        lax.all_gather(summed_parts[6].astype(jnp.bfloat16), "blk", axis=0, tiled=True).astype(
            jnp.float32
        ),
    )
    return (
        layer_out,
        input_grad,
        totals[6][:, 0],
        totals[6][:, 1],
        totals[6][:, 2],
        totals[6][:, 3],
        totals[0],
        totals[1],
        totals[2],
        totals[3],
        totals[4],
        totals[5],
    )


HINT = pl.CostEstimate(flops=1, bytes_accessed=1, transcendentals=1)
NEAR = pl.BlockSpec(memory_space=pltpu.VMEM)
FAR = pl.BlockSpec(memory_space=pltpu.HBM)
SCALAR = pl.BlockSpec(memory_space=pltpu.SMEM)
QT = 256
KT = 512
FT = 256
TT = 1024


def near(*arrays):
    return [pltpu.with_memory_space_constraint(array, pltpu.VMEM) for array in arrays]


def room(mib):
    return pltpu.CompilerParams(vmem_limit_bytes=mib << 20)


def full(shape):
    return pl.BlockSpec(shape, lambda *_: (0,) * len(shape))


def borders_of(len_ref):
    borders = [len_ref[0]]
    for s in range(1, len_ref.shape[0] - 1):
        borders.append(borders[-1] + len_ref[s])
    return borders


def scenes(positions, borders):
    scene = jnp.zeros_like(positions)
    for border in borders:
        scene += (positions >= border).astype(jnp.int32)
    return scene


def tiles_of(first, last, borders, total):
    low, high = 0, total
    for border in borders:
        low = jnp.where(border <= first, border, low)
    for border in reversed(borders):
        high = jnp.where(border > last, border, high)
    return lax.div(low, KT), lax.div(high + KT - 1, KT)


def project_kernel(flip, ids_ref, mine_ref, other_ref, gain_ref, bias_ref, k_ref, v_ref, t_ref, n_ref, *rest):
    h_out, k_out, v_out, t_out, n_out, h_s = rest[-6:]
    n, half, width = mine_ref.shape
    rows = 2 * half
    first = ids_ref[1] == 0

    def norm(b, carry):
        mine, other = mine_ref[b], other_ref[b]
        block = jnp.concatenate([jnp.where(first, mine, other), jnp.where(first, other, mine)], axis=0)
        h_s[b] = layer_norm(block.astype(f32), gain_ref[...], bias_ref[...]).astype(bf16)
        return carry

    lax.fori_loop(0, n, norm, 0)
    h = h_s[...].reshape(n * rows, width)
    keys = jnp.dot(h, k_ref[...], preferred_element_type=f32).astype(bf16)
    values = jnp.dot(h, v_ref[...], preferred_element_type=f32).astype(bf16)
    across = lax.dot_general(t_ref[...], h, LAST, preferred_element_type=f32).astype(bf16)
    down = jnp.dot(h, n_ref[...], preferred_element_type=f32).astype(bf16)
    for s in range(n):
        at = ((ids_ref[0] - 4 * s) & 15) ^ flip
        tokens = slice(s * rows, (s + 1) * rows)
        h_out[at] = h[tokens]
        k_out[at] = keys[tokens]
        v_out[at] = values[tokens]
        t_out[at] = across[:, tokens]
        n_out[at] = down[tokens]


def project_blocks(flip, ids, mine, other, params, count, held):
    half, width = mine.shape[1:]
    _, _, key_weight, value_weight, head_t, head_n = params
    shapes = [
        (2 * half, width),
        (2 * half, key_weight.shape[1]),
        (2 * half, value_weight.shape[1]),
        (head_t.shape[0], 2 * half),
        (2 * half, head_n.shape[1]),
    ]
    return pl.pallas_call(
        lambda *refs: project_kernel(flip, *refs),
        in_specs=[SCALAR] + [NEAR] * (8 + len(held)),
        out_specs=[NEAR] * 5,
        out_shape=[pltpu.VMEM((count,) + shape, bf16) for shape in shapes],
        scratch_shapes=[pltpu.VMEM((mine.shape[0], 2 * half, width), bf16)],
        input_output_aliases={9 + i: i for i in range(5)} if held else {},
        compiler_params=room(16),
        cost_estimate=HINT,
        name="project_blocks",
    )(ids, *near(mine, other, *params, *held))


def attend_kernel(ids_ref, len_ref, h_ref, k_ref, v_ref, q_ref, o_ref, out_ref, branch_ref, query_s):
    rows, width = out_ref.shape
    total = k_ref.shape[0]
    pair = 2 * HEAD
    borders = borders_of(len_ref)
    mine = scenes(lax.broadcasted_iota(jnp.int32, (rows, 1), 0) + ids_ref[0] * rows, borders)
    mask = mine == scenes(lax.broadcasted_iota(jnp.int32, (1, total), 1), borders)
    query = jnp.dot(h_ref[ids_ref[0]], q_ref[...], preferred_element_type=f32).astype(bf16)
    query = query * jnp.asarray(HEAD ** (-0.5), bf16)
    lane = lax.broadcasted_iota(jnp.int32, (rows, pair), 1) // HEAD
    query_s[...] = query

    def attend_pair(g, carry):
        lanes = pl.ds(pl.multiple_of(g * pair, pair), pair)
        keys, values, queries = k_ref[:, lanes], v_ref[:, lanes], query_s[:, lanes]
        parts = []
        for head in range(2):
            q = jnp.where(lane == head, queries, jnp.zeros_like(queries))
            s = lax.dot_general(q, keys, LAST, preferred_element_type=f32)
            s = jnp.where(mask, s, NEG)
            p = jnp.exp(s - jnp.max(s, axis=1, keepdims=True))
            weight = jnp.sum(p, axis=1, keepdims=True)
            parts.append(jnp.dot(p.astype(bf16), values, preferred_element_type=f32) / weight)
        out_ref[:, lanes] = jnp.where(lane == 0, parts[0], parts[1]).astype(bf16)
        return carry

    lax.fori_loop(0, width // pair, attend_pair, 0)
    branch = lax.dot_general(out_ref[...], o_ref[...], LAST, preferred_element_type=f32)
    branch_ref[...] = branch.astype(bf16)


def attend(ids, scene_len, h, k, v, query_weight, output_weight):
    rows = h.shape[1]
    return pl.pallas_call(
        attend_kernel,
        in_specs=[SCALAR] * 2 + [NEAR] * 5,
        out_specs=[NEAR] * 2,
        out_shape=[
            jax.ShapeDtypeStruct((rows, query_weight.shape[1]), bf16),
            jax.ShapeDtypeStruct((rows, output_weight.shape[0]), bf16),
        ],
        scratch_shapes=[pltpu.VMEM((rows, query_weight.shape[1]), bf16)],
        compiler_params=room(16),
        cost_estimate=HINT,
        name="attend",
    )(ids, scene_len, *near(h, k, v, query_weight, output_weight))


def gelu_both(pre, grad):
    half = 0.5 * (1.0 + lax.erf(pre * 0.7071067811865476))
    slope = half + pre * (jnp.exp(-0.5 * pre * pre) * 0.3989422804014327)
    return (pre * half).astype(bf16), (grad * slope).astype(bf16)


def own_kernel(h_ref, g_ref, up_ref, down_ref, feed_out, grad_out, feed_s, grad_s):
    step = pl.program_id(0)
    pre = jnp.dot(h_ref[...], up_ref[...], preferred_element_type=f32)
    grad = jnp.dot(g_ref[...], down_ref[...], preferred_element_type=f32)
    act, grad_pre = gelu_both(pre, grad)
    feed = lax.dot_general(act, down_ref[...], LAST, preferred_element_type=f32)
    grad_two = lax.dot_general(grad_pre, up_ref[...], LAST, preferred_element_type=f32)

    @pl.when(step == 0)
    def _():
        feed_s[...] = feed
        grad_s[...] = grad_two

    @pl.when(step > 0)
    def _():
        feed_s[...] += feed
        grad_s[...] += grad_two

    @pl.when(step == pl.num_programs(0) - 1)
    def _():
        feed_out[...] = feed_s[...].astype(bf16)
        grad_out[...] = grad_s[...].astype(bf16)


def own_ffn(h, g, up_weight, down_weight):
    width = h.shape[1]
    hidden = up_weight.shape[1]
    tile = 512
    return pl.pallas_call(
        own_kernel,
        grid=(hidden // tile,),
        in_specs=[NEAR, NEAR] + [pl.BlockSpec((width, tile), lambda i: (0, i))] * 2,
        out_specs=[NEAR] * 2,
        out_shape=[jax.ShapeDtypeStruct(h.shape, bf16)] * 2,
        scratch_shapes=[pltpu.VMEM(h.shape, f32)] * 2,
        cost_estimate=HINT,
        name="own_ffn",
    )(*near(h, g), up_weight, down_weight)


def norm_back_kernel(x_ref, mine_ref, other_ref, gain_ref, g_ref, o_ref, grad_out, low_out, sums_out, heads_out):
    x = x_ref[...]
    center = x - jnp.mean(x, axis=1, keepdims=True)
    scale = lax.rsqrt(jnp.mean(center * center, axis=1, keepdims=True) + 1e-05)
    normed = center * scale
    grad = mine_ref[...].astype(f32) + other_ref[...].astype(f32)
    sums_out[0:1, :] = jnp.sum(grad * normed, axis=0, keepdims=True)
    sums_out[1:2, :] = jnp.sum(grad, axis=0, keepdims=True)
    grad = grad * gain_ref[...]
    inner = jnp.mean(grad * normed, axis=1, keepdims=True)
    grad = scale * (grad - jnp.mean(grad, axis=1, keepdims=True) - normed * inner)
    grad = grad + g_ref[...].astype(f32)
    grad_out[...] = grad
    low = grad.astype(bf16)
    low_out[...] = low
    attended = jnp.dot(low, o_ref[...], preferred_element_type=f32)
    across = attended.T.astype(bf16)
    for head in range(heads_out.shape[0]):
        heads_out[head] = across[head * HEAD : (head + 1) * HEAD, :]


def norm_back(x, mine, other, gain, g, output_weight):
    rows, width = x.shape
    return pl.pallas_call(
        norm_back_kernel,
        in_specs=[NEAR] * 6,
        out_specs=[NEAR] * 4,
        out_shape=[
            jax.ShapeDtypeStruct((rows, width), f32),
            jax.ShapeDtypeStruct((rows, width), bf16),
            jax.ShapeDtypeStruct((2, width), f32),
            jax.ShapeDtypeStruct((output_weight.shape[1] // HEAD, HEAD, rows), bf16),
        ],
        compiler_params=room(16),
        cost_estimate=HINT,
        name="norm_back",
    )(*near(x, mine, other, gain.reshape(1, width), g, output_weight))


def prepare_kernel(ids_ref, len_ref, t_ref, n_ref, p_ref, s_s):
    step = pl.program_id(0)
    count, _, rows = t_ref.shape
    borders = borders_of(len_ref)
    blocks = [4 * step + 2 * i + (ids_ref[0] & 1) for i in range(2)]
    lo, hi = tiles_of(blocks[0] * rows, blocks[1] * rows + rows - 1, borders, count * rows)
    q = jnp.concatenate([t_ref[b, 0:HEAD, :] for b in blocks], axis=1)
    q = jnp.concatenate([q, jnp.zeros_like(q)], axis=0)
    places = lax.broadcasted_iota(jnp.int32, (1, rows), 1)
    row = scenes(jnp.concatenate([places + b * rows for b in blocks], axis=1), borders)

    def score(j, top):
        keys = pl.ds(pl.multiple_of(j * KT, KT), KT)
        s = jnp.dot(n_ref[keys, 0 : 2 * HEAD], q, preferred_element_type=f32)
        col = scenes(lax.broadcasted_iota(jnp.int32, (KT, 1), 0) + j * KT, borders)
        s = jnp.where(col == row, s, NEG)
        s_s[keys, :] = s
        return jnp.maximum(top, jnp.max(s, axis=0, keepdims=True))

    top = lax.fori_loop(lo, hi, score, jnp.full((1, QT), NEG, f32))

    def weigh(j, total):
        keys = pl.ds(pl.multiple_of(j * KT, KT), KT)
        p = jnp.exp(s_s[keys, :] - top)
        s_s[keys, :] = p
        return total + jnp.sum(p, axis=0, keepdims=True)

    total = lax.fori_loop(lo, hi, weigh, jnp.zeros((1, QT), f32))
    share = 1.0 / total

    def store(j, carry):
        keys = pl.ds(pl.multiple_of(j * KT, KT), KT)
        p_ref[0, keys, :] = (s_s[keys, :] * share).astype(bf16)
        return carry

    lax.fori_loop(lo, hi, store, 0)


def prepare(ids, scene_len, head_t, head_n):
    count, _, rows = head_t.shape
    total = count * rows
    tiles = total // 2 // QT
    return pl.pallas_call(
        prepare_kernel,
        grid_spec=pltpu.PrefetchScalarGridSpec(
            num_scalar_prefetch=2,
            grid=(tiles,),
            in_specs=[full(head_t.shape), full((total, 4 * HEAD))],
            out_specs=pl.BlockSpec((1, total, QT), lambda i, *_: (i, 0, 0)),
            scratch_shapes=[pltpu.VMEM((total, QT), f32)],
        ),
        out_shape=jax.ShapeDtypeStruct((tiles, total, QT), bf16),
        cost_estimate=HINT,
        name="prepare",
    )(ids, scene_len, head_t, head_n.reshape(total, 4 * HEAD))


def back_kernel(
    ids_ref, len_ref, p_ref, ga_ref, t_ref, n_ref, h_far,
    gq_out, mine_out, other_out, slice_mine, slice_other, dp_s, gkv_s, g_s, h_ref, sem,
):
    step = pl.program_id(0)
    part = ids_ref[0] & 1
    count, _, rows = t_ref.shape
    blocks = [4 * step + 2 * i + part for i in range(2)]
    lo, hi = tiles_of(blocks[0] * rows, blocks[1] * rows + rows - 1, borders_of(len_ref), count * rows)
    load = pltpu.make_async_copy(h_far, h_ref, sem)

    @pl.when(step == 0)
    def _():
        load.start()
        gkv_s[...] = jnp.zeros_like(gkv_s)
        g_s[...] = jnp.zeros_like(g_s)

    spans = [pl.ds(pl.multiple_of(b * rows, rows), rows) for b in blocks]
    ga_t = jnp.concatenate([ga_ref[0], ga_ref[1]], axis=1)
    ga_t = jnp.concatenate([ga_t, jnp.zeros_like(ga_t)], axis=0)
    ga = ga_t.T
    kq = jnp.concatenate([n_ref[span, 0 : 2 * HEAD] for span in spans], axis=0)
    q = jnp.where(lax.broadcasted_iota(jnp.int32, kq.shape, 1) >= HEAD, kq, jnp.zeros_like(kq))

    def first(j, delta):
        keys = pl.ds(pl.multiple_of(j * KT, KT), KT)
        p = p_ref[0, keys, :]
        dp = jnp.dot(n_ref[keys, 2 * HEAD :], ga_t, preferred_element_type=f32)
        dp_s[keys, :] = dp
        gkv_s[keys, :] += jnp.dot(p, ga, preferred_element_type=f32)
        return delta + jnp.sum(p.astype(f32) * dp, axis=0, keepdims=True)

    delta = lax.fori_loop(lo, hi, first, jnp.zeros((1, QT), f32))

    def second(j, gq):
        keys = pl.ds(pl.multiple_of(j * KT, KT), KT)
        ds = (p_ref[0, keys, :].astype(f32) * (dp_s[keys, :] - delta)).astype(bf16)
        gkv_s[keys, :] += jnp.dot(ds, q, preferred_element_type=f32)
        some = KT // rows
        k_t = jnp.concatenate([t_ref[j * some + i, HEAD : 2 * HEAD, :] for i in range(some)], axis=1)
        return gq + jnp.dot(k_t, ds, preferred_element_type=f32)

    gq = lax.fori_loop(lo, hi, second, jnp.zeros((HEAD, QT), f32))
    gq = (gq * HEAD ** (-0.5)).astype(bf16)
    for i in range(2):
        tile = gq[:, i * rows : (i + 1) * rows]
        gq_out[2 * step + i] = tile
        g_s[0:HEAD, spans[i]] = tile

    @pl.when(step == pl.num_programs(0) - 1)
    def _():
        for m in range(count // 2):
            for out, b in ((mine_out, 2 * m + part), (other_out, 2 * m + 1 - part)):
                tokens = pl.ds(pl.multiple_of(b * rows, rows), rows)
                both = gkv_s[tokens, :].T
                out[m] = both.astype(out.dtype)
                g_s[HEAD:, tokens] = both.astype(bf16)
        load.wait()
        slices = jnp.dot(g_s[...], h_ref[...], preferred_element_type=f32)
        wide = slice_mine.shape[1]
        left, right = slices[:, :wide], slices[:, wide:]
        slice_mine[...] = jnp.where(part == 0, left, right)
        slice_other[...] = jnp.where(part == 0, right, left).astype(bf16)


def back(ids, scene_len, p, ga, head_t, head_n, h1):
    count, three, rows = head_t.shape
    width = h1.shape[-1]
    total = count * rows
    half = count // 2
    kept = [
        ((half, HEAD, rows), bf16),
        ((half, 2 * HEAD, rows), f32),
        ((half, 2 * HEAD, rows), bf16),
        ((three, width // 2), f32),
        ((three, width // 2), bf16),
    ]
    return pl.pallas_call(
        back_kernel,
        grid_spec=pltpu.PrefetchScalarGridSpec(
            num_scalar_prefetch=2,
            grid=(p.shape[0],),
            in_specs=[
                pl.BlockSpec((1, total, QT), lambda i, *_: (i, 0, 0)),
                pl.BlockSpec((2, HEAD, rows), lambda i, *_: (i, 0, 0)),
                full(head_t.shape),
                full((total, 4 * HEAD)),
                FAR,
            ],
            out_specs=[NEAR] * 5,
            scratch_shapes=[
                pltpu.VMEM((total, QT), f32),
                pltpu.VMEM((total, 2 * HEAD), f32),
                pltpu.VMEM((three, total), bf16),
                pltpu.VMEM((total, width), bf16),
                pltpu.SemaphoreType.DMA,
            ],
        ),
        out_shape=[jax.ShapeDtypeStruct(shape, kind) for shape, kind in kept],
        cost_estimate=HINT,
        name="back",
    )(ids, scene_len, p, ga, head_t, head_n.reshape(total, 4 * HEAD), h1.reshape(total, width))


def share_kernel(ids_ref, low_ref, attended_ref, mine_out, other_out):
    part = ids_ref[0] & 1
    whole = lax.dot_general(low_ref[...], attended_ref[...], FIRST, preferred_element_type=f32)
    whole = whole.reshape(mine_out.shape[0], 2, mine_out.shape[1], mine_out.shape[2])
    mine_out[...] = jnp.where(part == 0, whole[:, 0], whole[:, 1])
    other_out[...] = jnp.where(part == 0, whole[:, 1], whole[:, 0]).astype(bf16)


def share_output(ids, low, attended, count):
    shape = (count // 2, low.shape[1] // count, attended.shape[1])
    return pl.pallas_call(
        share_kernel,
        in_specs=[SCALAR, NEAR, NEAR],
        out_specs=[NEAR] * 2,
        out_shape=[jax.ShapeDtypeStruct(shape, f32), jax.ShapeDtypeStruct(shape, bf16)],
        compiler_params=room(16),
        cost_estimate=HINT,
        name="share_output",
    )(ids, *near(low, attended))


def merge_kernel(gq_ref, kept_ref, given_ref, out_ref):
    out_ref[:, 0:HEAD, :] = gq_ref[...]
    out_ref[:, HEAD:, :] = (kept_ref[...] + given_ref[...].astype(f32)).astype(bf16)


def merge(gq, kept, given):
    half, _, rows = gq.shape
    return pl.pallas_call(
        merge_kernel,
        in_specs=[NEAR] * 3,
        out_specs=NEAR,
        out_shape=jax.ShapeDtypeStruct((half, 3 * HEAD, rows), bf16),
        compiler_params=room(8),
        cost_estimate=HINT,
        name="merge",
    )(*near(gq, kept, given))


def unit_kernel(mine_ref, other_ref, parts_ref, out_ref):
    rows = mine_ref.shape[0]
    out_ref[0:rows, :] = (mine_ref[...] + other_ref[...].astype(f32)).astype(bf16)
    out_ref[rows:, :] = jnp.sum(parts_ref[...].astype(f32), axis=0).astype(bf16)


def make_unit(mine, other, parts):
    rows, wide = mine.shape
    return pl.pallas_call(
        unit_kernel,
        in_specs=[NEAR] * 3,
        out_specs=NEAR,
        out_shape=jax.ShapeDtypeStruct((rows + parts.shape[1], wide), bf16),
        compiler_params=room(8),
        cost_estimate=HINT,
        name="make_unit",
    )(mine, other, parts)


def home_kernel(home_ref, q_ref, v_ref, k_ref, grad_out):
    rows = home_ref.shape[2]
    grad = 0.0
    for i, weight in enumerate((q_ref, v_ref, k_ref)):
        across = home_ref[:, i * HEAD : (i + 1) * HEAD, :].reshape(-1, rows)
        grad = grad + lax.dot_general(across.T, weight[...], LAST, preferred_element_type=f32)
    grad_out[...] = grad.astype(bf16)


def go_home(home, weights):
    return pl.pallas_call(
        home_kernel,
        in_specs=[NEAR] * 4,
        out_specs=NEAR,
        out_shape=jax.ShapeDtypeStruct((home.shape[2], weights[0].shape[0]), bf16),
        cost_estimate=HINT,
        name="go_home",
    )(home, *weights)


def input_back_kernel(x_ref, mine_ref, other_ref, gain_ref, grad_ref, sums_ref, grad_out, sums_out):
    x = x_ref[...].astype(f32)
    center = x - jnp.mean(x, axis=1, keepdims=True)
    scale = lax.rsqrt(jnp.mean(center * center, axis=1, keepdims=True) + 1e-05)
    normed = center * scale
    grad = mine_ref[...].astype(f32) + other_ref[...].astype(f32)
    sums = [jnp.sum(grad * normed, axis=0, keepdims=True), jnp.sum(grad, axis=0, keepdims=True), sums_ref[...]]
    sums = jnp.concatenate(sums, axis=0)
    for b in range(sums_out.shape[0]):
        sums_out[b] = sums
    grad = grad * gain_ref[...]
    inner = jnp.mean(grad * normed, axis=1, keepdims=True)
    grad_out[...] = grad_ref[...] + scale * (grad - jnp.mean(grad, axis=1, keepdims=True) - normed * inner)


def input_back(x, mine, other, gain, grad_middle, sums, count):
    rows, width = x.shape
    return pl.pallas_call(
        input_back_kernel,
        in_specs=[NEAR] * 6,
        out_specs=[NEAR] * 2,
        out_shape=[
            jax.ShapeDtypeStruct((rows, width), f32),
            jax.ShapeDtypeStruct((count, 4, width), f32),
        ],
        compiler_params=room(16),
        cost_estimate=HINT,
        name="input_back",
    )(x, mine, other, gain.reshape(1, width), grad_middle, sums)


def through_kernel(g_ref, down_ref, out_ref):
    out_ref[...] = jnp.dot(g_ref[...], down_ref[...], preferred_element_type=f32).astype(bf16)


def through(g, weight):
    total, width = g.shape
    hidden = weight.shape[1]
    rows, tile = TT // 2, hidden // 2
    return pl.pallas_call(
        through_kernel,
        grid=(hidden // tile, total // rows),
        in_specs=[
            pl.BlockSpec((rows, width), lambda i, j: (j, 0)),
            pl.BlockSpec((width, tile), lambda i, j: (0, i)),
        ],
        out_specs=pl.BlockSpec((rows, tile), lambda i, j: (j, i)),
        out_shape=jax.ShapeDtypeStruct((total, hidden), bf16),
        cost_estimate=pl.CostEstimate(
            flops=2 * total * width * hidden, bytes_accessed=8 * total * width, transcendentals=0
        ),
        name="through",
    )(g, weight)


def ffn_kernel(h_ref, g_ref, grad_ref, up_ref, *outs):
    up_out, down_out = outs[-2:]
    steps = h_ref.shape[0] // TT

    def product(j):
        return jnp.dot(h_ref[j * TT : (j + 1) * TT, :], up_ref[...], preferred_element_type=f32)

    pre = product(0)
    for j in range(steps):
        later = product(j + 1) if j + 1 < steps else None
        span = slice(j * TT, (j + 1) * TT)
        act, grad_pre = gelu_both(pre, grad_ref[span, :].astype(f32))
        up = lax.dot_general(h_ref[span, :], grad_pre, FIRST, preferred_element_type=f32)
        down = lax.dot_general(g_ref[span, :], act, FIRST, preferred_element_type=f32)
        if j == 0:
            up_out[...] = up
            down_out[...] = down
        else:
            up_out[...] += up
            down_out[...] += down
        pre = later


def ffn_grads(h, g, grad, up_weight, tiles, held):
    total, width = h.shape
    hidden = up_weight.shape[1]
    first, last = tiles
    tokens = pl.BlockSpec((total, width), lambda i: (0, 0), pipeline_mode=pl.Buffered(1))
    units = pl.BlockSpec((width, FT), lambda i: (0, first + i))
    return pl.pallas_call(
        ffn_kernel,
        grid=(last - first,),
        in_specs=[tokens, tokens, pl.BlockSpec((total, FT), lambda i: (0, first + i)), units] + [FAR] * len(held),
        out_specs=[units] * 2,
        out_shape=[jax.ShapeDtypeStruct((width, hidden), f32)] * 2,
        input_output_aliases={4: 0, 5: 1} if held else {},
        cost_estimate=pl.CostEstimate(
            flops=6 * total * width * FT * (last - first), bytes_accessed=4 * total * width, transcendentals=0
        ),
        name="ffn_grads",
    )(h, g, grad, up_weight, *held)


def finish_kernel(ids_ref, *refs):
    pieces, outs = refs[:5], refs[5:]
    row, part = (ids_ref[0] >> 1) & 1, ids_ref[0] & 1
    wide = pieces[0].shape[2]
    early = pl.program_id(0) < 2

    def rows_of(k, span):
        if k < 3:
            return pieces[k][0, span, :]
        return jnp.where(early, pieces[3][0, span, :], pieces[4][0, span, :])

    for k, x in ((0, part), (1, 1 - part)):
        rows = pl.ds(pl.multiple_of(x * wide, wide), wide)
        for i in range(3):
            span = slice(i * HEAD, (i + 1) * HEAD)
            this, that = rows_of(k, span), rows_of(k + 2, span)
            pair = [jnp.where(row == 0, this, that), jnp.where(row == 0, that, this)]
            outs[i][rows, :] = jnp.concatenate(pair, axis=0).T.astype(f32)
    slots = pieces[0].shape[1] - 3 * HEAD
    for k in range(4):
        at = pl.multiple_of(((ids_ref[0] & 3) ^ k) * slots, slots)
        outs[3][pl.ds(at, slots), :] = rows_of(k, slice(3 * HEAD, None)).astype(f32)


def finish(ids, pieces, width, columns):
    def plane(s, ids):
        return ((ids[0] - 4 * s) & 15) >> 2

    shape = (1,) + pieces[0].shape[1:]
    whole = pl.BlockSpec(shape, lambda s, ids: (s, 0, 0))
    early = pl.BlockSpec(shape, lambda s, ids: (jnp.minimum(s, 1), 0, 0))
    late = pl.BlockSpec(shape, lambda s, ids: (jnp.maximum(s - 2, 0), 0, 0))
    across = pl.BlockSpec((width, columns // 4), lambda s, ids: (0, plane(s, ids)))
    down = pl.BlockSpec((width // 4, columns), lambda s, ids: (plane(s, ids), 0))
    return pl.pallas_call(
        finish_kernel,
        grid_spec=pltpu.PrefetchScalarGridSpec(
            num_scalar_prefetch=1,
            grid=(4,),
            in_specs=[whole, whole, whole, early, late],
            out_specs=[across] * 3 + [down],
        ),
        out_shape=[jax.ShapeDtypeStruct((width, columns), f32)] * 4,
        cost_estimate=HINT,
        name="finish",
    )(ids, *pieces)


def shuffle(block, target):
    return lax.ppermute(block, "blk", [(i, target(i)) for i in range(16)])


def over_core(block):
    return lax.ppermute(block, "tp", [(0, 1), (1, 0)])


def send_column(unit):
    return (unit,) + tuple(shuffle(unit, lambda i, s=s: (i + 4 * s) % 16) for s in (1, 2, 3))


def stack_column(parts, *first):
    return jnp.stack(lax.optimization_barrier(parts + first)[:4])


def gather_sides(column):
    return shuffle(column, lambda i: i ^ 1), shuffle(column, lambda i: i ^ 2)


def after(value, *first):
    return lax.optimization_barrier((value,) + first)[0]


def fast_body(
    tokens,
    first_gain,
    first_bias,
    second_gain,
    second_bias,
    query_weight,
    key_weight,
    value_weight,
    output_weight,
    up_weight,
    down_weight,
    cotangent,
    scene_len,
):
    count = lax.axis_size("blk")
    place = lax.axis_index("blk")
    side = lax.axis_index("tp")
    rows, width = tokens.shape
    columns = query_weight.shape[1]
    heads_here = columns // HEAD
    share = count // heads_here
    scale = HEAD ** (-0.5)
    ids = jnp.stack([place, side])
    half_at = side.astype(jnp.uint32) * jnp.uint32(rows // 2)
    head_at = (place.astype(jnp.uint32) >> 1) * jnp.uint32(HEAD)
    alike = [list(range(r, count, share)) for r in range(share)]

    def half_of(block):
        return lax.dynamic_slice(block, (half_at, jnp.uint32(0)), (rows // 2, width))

    def head_of(weight):
        return lax.dynamic_slice(weight, (jnp.uint32(0), head_at), (width, HEAD))

    g_all = lax.all_gather(half_of(cotangent), ("blk", "tp"), axis=0, tiled=True)
    column = jnp.stack(send_column(half_of(tokens)))

    head_query = head_of(query_weight) * jnp.asarray(scale, bf16)
    head_key, head_value = head_of(key_weight), head_of(value_weight)
    head_t = jnp.concatenate([head_query, head_key, head_value], axis=1).T
    head_n = jnp.concatenate([head_key, head_query, head_value, jnp.zeros_like(head_value)], axis=1)
    params = (first_gain.reshape(1, -1), first_bias.reshape(1, -1), key_weight, value_weight, head_t, head_n)

    across_x = shuffle(column, lambda i: i ^ 1)
    across_y = shuffle(column, lambda i: i ^ 2)
    made = project_blocks(0, ids, column, over_core(column), params, count, ())
    across_y = after(across_y, made[0])
    diagonal = shuffle(across_y, lambda i: i ^ 1)
    for flip, piece in ((1, after(across_x, across_y)), (2, across_y), (3, diagonal)):
        piece = after(piece, made[0]) if piece is diagonal else piece
        made = project_blocks(flip, ids, piece, over_core(piece), params, count, made)
    h1_all, keys, values, head_t, head_n = made

    attended, branch = attend(
        ids, scene_len, h1_all, keys.reshape(-1, columns), values.reshape(-1, columns), query_weight, output_weight
    )
    inputs = tokens.astype(f32)
    middle = inputs + (branch.astype(f32) + over_core(branch).astype(f32))
    h2 = layer_norm(middle, second_gain, second_bias).astype(bf16)
    h2_all = lax.all_gather(half_of(h2), ("blk", "tp"), axis=0, tiled=True)

    feed, grad_two = own_ffn(h2, cotangent, up_weight, down_weight)
    grad_middle, grad_middle_low, second_sums, to_heads = norm_back(
        middle, grad_two, over_core(grad_two), second_gain, cotangent, output_weight
    )
    ga = lax.all_to_all(to_heads, "blk", 0, 0, tiled=True, axis_index_groups=alike)
    output_kept, output_given = share_output(ids, after(grad_middle_low, to_heads), attended, count)
    output_other = shuffle(output_given, lambda i: i ^ 1)
    p = prepare(ids, scene_len, after(head_t, to_heads, g_all, output_given), head_n)
    output_kept, output_other, _ = lax.optimization_barrier((output_kept, output_other, p))
    output_half = (output_kept + output_other.astype(f32)).astype(bf16)
    output_parts = lax.all_to_all(after(output_half, ga, p), "blk", 0, 0, tiled=True, axis_index_groups=alike)
    grad_q, kept, given, slice_kept, slice_given = back(ids, scene_len, p, ga, head_t, head_n, h1_all)

    grad_all = through(after(g_all, grad_q), down_weight)
    slice_other = shuffle(slice_given, lambda i: i ^ 1)
    unit = make_unit(after(slice_kept, grad_all), slice_other, output_parts)
    parts = send_column(unit)
    given = shuffle(after(given, unit), lambda i: i ^ 1)
    feed = after(feed, unit)
    layer_out = (middle + (feed.astype(f32) + over_core(feed).astype(f32))).astype(bf16)
    parcel = merge(after(grad_q, unit), kept, given)
    home = lax.all_to_all(parcel, "blk", 0, 0, tiled=True, axis_index_groups=alike)
    held = ffn_grads(after(h2_all, unit, parcel), g_all, grad_all, up_weight, (0, 3), ())
    column = stack_column(parts, held[0], layer_out)
    side_x, side_y = gather_sides(column)
    up_grad, down_grad = ffn_grads(after(h2_all, column), g_all, grad_all, up_weight, (3, 8), held)

    half_x, half_y = lax.optimization_barrier((side_x[2:], side_y[:2], up_grad))[:2]
    across = shuffle(half_y, lambda i: i ^ 1), shuffle(half_x, lambda i: i ^ 2)
    home = after(home, up_grad).reshape(heads_here, 3 * HEAD, rows)
    home = after(home, half_x, half_y)
    grad_one = go_home(home, (query_weight, value_weight, key_weight))
    input_grad, norm_part = input_back(
        tokens, grad_one, over_core(grad_one), first_gain, grad_middle, second_sums, count
    )
    norm_parts = lax.all_to_all(norm_part, "blk", 0, 0, tiled=True)
    heads = (after(column, norm_part), side_x, side_y) + across
    query_grad, value_grad, key_grad, output_grad = finish(ids, heads, width, columns)
    norm_sums = jnp.sum(after(norm_parts, output_grad), axis=0)
    return (
        layer_out,
        input_grad,
        norm_sums[0],
        norm_sums[1],
        norm_sums[2],
        norm_sums[3],
        query_grad,
        key_grad,
        value_grad,
        output_grad,
        up_grad,
        down_grad,
    )


def solution(mesh):
    body = fast_body if mesh.shape["blk"] == 16 else ring_body
    return jax.shard_map(
        body,
        mesh=mesh,
        in_specs=(
            P("blk", None),
            P(),
            P(),
            P(),
            P(),
            P(None, "tp"),
            P(None, "tp"),
            P(None, "tp"),
            P(None, "tp"),
            P(None, "tp"),
            P(None, "tp"),
            P("blk", None),
            P(),
        ),
        out_specs=(
            P("blk", None),
            P("blk", None),
            P(),
            P(),
            P(),
            P(),
            P(None, "tp"),
            P(None, "tp"),
            P(None, "tp"),
            P(None, "tp"),
            P(None, "tp"),
            P(None, "tp"),
        ),
        check_vma=False,
    )
```
